256 devices in a mesh: gx: 64 (over x, z, core), af: 4 (over y).
Axes of the slice: x: 4, y: 4, z: 8, core: 2. Of those that a mesh axis runs over, the one named last changes fastest.
Arguments:
- scalar_field: float32 [128, 512, 512], P('gx', 'af'), may hold values from -256 to 256
- plane_sketch: float32 [128, 2, 256], P('gx'), may hold values from -0.5 to 0.5
- second_sketch: float32 [512, 256], P('af'), may hold values from -0.25 to 0.25
- third_sketch: float32 [512, 256], replicated, may hold values from -0.25 to 0.25
- mixing: float32 [2, 256, 128], replicated, may hold values from -0.375 to 0.375
- plane_targets: int32 [128, 2], replicated, may hold values from 0 to 7
- plane_signs: int32 [128, 2], replicated, may hold values from 0 to 1
Outputs:
- factor_second: float32 [512, 128], P(('af', 'gx'))
- factor_third: float32 [512, 128], P(('gx', 'af'))
- core_sketch: float32 [128, 128, 128], P('gx', 'af')
The draws below stay inside these ranges and needn't reach their ends.
Inputs may be any that keep to these rules, and one draw needn't show every extreme that they name: `plane_targets`: block id of each of a plane's two entries in the core sketch; the two may coincide. `plane_signs`: 1 stands for a plus sign, 0 for a minus sign.
All inputs are finite; a program needn't handle non-finite values.
Results may differ from the reference program's by a relative error of at most 0.0003.
Values sent between devices are 32-bit elements; how exact they have to be, the bound alone decides.
A program may use at most 64 MiB of HBM per device.

```python
import jax
import jax.numpy as jnp
from jax import lax

NY = 512
NZ = 512
SKETCH = 256
RANK = 128
BLOCK = 16
BLOCKS = 8
NX = 128


def draw_scalar_field(key, part):
    keys = jax.random.split(jax.random.fold_in(key, 17), 4)
    pos_y = jnp.arange(NY, dtype=jnp.float32) / (NY - 1) - 0.5
    pos_z = jnp.arange(NZ, dtype=jnp.float32) / (NZ - 1) - 0.5
    scale_y = jnp.exp(jax.random.uniform(keys[0], (NY,), jnp.float32, -1.15, 1.15) + 1.0986 * pos_y)
    scale_z = jnp.exp(jax.random.uniform(keys[1], (NZ,), jnp.float32, -1.15, 1.15) - 1.0986 * pos_z)
    scale_x = jnp.exp(jax.random.uniform(keys[2], (NX,), jnp.float32, -0.69, 0.69))
    noise = jax.random.truncated_normal(keys[3], -4.0, 4.0, (NX, NY, NZ), jnp.float32)
    return noise * scale_x[:, None, None] * scale_y[None, :, None] * scale_z[None, None, :]


def with_ends(entries, key, smallest, largest):
    index_at = [jax.random.randint(jax.random.fold_in(key, axis), (), 0, length) for axis, length in enumerate(entries.shape)]
    main_axis = entries.shape.index(max(entries.shape))
    beside = index_at[:main_axis] + [(index_at[main_axis] + 1) % entries.shape[main_axis]] + index_at[main_axis + 1:]
    return entries.at[tuple(index_at)].set(smallest).at[tuple(beside)].set(largest)


def steps_of(stream_key, extent, cuts, low, high):
    level = 1.0
    for position, blocks in cuts:
        steps = jax.random.uniform(jax.random.fold_in(jax.random.fold_in(stream_key, 6), position), (blocks,), jnp.float32, low / len(cuts), high / len(cuts))
        level = level * jnp.repeat(jnp.exp(steps), extent[position] // blocks).reshape((-1,) + (1,) * (len(extent) - 1 - position))
    return level


def centred(key, extent, scale, most, pieces=(), kind=jnp.bfloat16):
    result = scale * jax.random.normal(key, extent, jnp.float32)
    if pieces:
        result = result * steps_of(key, extent, pieces, -0.22, 0.18)
    return jnp.clip(result, -most, most).astype(kind)


def setup_inputs(seed: int = 0) -> dict:
    streams_of = jax.random.split(jax.random.key(seed), 8)
    return {
        "scalar_field": draw_scalar_field(jax.random.fold_in(streams_of[7], 71), 0),
        "plane_sketch": centred(streams_of[1], (NX, 2, SKETCH), NX ** -0.5, 0.5, ((0, 64),), jnp.float32),
        "second_sketch": centred(streams_of[2], (NY, SKETCH), NY ** -0.5, 0.25, ((0, 4),), jnp.float32),
        "third_sketch": centred(streams_of[3], (NZ, SKETCH), NZ ** -0.5, 0.25, (), jnp.float32),
        "mixing": centred(streams_of[4], (2, SKETCH, RANK), SKETCH ** -0.5, 0.375, (), jnp.float32),
        "plane_targets": with_ends(jax.random.randint(streams_of[5], (NX, 2), 0, BLOCKS), jax.random.fold_in(streams_of[5], 1), 0, BLOCKS - 1).astype(jnp.int32),
        "plane_signs": with_ends(jax.random.randint(streams_of[6], (NX, 2), 0, 2), jax.random.fold_in(streams_of[6], 1), 0, 1).astype(jnp.int32),
    }


precise = lax.Precision.HIGHEST

def orthonormal(ranged):
    gram_matrix = jnp.dot(ranged.T, ranged, precision=precise)
    lower_factor = jnp.linalg.cholesky(gram_matrix)
    return jax.scipy.linalg.solve_triangular(lower_factor, ranged.T, lower=True).T

def reference(scalar_field, plane_sketch, second_sketch, third_sketch, mixing, plane_targets, plane_signs):

    def accumulate(totals, element):
        one_plane, plane_weights = element
        along_rows = jnp.dot(one_plane, third_sketch, precision=precise) * plane_weights[0][None, :]
        across = jnp.dot(one_plane.T, second_sketch, precision=precise) * plane_weights[1][None, :]
        return ((totals[0] + along_rows, totals[1] + across), None)
    initial = (jnp.zeros((NY, SKETCH), jnp.float32), jnp.zeros((NZ, SKETCH), jnp.float32))
    (second_mode, third_mode), unused = lax.scan(accumulate, initial, (scalar_field, plane_sketch))
    second_range = jnp.dot(second_mode, mixing[0], precision=precise)
    third_range = jnp.dot(third_mode, mixing[1], precision=precise)
    factor_second = orthonormal(second_range)
    factor_third = orthonormal(third_range)

    def project(one_plane):
        left_side = jnp.dot(factor_second.T, one_plane, precision=precise)
        return jnp.dot(left_side, factor_third, precision=precise)
    projected = lax.map(project, scalar_field)
    plane_ids = jnp.arange(NX, dtype=jnp.int32)
    targets = plane_targets * BLOCK + (plane_ids % BLOCK)[:, None]
    sign_values = (2 * plane_signs - 1).astype(jnp.float32)
    row_ids = jnp.arange(BLOCKS * BLOCK, dtype=jnp.int32)
    select = jnp.sum(jnp.where(targets[None, :, :] == row_ids[:, None, None], sign_values[None, :, :], 0.0), axis=2)
    core_sketch = jnp.dot(select, projected.reshape(NX, RANK * RANK), precision=precise)
    return (factor_second, factor_third, core_sketch.reshape(BLOCKS * BLOCK, RANK, RANK))
```

```python
import jax
import jax.numpy as jnp
from jax import lax
from jax.sharding import PartitionSpec as P

BLOCK = 16
BLOCKS = 8


precise = lax.Precision.HIGHEST


def gram_of(ranged):
    return jnp.dot(ranged.T, ranged, precision=precise)


def orthonormal_rows(ranged, gram_matrix):
    lower_factor = jnp.linalg.cholesky(gram_matrix)
    return jax.scipy.linalg.solve_triangular(lower_factor, ranged.T, lower=True).T


def selector(targets, sign_values, row_count):
    row_ids = jnp.arange(row_count, dtype=jnp.int32)
    return jnp.sum(
        jnp.where(targets[None, :, :] == row_ids[:, None, None], sign_values[None, :, :], 0.0),
        axis=2,
    )


def body(
    scalar_field, plane_sketch, second_sketch, third_sketch, mixing, plane_targets, plane_signs
):
    planes, rows, cells = scalar_field.shape
    rank_cols = mixing.shape[2]
    gx_index = lax.axis_index("gx")
    af_index = lax.axis_index("af")
    gx_size = lax.axis_size("gx")
    af_size = lax.axis_size("af")

    along_second = jnp.einsum("pjl,lk->pjk", scalar_field, third_sketch, precision=precise)
    partial_second = jnp.einsum(
        "pjk,pk->jk", along_second, plane_sketch[:, 0, :], precision=precise
    )
    along_third = jnp.einsum("pjl,jk->plk", scalar_field, second_sketch, precision=precise)
    partial_third = jnp.einsum("plk,pk->lk", along_third, plane_sketch[:, 1, :], precision=precise)

    range_second_block = jnp.dot(partial_second, mixing[0], precision=precise)
    range_third = jnp.dot(partial_third, mixing[1], precision=precise)
    full_rows = rows * af_size
    range_second = lax.dynamic_update_slice_in_dim(
        jnp.zeros((full_rows, rank_cols), jnp.float32), range_second_block, af_index * rows, 0
    )
    both = lax.psum(jnp.stack([range_second, range_third]), ("gx", "af"))
    rows_second, rows_third = both[0], both[1]

    factor_second_all = orthonormal_rows(rows_second, gram_of(rows_second))
    factor_third_all = orthonormal_rows(rows_third, gram_of(rows_third))

    out_second = full_rows // (gx_size * af_size)
    factor_second = lax.dynamic_slice_in_dim(
        factor_second_all, (af_index * gx_size + gx_index) * out_second, out_second, 0
    )
    factor_third = lax.dynamic_slice_in_dim(
        factor_third_all, (gx_index * af_size + af_index) * out_second, out_second, 0
    )
    basis_second = lax.dynamic_slice_in_dim(factor_second_all, af_index * rows, rows, 0)
    left_side = jnp.einsum("jr,pjl->prl", basis_second, scalar_field, precision=precise)
    projected = jnp.einsum("prl,ls->prs", left_side, factor_third_all, precision=precise)
    out_rows = BLOCKS * BLOCK // gx_size
    plane_ids = jnp.arange(plane_targets.shape[0], dtype=jnp.int32)
    all_targets = plane_targets * BLOCK + (plane_ids % BLOCK)[:, None]
    all_signs = (2 * plane_signs - 1).astype(jnp.float32)
    first_plane = gx_index * planes
    own_targets = lax.dynamic_slice_in_dim(all_targets, first_plane, planes, 0)
    own_signs = lax.dynamic_slice_in_dim(all_signs, first_plane, planes, 0)
    flattened = projected.reshape(planes, -1)
    select = selector(own_targets, own_signs, gx_size * out_rows)
    partial_core = lax.psum_scatter(
        jnp.dot(select, flattened, precision=precise).reshape(
            gx_size * out_rows, rank_cols, rank_cols
        ),
        "gx",
        scatter_dimension=0,
        tiled=True,
    )
    core_sketch = lax.psum_scatter(partial_core, "af", scatter_dimension=1, tiled=True)
    return (factor_second, factor_third, core_sketch)


def solution(mesh):
    in_specs = (P("gx", "af", None), P("gx", None, None), P("af", None), P(), P(), P(), P())
    out_specs = (P(("af", "gx"), None), P(("gx", "af"), None), P("gx", "af", None))
    return jax.shard_map(body, mesh=mesh, in_specs=in_specs, out_specs=out_specs, check_vma=False)
```

```python
import functools

import jax
import jax.numpy as jnp
from jax import lax
from jax.experimental import pallas as pl
from jax.experimental.pallas import tpu as pltpu
from jax.sharding import PartitionSpec as P

MESH = pl.DeviceIdType.MESH

BLOCK = 16
BLOCKS = 8


precise = lax.Precision.HIGHEST


def gram_of(ranged):
    return jnp.dot(ranged.T, ranged, precision=precise)


def orthonormal_rows(ranged, gram_matrix):
    lower_factor = jnp.linalg.cholesky(gram_matrix)
    return jax.scipy.linalg.solve_triangular(lower_factor, ranged.T, lower=True).T


def partner_list(gx_size, af_size):
    steps = []
    bit = 1
    while bit < gx_size:
        steps.append(("gx", bit))
        bit *= 2
    bit = 1
    while bit < af_size:
        steps.append(("af", bit))
        bit *= 2
    return steps


def allreduce_kernel(steps, x_ref, o_ref, recv, send_sem, recv_sem):
    g = lax.axis_index("gx")
    a = lax.axis_index("af")

    def partner(axis, bit):
        if axis == "gx":
            return (lax.bitwise_xor(g, bit), a)
        return (g, lax.bitwise_xor(a, bit))

    barrier = pltpu.get_barrier_semaphore()
    for axis, bit in steps:
        pl.semaphore_signal(barrier, inc=1, device_id=partner(axis, bit), device_id_type=MESH)
    pl.semaphore_wait(barrier, len(steps))

    o_ref[...] = x_ref[...]
    for s, (axis, bit) in enumerate(steps):
        copy = pltpu.make_async_remote_copy(
            src_ref=o_ref,
            dst_ref=recv.at[s],
            send_sem=send_sem.at[s],
            recv_sem=recv_sem.at[s],
            device_id=partner(axis, bit),
            device_id_type=MESH,
        )
        copy.start()
        copy.wait()
        o_ref[...] = o_ref[...] + recv[s]


def allreduce_all(x):
    steps = partner_list(lax.axis_size("gx"), lax.axis_size("af"))
    return pl.pallas_call(
        functools.partial(allreduce_kernel, steps),
        out_shape=jax.ShapeDtypeStruct(x.shape, x.dtype),
        in_specs=[pl.BlockSpec(memory_space=pltpu.VMEM)],
        out_specs=pl.BlockSpec(memory_space=pltpu.VMEM),
        scratch_shapes=[
            pltpu.VMEM((len(steps),) + x.shape, x.dtype),
            pltpu.SemaphoreType.DMA((len(steps),)),
            pltpu.SemaphoreType.DMA((len(steps),)),
        ],
        compiler_params=pltpu.CompilerParams(collective_id=0, has_side_effects=True),
    )(x)


def selector(targets, sign_values, row_count):
    row_ids = jnp.arange(row_count, dtype=jnp.int32)
    return jnp.sum(
        jnp.where(targets[None, :, :] == row_ids[:, None, None], sign_values[None, :, :], 0.0),
        axis=2,
    )


def body(
    scalar_field, plane_sketch, second_sketch, third_sketch, mixing, plane_targets, plane_signs
):
    planes, rows, cells = scalar_field.shape
    rank_cols = mixing.shape[2]
    gx_index = lax.axis_index("gx")
    af_index = lax.axis_index("af")
    gx_size = lax.axis_size("gx")
    af_size = lax.axis_size("af")

    along_second = jnp.einsum("pjl,lk->pjk", scalar_field, third_sketch, precision=precise)
    partial_second = jnp.einsum(
        "pjk,pk->jk", along_second, plane_sketch[:, 0, :], precision=precise
    )
    along_third = jnp.einsum("pjl,jk->plk", scalar_field, second_sketch, precision=precise)
    partial_third = jnp.einsum("plk,pk->lk", along_third, plane_sketch[:, 1, :], precision=precise)

    range_second_block = jnp.dot(partial_second, mixing[0], precision=precise)
    range_third = jnp.dot(partial_third, mixing[1], precision=precise)
    full_rows = rows * af_size
    range_second = lax.dynamic_update_slice_in_dim(
        jnp.zeros((full_rows, rank_cols), jnp.float32), range_second_block, af_index * rows, 0
    )
    both = allreduce_all(jnp.concatenate([range_second, range_third], axis=0))
    rows_second, rows_third = both[:full_rows], both[full_rows:]

    factor_second_all = orthonormal_rows(rows_second, gram_of(rows_second))
    factor_third_all = orthonormal_rows(rows_third, gram_of(rows_third))

    out_second = full_rows // (gx_size * af_size)
    factor_second = lax.dynamic_slice_in_dim(
        factor_second_all, (af_index * gx_size + gx_index) * out_second, out_second, 0
    )
    factor_third = lax.dynamic_slice_in_dim(
        factor_third_all, (gx_index * af_size + af_index) * out_second, out_second, 0
    )
    basis_second = lax.dynamic_slice_in_dim(factor_second_all, af_index * rows, rows, 0)
    left_side = jnp.einsum("jr,pjl->prl", basis_second, scalar_field, precision=precise)
    projected = jnp.einsum("prl,ls->prs", left_side, factor_third_all, precision=precise)
    out_rows = BLOCKS * BLOCK // gx_size
    plane_ids = jnp.arange(plane_targets.shape[0], dtype=jnp.int32)
    all_targets = plane_targets * BLOCK + (plane_ids % BLOCK)[:, None]
    all_signs = (2 * plane_signs - 1).astype(jnp.float32)
    first_plane = gx_index * planes
    own_targets = lax.dynamic_slice_in_dim(all_targets, first_plane, planes, 0)
    own_signs = lax.dynamic_slice_in_dim(all_signs, first_plane, planes, 0)
    flattened = projected.reshape(planes, -1)
    select = selector(own_targets, own_signs, gx_size * out_rows)
    partial_core = lax.psum_scatter(
        jnp.dot(select, flattened, precision=precise).reshape(
            gx_size * out_rows, rank_cols, rank_cols
        ),
        "gx",
        scatter_dimension=0,
        tiled=True,
    )
    core_sketch = lax.psum_scatter(partial_core, "af", scatter_dimension=1, tiled=True)
    return (factor_second, factor_third, core_sketch)


def solution(mesh):
    in_specs = (P("gx", "af", None), P("gx", None, None), P("af", None), P(), P(), P(), P())
    out_specs = (P(("af", "gx"), None), P(("gx", "af"), None), P("gx", "af", None))
    return jax.shard_map(body, mesh=mesh, in_specs=in_specs, out_specs=out_specs, check_vma=False)
```

```python
import functools

import jax
import jax.numpy as jnp
from jax import lax
from jax.experimental import pallas as pl
from jax.experimental.pallas import tpu as pltpu
from jax.sharding import PartitionSpec as P

MESH = pl.DeviceIdType.MESH

BLOCK = 16
BLOCKS = 8


precise = lax.Precision.HIGHEST


def gram_of(ranged):
    return jnp.dot(ranged.T, ranged, precision=precise)


def orthonormal_rows(ranged, gram_matrix):
    lower_factor = jnp.linalg.cholesky(gram_matrix)
    return jax.scipy.linalg.solve_triangular(lower_factor, ranged.T, lower=True).T


def partner_list(gx_size, af_size):
    steps = []
    bit = 1
    while bit < gx_size:
        steps.append(("gx", bit))
        bit *= 2
    bit = 1
    while bit < af_size:
        steps.append(("af", bit))
        bit *= 2
    return steps


def allreduce_kernel(steps, x_ref, o_ref, recv, send_sem, recv_sem):
    g = lax.axis_index("gx")
    a = lax.axis_index("af")

    def partner(axis, bit):
        if axis == "gx":
            return (lax.bitwise_xor(g, bit), a)
        return (g, lax.bitwise_xor(a, bit))

    barrier = pltpu.get_barrier_semaphore()
    for axis, bit in steps:
        pl.semaphore_signal(barrier, inc=1, device_id=partner(axis, bit), device_id_type=MESH)
    pl.semaphore_wait(barrier, len(steps))

    o_ref[...] = x_ref[...]
    for s, (axis, bit) in enumerate(steps):
        copy = pltpu.make_async_remote_copy(
            src_ref=o_ref,
            dst_ref=recv.at[s],
            send_sem=send_sem.at[s],
            recv_sem=recv_sem.at[s],
            device_id=partner(axis, bit),
            device_id_type=MESH,
        )
        copy.start()
        copy.wait()
        o_ref[...] = o_ref[...] + recv[s]


def allreduce_all(x):
    steps = partner_list(lax.axis_size("gx"), lax.axis_size("af"))
    return pl.pallas_call(
        functools.partial(allreduce_kernel, steps),
        out_shape=jax.ShapeDtypeStruct(x.shape, x.dtype),
        in_specs=[pl.BlockSpec(memory_space=pltpu.VMEM)],
        out_specs=pl.BlockSpec(memory_space=pltpu.VMEM),
        scratch_shapes=[
            pltpu.VMEM((len(steps),) + x.shape, x.dtype),
            pltpu.SemaphoreType.DMA((len(steps),)),
            pltpu.SemaphoreType.DMA((len(steps),)),
        ],
        compiler_params=pltpu.CompilerParams(collective_id=0, has_side_effects=True),
    )(x)


def core_kernel(cycle, send_ref, o_ref, recv, send_sem, recv_sem):
    g = lax.axis_index("gx")
    a = lax.axis_index("af")
    groups, af_size = send_ref.shape[0], send_ref.shape[1]
    k = g // cycle
    c = g % cycle
    offsets = [(db, da) for db in range(groups) for da in range(af_size) if (db, da) != (0, 0)]

    def target(db, da):
        return ((k + db) % groups, (a + da) % af_size)

    barrier = pltpu.get_barrier_semaphore()
    for db, da in offsets:
        tb, ta = target(db, da)
        pl.semaphore_signal(barrier, inc=1, device_id=(tb * cycle + c, ta), device_id_type=MESH)
    pl.semaphore_wait(barrier, len(offsets))

    copies = []
    for n, (db, da) in enumerate(offsets):
        tb, ta = target(db, da)
        copy = pltpu.make_async_remote_copy(
            src_ref=send_ref.at[tb, ta],
            dst_ref=recv.at[n],
            send_sem=send_sem.at[n],
            recv_sem=recv_sem.at[n],
            device_id=(tb * cycle + c, ta),
            device_id_type=MESH,
        )
        copy.start()
        copies.append(copy)
    for copy in copies:
        copy.wait()
    total = send_ref[k, a]
    for n in range(len(offsets)):
        total = total + recv[n]
    o_ref[...] = total


def core_exchange(contributions, cycle):
    groups, af_size = contributions.shape[:2]
    piece = contributions.shape[2:]
    slots = groups * af_size - 1
    return pl.pallas_call(
        functools.partial(core_kernel, cycle),
        out_shape=jax.ShapeDtypeStruct(piece, contributions.dtype),
        in_specs=[pl.BlockSpec(memory_space=pltpu.VMEM)],
        out_specs=pl.BlockSpec(memory_space=pltpu.VMEM),
        scratch_shapes=[
            pltpu.VMEM((slots,) + piece, contributions.dtype),
            pltpu.SemaphoreType.DMA((slots,)),
            pltpu.SemaphoreType.DMA((slots,)),
        ],
        compiler_params=pltpu.CompilerParams(collective_id=1, has_side_effects=True),
    )(contributions)


def body(
    scalar_field, plane_sketch, second_sketch, third_sketch, mixing, plane_targets, plane_signs
):
    planes, rows, cells = scalar_field.shape
    rank_cols = mixing.shape[2]
    gx_index = lax.axis_index("gx")
    af_index = lax.axis_index("af")
    gx_size = lax.axis_size("gx")
    af_size = lax.axis_size("af")

    along_second = jnp.einsum("pjl,lk->pjk", scalar_field, third_sketch, precision=precise)
    partial_second = jnp.einsum(
        "pjk,pk->jk", along_second, plane_sketch[:, 0, :], precision=precise
    )
    along_third = jnp.einsum("pjl,jk->plk", scalar_field, second_sketch, precision=precise)
    partial_third = jnp.einsum("plk,pk->lk", along_third, plane_sketch[:, 1, :], precision=precise)

    range_second_block = jnp.dot(partial_second, mixing[0], precision=precise)
    range_third = jnp.dot(partial_third, mixing[1], precision=precise)
    full_rows = rows * af_size
    range_second = lax.dynamic_update_slice_in_dim(
        jnp.zeros((full_rows, rank_cols), jnp.float32), range_second_block, af_index * rows, 0
    )
    both = allreduce_all(jnp.concatenate([range_second, range_third], axis=0))
    rows_second, rows_third = both[:full_rows], both[full_rows:]

    factor_second_all = orthonormal_rows(rows_second, gram_of(rows_second))
    factor_third_all = orthonormal_rows(rows_third, gram_of(rows_third))

    out_second = full_rows // (gx_size * af_size)
    factor_second = lax.dynamic_slice_in_dim(
        factor_second_all, (af_index * gx_size + gx_index) * out_second, out_second, 0
    )
    factor_third = lax.dynamic_slice_in_dim(
        factor_third_all, (gx_index * af_size + af_index) * out_second, out_second, 0
    )
    basis_second = lax.dynamic_slice_in_dim(factor_second_all, af_index * rows, rows, 0)
    left_side = jnp.einsum("jr,pjl->prl", basis_second, scalar_field, precision=precise)
    projected = jnp.einsum("prl,ls->prs", left_side, factor_third_all, precision=precise)
    cycle = BLOCK // planes
    groups = gx_size // cycle
    assert planes * gx_size == BLOCKS * BLOCK and groups == BLOCKS
    own_targets = lax.dynamic_slice_in_dim(plane_targets, gx_index * planes, planes, 0)
    own_signs = lax.dynamic_slice_in_dim(plane_signs, gx_index * planes, planes, 0)
    sign_values = (2 * own_signs - 1).astype(jnp.float32)
    block_ids = jnp.arange(groups, dtype=jnp.int32)
    weights = jnp.sum(
        jnp.where(own_targets[None, :, :] == block_ids[:, None, None], sign_values[None, :, :], 0.0),
        axis=2,
    )
    slab = rank_cols // af_size
    pieces = projected.reshape(planes, af_size, slab, rank_cols).transpose(1, 0, 2, 3)
    contributions = weights[:, None, :, None, None] * pieces[None]
    core_sketch = core_exchange(contributions, cycle)
    return (factor_second, factor_third, core_sketch)


def solution(mesh):
    in_specs = (P("gx", "af", None), P("gx", None, None), P("af", None), P(), P(), P(), P())
    out_specs = (P(("af", "gx"), None), P(("gx", "af"), None), P("gx", "af", None))
    return jax.shard_map(body, mesh=mesh, in_specs=in_specs, out_specs=out_specs, check_vma=False)
```

```python
import functools

import jax
import jax.numpy as jnp
from jax import lax
from jax.experimental import pallas as pl
from jax.experimental.pallas import tpu as pltpu
from jax.sharding import PartitionSpec as P

MESH = pl.DeviceIdType.MESH

BLOCK = 16
BLOCKS = 8


precise = lax.Precision.HIGHEST


def partner_list(gx_size, af_size):
    steps = []
    bit = 1
    while bit < gx_size:
        steps.append(("gx", bit))
        bit *= 2
    bit = 1
    while bit < af_size:
        steps.append(("af", bit))
        bit *= 2
    return steps


def allreduce_kernel(steps, x_ref, o_ref, recv, send_sem, recv_sem):
    g = lax.axis_index("gx")
    a = lax.axis_index("af")

    def partner(axis, bit):
        if axis == "gx":
            return (lax.bitwise_xor(g, bit), a)
        return (g, lax.bitwise_xor(a, bit))

    barrier = pltpu.get_barrier_semaphore()
    for axis, bit in steps:
        pl.semaphore_signal(barrier, inc=1, device_id=partner(axis, bit), device_id_type=MESH)
    pl.semaphore_wait(barrier, len(steps))

    o_ref[...] = x_ref[...]
    for s, (axis, bit) in enumerate(steps):
        copy = pltpu.make_async_remote_copy(
            src_ref=o_ref,
            dst_ref=recv.at[s],
            send_sem=send_sem.at[s],
            recv_sem=recv_sem.at[s],
            device_id=partner(axis, bit),
            device_id_type=MESH,
        )
        copy.start()
        copy.wait()
        o_ref[...] = o_ref[...] + recv[s]


def allreduce_all(x):
    steps = partner_list(lax.axis_size("gx"), lax.axis_size("af"))
    return pl.pallas_call(
        functools.partial(allreduce_kernel, steps),
        out_shape=jax.ShapeDtypeStruct(x.shape, x.dtype),
        in_specs=[pl.BlockSpec(memory_space=pltpu.VMEM)],
        out_specs=pl.BlockSpec(memory_space=pltpu.VMEM),
        scratch_shapes=[
            pltpu.VMEM((len(steps),) + x.shape, x.dtype),
            pltpu.SemaphoreType.DMA((len(steps),)),
            pltpu.SemaphoreType.DMA((len(steps),)),
        ],
        compiler_params=pltpu.CompilerParams(collective_id=0, has_side_effects=True),
    )(x)


def core_kernel(cycle, send_ref, o_ref, recv, send_sem, recv_sem):
    g = lax.axis_index("gx")
    a = lax.axis_index("af")
    groups, af_size = send_ref.shape[0], send_ref.shape[1]
    k = g // cycle
    c = g % cycle
    offsets = [(db, da) for db in range(groups) for da in range(af_size) if (db, da) != (0, 0)]

    def target(db, da):
        return ((k + db) % groups, (a + da) % af_size)

    barrier = pltpu.get_barrier_semaphore()
    for db, da in offsets:
        tb, ta = target(db, da)
        pl.semaphore_signal(barrier, inc=1, device_id=(tb * cycle + c, ta), device_id_type=MESH)
    pl.semaphore_wait(barrier, len(offsets))

    copies = []
    for n, (db, da) in enumerate(offsets):
        tb, ta = target(db, da)
        copy = pltpu.make_async_remote_copy(
            src_ref=send_ref.at[tb, ta],
            dst_ref=recv.at[n],
            send_sem=send_sem.at[n],
            recv_sem=recv_sem.at[n],
            device_id=(tb * cycle + c, ta),
            device_id_type=MESH,
        )
        copy.start()
        copies.append(copy)
    for copy in copies:
        copy.wait()
    total = send_ref[k, a]
    for n in range(len(offsets)):
        total = total + recv[n]
    o_ref[...] = total


def core_exchange(contributions, cycle):
    groups, af_size = contributions.shape[:2]
    piece = contributions.shape[2:]
    slots = groups * af_size - 1
    return pl.pallas_call(
        functools.partial(core_kernel, cycle),
        out_shape=jax.ShapeDtypeStruct(piece, contributions.dtype),
        in_specs=[pl.BlockSpec(memory_space=pltpu.VMEM)],
        out_specs=pl.BlockSpec(memory_space=pltpu.VMEM),
        scratch_shapes=[
            pltpu.VMEM((slots,) + piece, contributions.dtype),
            pltpu.SemaphoreType.DMA((slots,)),
            pltpu.SemaphoreType.DMA((slots,)),
        ],
        compiler_params=pltpu.CompilerParams(collective_id=1, has_side_effects=True),
    )(contributions)


def body(
    scalar_field, plane_sketch, second_sketch, third_sketch, mixing, plane_targets, plane_signs
):
    planes, rows, cells = scalar_field.shape
    rank_cols = mixing.shape[2]
    gx_index = lax.axis_index("gx")
    af_index = lax.axis_index("af")
    gx_size = lax.axis_size("gx")
    af_size = lax.axis_size("af")

    along_second = jnp.einsum("pjl,lk->pjk", scalar_field, third_sketch, precision=precise)
    partial_second = jnp.einsum(
        "pjk,pk->jk", along_second, plane_sketch[:, 0, :], precision=precise
    )
    along_third = jnp.einsum("pjl,jk->plk", scalar_field, second_sketch, precision=precise)
    partial_third = jnp.einsum("plk,pk->lk", along_third, plane_sketch[:, 1, :], precision=precise)

    range_second_block = jnp.dot(partial_second, mixing[0], precision=precise)
    range_third = jnp.dot(partial_third, mixing[1], precision=precise)
    full_rows = rows * af_size
    range_second = lax.dynamic_update_slice_in_dim(
        jnp.zeros((full_rows, rank_cols), jnp.float32), range_second_block, af_index * rows, 0
    )
    both = allreduce_all(jnp.concatenate([range_second, range_third], axis=0))

    ranges = both.reshape(2, full_rows, rank_cols)
    grams = jnp.einsum("nji,njk->nik", ranges, ranges, precision=precise)
    lower_factors = jnp.linalg.cholesky(grams)
    factors = jax.scipy.linalg.solve_triangular(
        lower_factors, ranges.transpose(0, 2, 1), lower=True
    ).transpose(0, 2, 1)
    factor_second_all, factor_third_all = factors[0], factors[1]

    out_second = full_rows // (gx_size * af_size)
    factor_second = lax.dynamic_slice_in_dim(
        factor_second_all, (af_index * gx_size + gx_index) * out_second, out_second, 0
    )
    factor_third = lax.dynamic_slice_in_dim(
        factor_third_all, (gx_index * af_size + af_index) * out_second, out_second, 0
    )
    basis_second = lax.dynamic_slice_in_dim(factor_second_all, af_index * rows, rows, 0)
    left_side = jnp.einsum("jr,pjl->prl", basis_second, scalar_field, precision=precise)
    projected = jnp.einsum("prl,ls->prs", left_side, factor_third_all, precision=precise)
    cycle = BLOCK // planes
    groups = gx_size // cycle
    assert planes * gx_size == BLOCKS * BLOCK and groups == BLOCKS
    own_targets = lax.dynamic_slice_in_dim(plane_targets, gx_index * planes, planes, 0)
    own_signs = lax.dynamic_slice_in_dim(plane_signs, gx_index * planes, planes, 0)
    sign_values = (2 * own_signs - 1).astype(jnp.float32)
    block_ids = jnp.arange(groups, dtype=jnp.int32)
    weights = jnp.sum(
        jnp.where(own_targets[None, :, :] == block_ids[:, None, None], sign_values[None, :, :], 0.0),
        axis=2,
    )
    slab = rank_cols // af_size
    pieces = projected.reshape(planes, af_size, slab, rank_cols).transpose(1, 0, 2, 3)
    contributions = weights[:, None, :, None, None] * pieces[None]
    core_sketch = core_exchange(contributions, cycle)
    return (factor_second, factor_third, core_sketch)


def solution(mesh):
    in_specs = (P("gx", "af", None), P("gx", None, None), P("af", None), P(), P(), P(), P())
    out_specs = (P(("af", "gx"), None), P(("gx", "af"), None), P("gx", "af", None))
    return jax.shard_map(body, mesh=mesh, in_specs=in_specs, out_specs=out_specs, check_vma=False)
```

```python
import functools

import jax
import jax.numpy as jnp
from jax import lax
from jax.experimental import pallas as pl
from jax.experimental.pallas import tpu as pltpu
from jax.sharding import PartitionSpec as P

MESH = pl.DeviceIdType.MESH

BLOCK = 16
BLOCKS = 8


precise = lax.Precision.HIGHEST


def partner_list(gx_size, af_size):
    preferred = [("gx", 1), ("gx", 2), ("gx", 16), ("af", 1), ("gx", 4), ("gx", 32), ("af", 2), ("gx", 8)]
    sizes = {"gx": gx_size, "af": af_size}
    steps = [(axis, bit) for axis, bit in preferred if bit < sizes[axis]]
    for axis in ("gx", "af"):
        bit = 1
        while bit < sizes[axis]:
            if (axis, bit) not in steps:
                steps.append((axis, bit))
            bit *= 2
    return steps


def allreduce_kernel(steps, x_ref, o_ref, acc, recv, gathered, send_sem, recv_sem):
    index = {"gx": lax.axis_index("gx"), "af": lax.axis_index("af")}

    def partner(axis, bit):
        own = index[axis]
        side = (own // bit) % 2
        other = own + bit - 2 * bit * side
        device = (other, index["af"]) if axis == "gx" else (index["gx"], other)
        return device, side

    barrier = pltpu.get_barrier_semaphore()
    for axis, bit in steps:
        pl.semaphore_signal(barrier, inc=1, device_id=partner(axis, bit)[0], device_id_type=MESH)
    pl.semaphore_wait(barrier, len(steps))

    def send(n, device, source, target):
        copy = pltpu.make_async_remote_copy(
            src_ref=source,
            dst_ref=target,
            send_sem=send_sem.at[n],
            recv_sem=recv_sem.at[n],
            device_id=device,
            device_id_type=MESH,
        )
        copy.start()
        copy.wait()

    acc[...] = x_ref[...]
    offset, length, slot = 0, acc.shape[0], 0
    parents = []
    for n, (axis, bit) in enumerate(steps[:-1]):
        device, side = partner(axis, bit)
        half = length // 2
        give = pl.multiple_of(offset + half * (1 - side), 8)
        keep = pl.multiple_of(offset + half * side, 8)
        send(n, device, acc.at[pl.ds(give, half)], recv.at[pl.ds(slot, half)])
        acc[pl.ds(keep, half), :] = acc[pl.ds(keep, half), :] + recv[pl.ds(slot, half), :]
        parents.append((offset, length))
        offset, length, slot = keep, half, slot + half
    n = len(steps) - 1
    device, side = partner(*steps[-1])
    send(n, device, acc.at[pl.ds(offset, length)], recv.at[pl.ds(slot, length)])
    gathered[pl.ds(offset, length), :] = (
        acc[pl.ds(offset, length), :] + recv[pl.ds(slot, length), :]
    )
    for (axis, bit), (parent_offset, parent_length) in zip(reversed(steps[:-1]), reversed(parents)):
        n += 1
        device, side = partner(axis, bit)
        send(n, device, gathered.at[pl.ds(offset, length)], gathered.at[pl.ds(offset, length)])
        offset, length = parent_offset, parent_length
    o_ref[...] = gathered[...]


def allreduce_all(x):
    steps = partner_list(lax.axis_size("gx"), lax.axis_size("af"))
    assert x.shape[0] % (8 << (len(steps) - 1)) == 0
    return pl.pallas_call(
        functools.partial(allreduce_kernel, steps),
        out_shape=jax.ShapeDtypeStruct(x.shape, x.dtype),
        in_specs=[pl.BlockSpec(memory_space=pltpu.VMEM)],
        out_specs=pl.BlockSpec(memory_space=pltpu.VMEM),
        scratch_shapes=[
            pltpu.VMEM(x.shape, x.dtype),
            pltpu.VMEM(x.shape, x.dtype),
            pltpu.VMEM(x.shape, x.dtype),
            pltpu.SemaphoreType.DMA((2 * len(steps) - 1,)),
            pltpu.SemaphoreType.DMA((2 * len(steps) - 1,)),
        ],
        compiler_params=pltpu.CompilerParams(collective_id=0, has_side_effects=True),
    )(x)


def core_kernel(cycle, send_ref, o_ref, recv, send_sem, recv_sem):
    g = lax.axis_index("gx")
    a = lax.axis_index("af")
    groups, af_size = send_ref.shape[0], send_ref.shape[1]
    k = g // cycle
    c = g % cycle
    offsets = [(db, da) for db in range(groups) for da in range(af_size) if (db, da) != (0, 0)]

    def target(db, da):
        return ((k + db) % groups, (a + da) % af_size)

    barrier = pltpu.get_barrier_semaphore()
    for db, da in offsets:
        tb, ta = target(db, da)
        pl.semaphore_signal(barrier, inc=1, device_id=(tb * cycle + c, ta), device_id_type=MESH)
    pl.semaphore_wait(barrier, len(offsets))

    copies = []
    for n, (db, da) in enumerate(offsets):
        tb, ta = target(db, da)
        copy = pltpu.make_async_remote_copy(
            src_ref=send_ref.at[tb, ta],
            dst_ref=recv.at[n],
            send_sem=send_sem.at[n],
            recv_sem=recv_sem.at[n],
            device_id=(tb * cycle + c, ta),
            device_id_type=MESH,
        )
        copy.start()
        copies.append(copy)
    for copy in copies:
        copy.wait()
    total = send_ref[k, a]
    for n in range(len(offsets)):
        total = total + recv[n]
    o_ref[...] = total


def core_exchange(contributions, cycle):
    groups, af_size = contributions.shape[:2]
    piece = contributions.shape[2:]
    slots = groups * af_size - 1
    return pl.pallas_call(
        functools.partial(core_kernel, cycle),
        out_shape=jax.ShapeDtypeStruct(piece, contributions.dtype),
        in_specs=[pl.BlockSpec(memory_space=pltpu.VMEM)],
        out_specs=pl.BlockSpec(memory_space=pltpu.VMEM),
        scratch_shapes=[
            pltpu.VMEM((slots,) + piece, contributions.dtype),
            pltpu.SemaphoreType.DMA((slots,)),
            pltpu.SemaphoreType.DMA((slots,)),
        ],
        compiler_params=pltpu.CompilerParams(collective_id=1, has_side_effects=True),
    )(contributions)


def body(
    scalar_field, plane_sketch, second_sketch, third_sketch, mixing, plane_targets, plane_signs
):
    planes, rows, cells = scalar_field.shape
    rank_cols = mixing.shape[2]
    gx_index = lax.axis_index("gx")
    af_index = lax.axis_index("af")
    gx_size = lax.axis_size("gx")
    af_size = lax.axis_size("af")

    along_second = jnp.einsum("pjl,lk->pjk", scalar_field, third_sketch, precision=precise)
    partial_second = jnp.einsum(
        "pjk,pk->jk", along_second, plane_sketch[:, 0, :], precision=precise
    )
    along_third = jnp.einsum("pjl,jk->plk", scalar_field, second_sketch, precision=precise)
    partial_third = jnp.einsum("plk,pk->lk", along_third, plane_sketch[:, 1, :], precision=precise)

    range_second_block = jnp.dot(partial_second, mixing[0], precision=precise)
    range_third = jnp.dot(partial_third, mixing[1], precision=precise)
    full_rows = rows * af_size
    range_second = lax.dynamic_update_slice_in_dim(
        jnp.zeros((full_rows, rank_cols), jnp.float32), range_second_block, af_index * rows, 0
    )
    both = allreduce_all(jnp.concatenate([range_second, range_third], axis=0))

    ranges = both.reshape(2, full_rows, rank_cols)
    grams = jnp.einsum("nji,njk->nik", ranges, ranges, precision=precise)
    lower_factors = jnp.linalg.cholesky(grams)
    factors = jax.scipy.linalg.solve_triangular(
        lower_factors, ranges.transpose(0, 2, 1), lower=True
    ).transpose(0, 2, 1)
    factor_second_all, factor_third_all = factors[0], factors[1]

    out_second = full_rows // (gx_size * af_size)
    factor_second = lax.dynamic_slice_in_dim(
        factor_second_all, (af_index * gx_size + gx_index) * out_second, out_second, 0
    )
    factor_third = lax.dynamic_slice_in_dim(
        factor_third_all, (gx_index * af_size + af_index) * out_second, out_second, 0
    )
    basis_second = lax.dynamic_slice_in_dim(factor_second_all, af_index * rows, rows, 0)
    left_side = jnp.einsum("jr,pjl->prl", basis_second, scalar_field, precision=precise)
    projected = jnp.einsum("prl,ls->prs", left_side, factor_third_all, precision=precise)
    cycle = BLOCK // planes
    groups = gx_size // cycle
    assert planes * gx_size == BLOCKS * BLOCK and groups == BLOCKS
    own_targets = lax.dynamic_slice_in_dim(plane_targets, gx_index * planes, planes, 0)
    own_signs = lax.dynamic_slice_in_dim(plane_signs, gx_index * planes, planes, 0)
    sign_values = (2 * own_signs - 1).astype(jnp.float32)
    block_ids = jnp.arange(groups, dtype=jnp.int32)
    weights = jnp.sum(
        jnp.where(own_targets[None, :, :] == block_ids[:, None, None], sign_values[None, :, :], 0.0),
        axis=2,
    )
    slab = rank_cols // af_size
    pieces = projected.reshape(planes, af_size, slab, rank_cols).transpose(1, 0, 2, 3)
    contributions = weights[:, None, :, None, None] * pieces[None]
    core_sketch = core_exchange(contributions, cycle)
    return (factor_second, factor_third, core_sketch)


def solution(mesh):
    in_specs = (P("gx", "af", None), P("gx", None, None), P("af", None), P(), P(), P(), P())
    out_specs = (P(("af", "gx"), None), P(("gx", "af"), None), P("gx", "af", None))
    return jax.shard_map(body, mesh=mesh, in_specs=in_specs, out_specs=out_specs, check_vma=False)
```

```python
import functools

import jax
import jax.numpy as jnp
from jax import lax
from jax.experimental import pallas as pl
from jax.experimental.pallas import tpu as pltpu
from jax.sharding import PartitionSpec as P

MESH = pl.DeviceIdType.MESH

BLOCK = 16
BLOCKS = 8


precise = lax.Precision.HIGHEST


def partner_list(gx_size, af_size):
    preferred = [("gx", 1), ("gx", 2), ("gx", 16), ("af", 1), ("gx", 4), ("gx", 32), ("af", 2), ("gx", 8)]
    sizes = {"gx": gx_size, "af": af_size}
    steps = [(axis, bit) for axis, bit in preferred if bit < sizes[axis]]
    for axis in ("gx", "af"):
        bit = 1
        while bit < sizes[axis]:
            if (axis, bit) not in steps:
                steps.append((axis, bit))
            bit *= 2
    return steps


def allreduce_kernel(steps, x_ref, o_ref, acc, recv, gathered, send_sem, recv_sem):
    index = {"gx": lax.axis_index("gx"), "af": lax.axis_index("af")}

    def partner(axis, bit):
        own = index[axis]
        side = (own // bit) % 2
        other = own + bit - 2 * bit * side
        device = (other, index["af"]) if axis == "gx" else (index["gx"], other)
        return device, side

    barrier = pltpu.get_barrier_semaphore()
    for axis, bit in steps:
        pl.semaphore_signal(barrier, inc=1, device_id=partner(axis, bit)[0], device_id_type=MESH)
    pl.semaphore_wait(barrier, len(steps))

    def send(n, device, source, target):
        copy = pltpu.make_async_remote_copy(
            src_ref=source,
            dst_ref=target,
            send_sem=send_sem.at[n],
            recv_sem=recv_sem.at[n],
            device_id=device,
            device_id_type=MESH,
        )
        copy.start()
        copy.wait()

    acc[...] = x_ref[...]
    offset, length, slot = 0, acc.shape[0], 0
    parents = []
    for n, (axis, bit) in enumerate(steps[:-1]):
        device, side = partner(axis, bit)
        half = length // 2
        give = pl.multiple_of(offset + half * (1 - side), 8)
        keep = pl.multiple_of(offset + half * side, 8)
        send(n, device, acc.at[pl.ds(give, half)], recv.at[pl.ds(slot, half)])
        acc[pl.ds(keep, half), :] = acc[pl.ds(keep, half), :] + recv[pl.ds(slot, half), :]
        parents.append((offset, length))
        offset, length, slot = keep, half, slot + half
    n = len(steps) - 1
    device, side = partner(*steps[-1])
    send(n, device, acc.at[pl.ds(offset, length)], recv.at[pl.ds(slot, length)])
    gathered[pl.ds(offset, length), :] = (
        acc[pl.ds(offset, length), :] + recv[pl.ds(slot, length), :]
    )
    for (axis, bit), (parent_offset, parent_length) in zip(reversed(steps[:-1]), reversed(parents)):
        n += 1
        device, side = partner(axis, bit)
        send(n, device, gathered.at[pl.ds(offset, length)], gathered.at[pl.ds(offset, length)])
        offset, length = parent_offset, parent_length
    o_ref[...] = gathered[...]


def allreduce_all(x):
    steps = partner_list(lax.axis_size("gx"), lax.axis_size("af"))
    assert x.shape[0] % (8 << (len(steps) - 1)) == 0
    return pl.pallas_call(
        functools.partial(allreduce_kernel, steps),
        out_shape=jax.ShapeDtypeStruct(x.shape, x.dtype),
        in_specs=[pl.BlockSpec(memory_space=pltpu.VMEM)],
        out_specs=pl.BlockSpec(memory_space=pltpu.VMEM),
        scratch_shapes=[
            pltpu.VMEM(x.shape, x.dtype),
            pltpu.VMEM(x.shape, x.dtype),
            pltpu.VMEM(x.shape, x.dtype),
            pltpu.SemaphoreType.DMA((2 * len(steps) - 1,)),
            pltpu.SemaphoreType.DMA((2 * len(steps) - 1,)),
        ],
        compiler_params=pltpu.CompilerParams(collective_id=0, has_side_effects=True),
    )(x)


def group_kernel(kind, cycle, send_ref, o_ref, recv, send_sem, recv_sem):
    g = lax.axis_index("gx")
    a = lax.axis_index("af")
    size = send_ref.shape[0]
    if kind == "af":
        me = a

        def device(j):
            return (g, j)
    else:
        me = g // cycle

        def device(j):
            return (j * cycle + g % cycle, a)

    members = [(me + d) % size for d in range(1, size)]
    barrier = pltpu.get_barrier_semaphore()
    for j in members:
        pl.semaphore_signal(barrier, inc=1, device_id=device(j), device_id_type=MESH)
    pl.semaphore_wait(barrier, len(members))

    copies = []
    for n, j in enumerate(members):
        copy = pltpu.make_async_remote_copy(
            src_ref=send_ref.at[j],
            dst_ref=recv.at[n],
            send_sem=send_sem.at[n],
            recv_sem=recv_sem.at[n],
            device_id=device(j),
            device_id_type=MESH,
        )
        copy.start()
        copies.append(copy)
    for copy in copies:
        copy.wait()
    total = send_ref[me]
    for n in range(len(members)):
        total = total + recv[n]
    o_ref[...] = total


def group_sum(pieces, kind, cycle, collective_id):
    size = pieces.shape[0]
    piece = pieces.shape[1:]
    return pl.pallas_call(
        functools.partial(group_kernel, kind, cycle),
        out_shape=jax.ShapeDtypeStruct(piece, pieces.dtype),
        in_specs=[pl.BlockSpec(memory_space=pltpu.VMEM)],
        out_specs=pl.BlockSpec(memory_space=pltpu.VMEM),
        scratch_shapes=[
            pltpu.VMEM((size - 1,) + piece, pieces.dtype),
            pltpu.SemaphoreType.DMA((size - 1,)),
            pltpu.SemaphoreType.DMA((size - 1,)),
        ],
        compiler_params=pltpu.CompilerParams(collective_id=collective_id, has_side_effects=True),
    )(pieces)


def body(
    scalar_field, plane_sketch, second_sketch, third_sketch, mixing, plane_targets, plane_signs
):
    planes, rows, cells = scalar_field.shape
    rank_cols = mixing.shape[2]
    gx_index = lax.axis_index("gx")
    af_index = lax.axis_index("af")
    gx_size = lax.axis_size("gx")
    af_size = lax.axis_size("af")

    along_second = jnp.einsum("pjl,lk->pjk", scalar_field, third_sketch, precision=precise)
    partial_second = jnp.einsum(
        "pjk,pk->jk", along_second, plane_sketch[:, 0, :], precision=precise
    )
    along_third = jnp.einsum("pjl,jk->plk", scalar_field, second_sketch, precision=precise)
    partial_third = jnp.einsum("plk,pk->lk", along_third, plane_sketch[:, 1, :], precision=precise)

    range_second_block = jnp.dot(partial_second, mixing[0], precision=precise)
    range_third = jnp.dot(partial_third, mixing[1], precision=precise)
    full_rows = rows * af_size
    range_second = lax.dynamic_update_slice_in_dim(
        jnp.zeros((full_rows, rank_cols), jnp.float32), range_second_block, af_index * rows, 0
    )
    both = allreduce_all(jnp.concatenate([range_second, range_third], axis=0))

    ranges = both.reshape(2, full_rows, rank_cols)
    grams = jnp.einsum("nji,njk->nik", ranges, ranges, precision=precise)
    lower_factors = jnp.linalg.cholesky(grams)
    factors = jax.scipy.linalg.solve_triangular(
        lower_factors, ranges.transpose(0, 2, 1), lower=True
    ).transpose(0, 2, 1)
    factor_second_all, factor_third_all = factors[0], factors[1]

    out_second = full_rows // (gx_size * af_size)
    factor_second = lax.dynamic_slice_in_dim(
        factor_second_all, (af_index * gx_size + gx_index) * out_second, out_second, 0
    )
    factor_third = lax.dynamic_slice_in_dim(
        factor_third_all, (gx_index * af_size + af_index) * out_second, out_second, 0
    )
    basis_second = lax.dynamic_slice_in_dim(factor_second_all, af_index * rows, rows, 0)
    left_side = jnp.einsum("jr,pjl->prl", basis_second, scalar_field, precision=precise)
    projected = jnp.einsum("prl,ls->prs", left_side, factor_third_all, precision=precise)
    cycle = BLOCK // planes
    groups = gx_size // cycle
    assert planes * gx_size == BLOCKS * BLOCK and groups == BLOCKS
    own_targets = lax.dynamic_slice_in_dim(plane_targets, gx_index * planes, planes, 0)
    own_signs = lax.dynamic_slice_in_dim(plane_signs, gx_index * planes, planes, 0)
    sign_values = (2 * own_signs - 1).astype(jnp.float32)
    block_ids = jnp.arange(groups, dtype=jnp.int32)
    weights = jnp.sum(
        jnp.where(own_targets[None, :, :] == block_ids[:, None, None], sign_values[None, :, :], 0.0),
        axis=2,
    )
    slab = rank_cols // af_size
    pieces = projected.reshape(planes, af_size, slab, rank_cols).transpose(1, 0, 2, 3)
    summed = group_sum(pieces, "af", cycle, 1)
    contributions = weights[:, :, None, None] * summed[None]
    core_sketch = group_sum(contributions, "gx", cycle, 2)
    return (factor_second, factor_third, core_sketch)


def solution(mesh):
    in_specs = (P("gx", "af", None), P("gx", None, None), P("af", None), P(), P(), P(), P())
    out_specs = (P(("af", "gx"), None), P(("gx", "af"), None), P("gx", "af", None))
    return jax.shard_map(body, mesh=mesh, in_specs=in_specs, out_specs=out_specs, check_vma=False)
```

```python
import functools

import jax
import jax.numpy as jnp
from jax import lax
from jax.experimental import pallas as pl
from jax.experimental.pallas import tpu as pltpu
from jax.sharding import PartitionSpec as P

MESH = pl.DeviceIdType.MESH

BLOCK = 16
BLOCKS = 8


precise = lax.Precision.HIGHEST


def partner_list(gx_size, af_size):
    preferred = [("gx", 1), ("gx", 2), ("gx", 16), ("af", 1), ("gx", 4), ("gx", 32), ("af", 2), ("gx", 8)]
    sizes = {"gx": gx_size, "af": af_size}
    steps = [(axis, bit) for axis, bit in preferred if bit < sizes[axis]]
    for axis in ("gx", "af"):
        bit = 1
        while bit < sizes[axis]:
            if (axis, bit) not in steps:
                steps.append((axis, bit))
            bit *= 2
    return steps


def allreduce_kernel(digits, x_ref, o_ref, acc, recv, exchange, gathered, send_sem, recv_sem):
    index = {"gx": lax.axis_index("gx"), "af": lax.axis_index("af")}

    def bits_of(digit):
        return [(index[axis] // bit) % 2 for axis, bit in digit]

    def member(digit):
        own = bits_of(digit)
        return own[0] + 2 * own[1]

    def device(digit, d):
        values = dict(index)
        for t, ((axis, bit), own) in enumerate(zip(digit, bits_of(digit))):
            flip = (d >> t) & 1
            values[axis] = values[axis] + bit * flip * (1 - 2 * own)
        return (values["gx"], values["af"])

    barrier = pltpu.get_barrier_semaphore()
    for digit in digits:
        for d in (1, 2, 3):
            pl.semaphore_signal(barrier, inc=1, device_id=device(digit, d), device_id_type=MESH)
    pl.semaphore_wait(barrier, 3 * len(digits))

    counter = [0]

    def start(device_id, source, target):
        n = counter[0]
        counter[0] += 1
        copy = pltpu.make_async_remote_copy(
            src_ref=source,
            dst_ref=target,
            send_sem=send_sem.at[n],
            recv_sem=recv_sem.at[n],
            device_id=device_id,
            device_id_type=MESH,
        )
        copy.start()
        return copy

    def flipped(me, d):
        low, high = me % 2, me // 2
        low = low + (d & 1) * (1 - 2 * low)
        high = high + ((d >> 1) & 1) * (1 - 2 * high)
        return low + 2 * high

    acc[...] = x_ref[...]
    offset, length, slot = 0, acc.shape[0], 0
    parents = []
    for digit in digits[:-1]:
        me = member(digit)
        quarter = length // 4
        copies = []
        for d in (1, 2, 3):
            give = pl.multiple_of(offset + flipped(me, d) * quarter, 8)
            target = recv.at[pl.ds(slot + (d - 1) * quarter, quarter)]
            copies.append(start(device(digit, d), acc.at[pl.ds(give, quarter)], target))
        for copy in copies:
            copy.wait()
        keep = pl.multiple_of(offset + me * quarter, 8)
        total = acc[pl.ds(keep, quarter), :]
        for d in (1, 2, 3):
            total = total + recv[pl.ds(slot + (d - 1) * quarter, quarter), :]
        acc[pl.ds(keep, quarter), :] = total
        parents.append((offset, length))
        offset, length, slot = keep, quarter, slot + 3 * quarter

    last = digits[-1]
    me = member(last)
    segment = acc.at[pl.ds(offset, length)]
    copies = [start(device(last, d), segment, exchange.at[me]) for d in (1, 2, 3)]
    exchange[me] = acc[pl.ds(offset, length), :]
    for copy in copies:
        copy.wait()
    gathered[pl.ds(offset, length), :] = ((exchange[0] + exchange[1]) + exchange[2]) + exchange[3]

    for digit, (parent_offset, parent_length) in zip(reversed(digits[:-1]), reversed(parents)):
        part = gathered.at[pl.ds(offset, length)]
        copies = [start(device(digit, d), part, part) for d in (1, 2, 3)]
        for copy in copies:
            copy.wait()
        offset, length = parent_offset, parent_length
    o_ref[...] = gathered[...]


def allreduce_all(x):
    steps = partner_list(lax.axis_size("gx"), lax.axis_size("af"))
    assert len(steps) % 2 == 0
    digits = [steps[t:t + 2] for t in range(0, len(steps), 2)]
    last_rows = x.shape[0] // 4 ** (len(digits) - 1)
    assert last_rows % 8 == 0
    copies = 3 * (2 * len(digits) - 1)
    return pl.pallas_call(
        functools.partial(allreduce_kernel, digits),
        out_shape=jax.ShapeDtypeStruct(x.shape, x.dtype),
        in_specs=[pl.BlockSpec(memory_space=pltpu.VMEM)],
        out_specs=pl.BlockSpec(memory_space=pltpu.VMEM),
        scratch_shapes=[
            pltpu.VMEM(x.shape, x.dtype),
            pltpu.VMEM(x.shape, x.dtype),
            pltpu.VMEM((4, last_rows) + x.shape[1:], x.dtype),
            pltpu.VMEM(x.shape, x.dtype),
            pltpu.SemaphoreType.DMA((copies,)),
            pltpu.SemaphoreType.DMA((copies,)),
        ],
        compiler_params=pltpu.CompilerParams(collective_id=0, has_side_effects=True),
    )(x)


def group_kernel(kind, cycle, send_ref, o_ref, recv, send_sem, recv_sem):
    g = lax.axis_index("gx")
    a = lax.axis_index("af")
    size = send_ref.shape[0]
    if kind == "af":
        me = a

        def device(j):
            return (g, j)
    else:
        me = g // cycle

        def device(j):
            return (j * cycle + g % cycle, a)

    members = [(me + d) % size for d in range(1, size)]
    barrier = pltpu.get_barrier_semaphore()
    for j in members:
        pl.semaphore_signal(barrier, inc=1, device_id=device(j), device_id_type=MESH)
    pl.semaphore_wait(barrier, len(members))

    copies = []
    for n, j in enumerate(members):
        copy = pltpu.make_async_remote_copy(
            src_ref=send_ref.at[j],
            dst_ref=recv.at[n],
            send_sem=send_sem.at[n],
            recv_sem=recv_sem.at[n],
            device_id=device(j),
            device_id_type=MESH,
        )
        copy.start()
        copies.append(copy)
    for copy in copies:
        copy.wait()
    total = send_ref[me]
    for n in range(len(members)):
        total = total + recv[n]
    o_ref[...] = total


def group_sum(pieces, kind, cycle, collective_id):
    size = pieces.shape[0]
    piece = pieces.shape[1:]
    return pl.pallas_call(
        functools.partial(group_kernel, kind, cycle),
        out_shape=jax.ShapeDtypeStruct(piece, pieces.dtype),
        in_specs=[pl.BlockSpec(memory_space=pltpu.VMEM)],
        out_specs=pl.BlockSpec(memory_space=pltpu.VMEM),
        scratch_shapes=[
            pltpu.VMEM((size - 1,) + piece, pieces.dtype),
            pltpu.SemaphoreType.DMA((size - 1,)),
            pltpu.SemaphoreType.DMA((size - 1,)),
        ],
        compiler_params=pltpu.CompilerParams(collective_id=collective_id, has_side_effects=True),
    )(pieces)


def body(
    scalar_field, plane_sketch, second_sketch, third_sketch, mixing, plane_targets, plane_signs
):
    planes, rows, cells = scalar_field.shape
    rank_cols = mixing.shape[2]
    gx_index = lax.axis_index("gx")
    af_index = lax.axis_index("af")
    gx_size = lax.axis_size("gx")
    af_size = lax.axis_size("af")

    along_second = jnp.einsum("pjl,lk->pjk", scalar_field, third_sketch, precision=precise)
    partial_second = jnp.einsum(
        "pjk,pk->jk", along_second, plane_sketch[:, 0, :], precision=precise
    )
    along_third = jnp.einsum("pjl,jk->plk", scalar_field, second_sketch, precision=precise)
    partial_third = jnp.einsum("plk,pk->lk", along_third, plane_sketch[:, 1, :], precision=precise)

    range_second_block = jnp.dot(partial_second, mixing[0], precision=precise)
    range_third = jnp.dot(partial_third, mixing[1], precision=precise)
    full_rows = rows * af_size
    range_second = lax.dynamic_update_slice_in_dim(
        jnp.zeros((full_rows, rank_cols), jnp.float32), range_second_block, af_index * rows, 0
    )
    both = allreduce_all(jnp.concatenate([range_second, range_third], axis=0))

    ranges = both.reshape(2, full_rows, rank_cols)
    grams = jnp.einsum("nji,njk->nik", ranges, ranges, precision=precise)
    lower_factors = jnp.linalg.cholesky(grams)
    factors = jax.scipy.linalg.solve_triangular(
        lower_factors, ranges.transpose(0, 2, 1), lower=True
    ).transpose(0, 2, 1)
    factor_second_all, factor_third_all = factors[0], factors[1]

    out_second = full_rows // (gx_size * af_size)
    factor_second = lax.dynamic_slice_in_dim(
        factor_second_all, (af_index * gx_size + gx_index) * out_second, out_second, 0
    )
    factor_third = lax.dynamic_slice_in_dim(
        factor_third_all, (gx_index * af_size + af_index) * out_second, out_second, 0
    )
    basis_second = lax.dynamic_slice_in_dim(factor_second_all, af_index * rows, rows, 0)
    left_side = jnp.einsum("jr,pjl->prl", basis_second, scalar_field, precision=precise)
    projected = jnp.einsum("prl,ls->prs", left_side, factor_third_all, precision=precise)
    cycle = BLOCK // planes
    groups = gx_size // cycle
    assert planes * gx_size == BLOCKS * BLOCK and groups == BLOCKS
    own_targets = lax.dynamic_slice_in_dim(plane_targets, gx_index * planes, planes, 0)
    own_signs = lax.dynamic_slice_in_dim(plane_signs, gx_index * planes, planes, 0)
    sign_values = (2 * own_signs - 1).astype(jnp.float32)
    block_ids = jnp.arange(groups, dtype=jnp.int32)
    weights = jnp.sum(
        jnp.where(own_targets[None, :, :] == block_ids[:, None, None], sign_values[None, :, :], 0.0),
        axis=2,
    )
    slab = rank_cols // af_size
    pieces = projected.reshape(planes, af_size, slab, rank_cols).transpose(1, 0, 2, 3)
    summed = group_sum(pieces, "af", cycle, 1)
    contributions = weights[:, :, None, None] * summed[None]
    core_sketch = group_sum(contributions, "gx", cycle, 2)
    return (factor_second, factor_third, core_sketch)


def solution(mesh):
    in_specs = (P("gx", "af", None), P("gx", None, None), P("af", None), P(), P(), P(), P())
    out_specs = (P(("af", "gx"), None), P(("gx", "af"), None), P("gx", "af", None))
    return jax.shard_map(body, mesh=mesh, in_specs=in_specs, out_specs=out_specs, check_vma=False)
```

```python
import functools

import jax
import jax.numpy as jnp
from jax import lax
from jax.experimental import pallas as pl
from jax.experimental.pallas import tpu as pltpu
from jax.sharding import PartitionSpec as P

MESH = pl.DeviceIdType.MESH

BLOCK = 16
BLOCKS = 8


precise = lax.Precision.HIGHEST


def partner_list(gx_size, af_size):
    preferred = [("gx", 1), ("gx", 2), ("gx", 16), ("af", 1), ("gx", 4), ("gx", 32), ("af", 2), ("gx", 8)]
    sizes = {"gx": gx_size, "af": af_size}
    steps = [(axis, bit) for axis, bit in preferred if bit < sizes[axis]]
    for axis in ("gx", "af"):
        bit = 1
        while bit < sizes[axis]:
            if (axis, bit) not in steps:
                steps.append((axis, bit))
            bit *= 2
    return steps


def allreduce_kernel(digits, x_ref, o_ref, acc, recv, exchange, gathered, send_sem, recv_sem):
    index = {"gx": lax.axis_index("gx"), "af": lax.axis_index("af")}

    def bits_of(digit):
        return [(index[axis] // bit) % 2 for axis, bit in digit]

    def member(digit):
        own = bits_of(digit)
        return own[0] + 2 * own[1]

    def device(digit, d):
        values = dict(index)
        for t, ((axis, bit), own) in enumerate(zip(digit, bits_of(digit))):
            flip = (d >> t) & 1
            values[axis] = values[axis] + bit * flip * (1 - 2 * own)
        return (values["gx"], values["af"])

    barrier = pltpu.get_barrier_semaphore()
    for digit in digits:
        for d in (1, 2, 3):
            pl.semaphore_signal(barrier, inc=1, device_id=device(digit, d), device_id_type=MESH)
    pl.semaphore_wait(barrier, 3 * len(digits))

    counter = [0]

    def start(device_id, source, target):
        n = counter[0]
        counter[0] += 1
        copy = pltpu.make_async_remote_copy(
            src_ref=source,
            dst_ref=target,
            send_sem=send_sem.at[n],
            recv_sem=recv_sem.at[n],
            device_id=device_id,
            device_id_type=MESH,
        )
        copy.start()
        return copy

    def flipped(me, d):
        low, high = me % 2, me // 2
        low = low + (d & 1) * (1 - 2 * low)
        high = high + ((d >> 1) & 1) * (1 - 2 * high)
        return low + 2 * high

    acc[...] = x_ref[...]
    offset, length, slot = 0, acc.shape[0], 0
    parents = []
    for digit in digits[:-1]:
        me = member(digit)
        quarter = length // 4
        copies = []
        for d in (1, 2, 3):
            give = pl.multiple_of(offset + flipped(me, d) * quarter, 8)
            target = recv.at[pl.ds(slot + (d - 1) * quarter, quarter)]
            copies.append(start(device(digit, d), acc.at[pl.ds(give, quarter)], target))
        for copy in copies:
            copy.wait()
        keep = pl.multiple_of(offset + me * quarter, 8)
        total = acc[pl.ds(keep, quarter), :]
        for d in (1, 2, 3):
            total = total + recv[pl.ds(slot + (d - 1) * quarter, quarter), :]
        acc[pl.ds(keep, quarter), :] = total
        parents.append((offset, length))
        offset, length, slot = keep, quarter, slot + 3 * quarter

    last = digits[-1]
    me = member(last)
    segment = acc.at[pl.ds(offset, length)]
    copies = [start(device(last, d), segment, exchange.at[me]) for d in (1, 2, 3)]
    exchange[me] = acc[pl.ds(offset, length), :]
    for copy in copies:
        copy.wait()
    gathered[pl.ds(offset, length), :] = ((exchange[0] + exchange[1]) + exchange[2]) + exchange[3]

    for digit, (parent_offset, parent_length) in zip(reversed(digits[:-1]), reversed(parents)):
        part = gathered.at[pl.ds(offset, length)]
        copies = [start(device(digit, d), part, part) for d in (1, 2, 3)]
        for copy in copies:
            copy.wait()
        offset, length = parent_offset, parent_length
    o_ref[...] = gathered[...]


def allreduce_all(x):
    steps = partner_list(lax.axis_size("gx"), lax.axis_size("af"))
    assert len(steps) % 2 == 0
    digits = [steps[t:t + 2] for t in range(0, len(steps), 2)]
    last_rows = x.shape[0] // 4 ** (len(digits) - 1)
    assert last_rows % 8 == 0
    copies = 3 * (2 * len(digits) - 1)
    return pl.pallas_call(
        functools.partial(allreduce_kernel, digits),
        out_shape=jax.ShapeDtypeStruct(x.shape, x.dtype),
        in_specs=[pl.BlockSpec(memory_space=pltpu.VMEM)],
        out_specs=pl.BlockSpec(memory_space=pltpu.VMEM),
        scratch_shapes=[
            pltpu.VMEM(x.shape, x.dtype),
            pltpu.VMEM(x.shape, x.dtype),
            pltpu.VMEM((4, last_rows) + x.shape[1:], x.dtype),
            pltpu.VMEM(x.shape, x.dtype),
            pltpu.SemaphoreType.DMA((copies,)),
            pltpu.SemaphoreType.DMA((copies,)),
        ],
        compiler_params=pltpu.CompilerParams(collective_id=0, has_side_effects=True),
    )(x)


def panel_kernel(*refs):
    count = len(refs) // 2
    inputs, outputs = refs[:count], refs[count:]
    for source, target in zip(inputs, outputs):
        target[...] = source[...]
    rank = outputs[0].shape[0]

    def step(j, carry):
        for ref in outputs:
            width = ref.shape[1]
            row = ref[pl.ds(j, 1), :]
            lanes = lax.broadcasted_iota(jnp.int32, (1, width), 1)
            pivot = jnp.sum(jnp.where(lanes == j, row, 0.0), axis=1, keepdims=True)
            root = jnp.sqrt(pivot)
            column = jnp.where(lanes < j, 0.0, row / root)
            square = ref[:, pl.ds(0, rank)]
            cols = lax.broadcasted_iota(jnp.int32, (rank, rank), 1)
            upper = jnp.sum(jnp.where(cols == j, square, 0.0), axis=1, keepdims=True)
            below = lax.broadcasted_iota(jnp.int32, (rank, 1), 0) > j
            scale = jnp.where(below, upper / root, 0.0)
            ref[...] = ref[...] - scale * column
            ref[pl.ds(j, 1), :] = column
        return carry

    lax.fori_loop(0, rank, step, 0)


def factor_panels(*panels):
    return pl.pallas_call(
        panel_kernel,
        out_shape=[jax.ShapeDtypeStruct(p.shape, p.dtype) for p in panels],
        in_specs=[pl.BlockSpec(memory_space=pltpu.VMEM)] * len(panels),
        out_specs=[pl.BlockSpec(memory_space=pltpu.VMEM)] * len(panels),
    )(*panels)


def group_kernel(kind, cycle, send_ref, o_ref, recv, send_sem, recv_sem):
    g = lax.axis_index("gx")
    a = lax.axis_index("af")
    size = send_ref.shape[0]
    if kind == "af":
        me = a

        def device(j):
            return (g, j)
    else:
        me = g // cycle

        def device(j):
            return (j * cycle + g % cycle, a)

    members = [(me + d) % size for d in range(1, size)]
    barrier = pltpu.get_barrier_semaphore()
    for j in members:
        pl.semaphore_signal(barrier, inc=1, device_id=device(j), device_id_type=MESH)
    pl.semaphore_wait(barrier, len(members))

    copies = []
    for n, j in enumerate(members):
        copy = pltpu.make_async_remote_copy(
            src_ref=send_ref.at[j],
            dst_ref=recv.at[n],
            send_sem=send_sem.at[n],
            recv_sem=recv_sem.at[n],
            device_id=device(j),
            device_id_type=MESH,
        )
        copy.start()
        copies.append(copy)
    for copy in copies:
        copy.wait()
    total = send_ref[me]
    for n in range(len(members)):
        total = total + recv[n]
    o_ref[...] = total


def group_sum(pieces, kind, cycle, collective_id):
    size = pieces.shape[0]
    piece = pieces.shape[1:]
    return pl.pallas_call(
        functools.partial(group_kernel, kind, cycle),
        out_shape=jax.ShapeDtypeStruct(piece, pieces.dtype),
        in_specs=[pl.BlockSpec(memory_space=pltpu.VMEM)],
        out_specs=pl.BlockSpec(memory_space=pltpu.VMEM),
        scratch_shapes=[
            pltpu.VMEM((size - 1,) + piece, pieces.dtype),
            pltpu.SemaphoreType.DMA((size - 1,)),
            pltpu.SemaphoreType.DMA((size - 1,)),
        ],
        compiler_params=pltpu.CompilerParams(collective_id=collective_id, has_side_effects=True),
    )(pieces)


def body(
    scalar_field, plane_sketch, second_sketch, third_sketch, mixing, plane_targets, plane_signs
):
    planes, rows, cells = scalar_field.shape
    rank_cols = mixing.shape[2]
    gx_index = lax.axis_index("gx")
    af_index = lax.axis_index("af")
    gx_size = lax.axis_size("gx")
    af_size = lax.axis_size("af")

    along_second = jnp.einsum("pjl,lk->pjk", scalar_field, third_sketch, precision=precise)
    partial_second = jnp.einsum(
        "pjk,pk->jk", along_second, plane_sketch[:, 0, :], precision=precise
    )
    along_third = jnp.einsum("pjl,jk->plk", scalar_field, second_sketch, precision=precise)
    partial_third = jnp.einsum("plk,pk->lk", along_third, plane_sketch[:, 1, :], precision=precise)

    range_second_block = jnp.dot(partial_second, mixing[0], precision=precise)
    range_third = jnp.dot(partial_third, mixing[1], precision=precise)
    full_rows = rows * af_size
    range_second = lax.dynamic_update_slice_in_dim(
        jnp.zeros((full_rows, rank_cols), jnp.float32), range_second_block, af_index * rows, 0
    )
    both = allreduce_all(jnp.concatenate([range_second, range_third], axis=0))

    ranges = both.reshape(2, full_rows, rank_cols)
    grams = jnp.einsum("nji,njk->nik", ranges, ranges, precision=precise)
    own_second = lax.dynamic_slice_in_dim(ranges[0], af_index * rows, rows, 0)
    panel_third, panel_second = factor_panels(
        jnp.concatenate([grams[1], ranges[1].T], axis=1),
        jnp.concatenate([grams[0], own_second.T], axis=1),
    )
    factor_third_all = panel_third[:, rank_cols:].T
    basis_second = panel_second[:, rank_cols:].T

    out_second = full_rows // (gx_size * af_size)
    assert rows == gx_size * out_second
    factor_second = lax.dynamic_slice_in_dim(basis_second, gx_index * out_second, out_second, 0)
    factor_third = lax.dynamic_slice_in_dim(
        factor_third_all, (gx_index * af_size + af_index) * out_second, out_second, 0
    )
    left_side = jnp.einsum("jr,pjl->prl", basis_second, scalar_field, precision=precise)
    projected = jnp.einsum("prl,ls->prs", left_side, factor_third_all, precision=precise)
    cycle = BLOCK // planes
    groups = gx_size // cycle
    assert planes * gx_size == BLOCKS * BLOCK and groups == BLOCKS
    own_targets = lax.dynamic_slice_in_dim(plane_targets, gx_index * planes, planes, 0)
    own_signs = lax.dynamic_slice_in_dim(plane_signs, gx_index * planes, planes, 0)
    sign_values = (2 * own_signs - 1).astype(jnp.float32)
    block_ids = jnp.arange(groups, dtype=jnp.int32)
    weights = jnp.sum(
        jnp.where(own_targets[None, :, :] == block_ids[:, None, None], sign_values[None, :, :], 0.0),
        axis=2,
    )
    slab = rank_cols // af_size
    pieces = projected.reshape(planes, af_size, slab, rank_cols).transpose(1, 0, 2, 3)
    summed = group_sum(pieces, "af", cycle, 1)
    contributions = weights[:, :, None, None] * summed[None]
    core_sketch = group_sum(contributions, "gx", cycle, 2)
    return (factor_second, factor_third, core_sketch)


def solution(mesh):
    in_specs = (P("gx", "af", None), P("gx", None, None), P("af", None), P(), P(), P(), P())
    out_specs = (P(("af", "gx"), None), P(("gx", "af"), None), P("gx", "af", None))
    return jax.shard_map(body, mesh=mesh, in_specs=in_specs, out_specs=out_specs, check_vma=False)
```

```python
import functools

import jax
import jax.numpy as jnp
from jax import lax
from jax.experimental import pallas as pl
from jax.experimental.pallas import tpu as pltpu
from jax.sharding import PartitionSpec as P

MESH = pl.DeviceIdType.MESH

BLOCK = 16
BLOCKS = 8


precise = lax.Precision.HIGHEST


def partner_list(gx_size, af_size):
    preferred = [("gx", 1), ("gx", 2), ("gx", 16), ("af", 1), ("gx", 4), ("gx", 32), ("af", 2), ("gx", 8)]
    sizes = {"gx": gx_size, "af": af_size}
    steps = [(axis, bit) for axis, bit in preferred if bit < sizes[axis]]
    for axis in ("gx", "af"):
        bit = 1
        while bit < sizes[axis]:
            if (axis, bit) not in steps:
                steps.append((axis, bit))
            bit *= 2
    return steps


def allreduce_kernel(digits, x_ref, o_ref, acc, recv, exchange, gathered, send_sem, recv_sem):
    index = {"gx": lax.axis_index("gx"), "af": lax.axis_index("af")}

    def bits_of(digit):
        return [(index[axis] // bit) % 2 for axis, bit in digit]

    def member(digit):
        own = bits_of(digit)
        return own[0] + 2 * own[1]

    def device(digit, d):
        values = dict(index)
        for t, ((axis, bit), own) in enumerate(zip(digit, bits_of(digit))):
            flip = (d >> t) & 1
            values[axis] = values[axis] + bit * flip * (1 - 2 * own)
        return (values["gx"], values["af"])

    barrier = pltpu.get_barrier_semaphore()
    for digit in digits:
        for d in (1, 2, 3):
            pl.semaphore_signal(barrier, inc=1, device_id=device(digit, d), device_id_type=MESH)
    pl.semaphore_wait(barrier, 3 * len(digits))

    counter = [0]

    def start(device_id, source, target):
        n = counter[0]
        counter[0] += 1
        copy = pltpu.make_async_remote_copy(
            src_ref=source,
            dst_ref=target,
            send_sem=send_sem.at[n],
            recv_sem=recv_sem.at[n],
            device_id=device_id,
            device_id_type=MESH,
        )
        copy.start()
        return copy

    def flipped(me, d):
        low, high = me % 2, me // 2
        low = low + (d & 1) * (1 - 2 * low)
        high = high + ((d >> 1) & 1) * (1 - 2 * high)
        return low + 2 * high

    acc[...] = x_ref[...]
    offset, length, slot = 0, acc.shape[0], 0
    parents = []
    for digit in digits[:-1]:
        me = member(digit)
        quarter = length // 4
        copies = []
        for d in (1, 2, 3):
            give = pl.multiple_of(offset + flipped(me, d) * quarter, 8)
            target = recv.at[pl.ds(slot + (d - 1) * quarter, quarter)]
            copies.append(start(device(digit, d), acc.at[pl.ds(give, quarter)], target))
        for copy in copies:
            copy.wait()
        keep = pl.multiple_of(offset + me * quarter, 8)
        total = acc[pl.ds(keep, quarter), :]
        for d in (1, 2, 3):
            total = total + recv[pl.ds(slot + (d - 1) * quarter, quarter), :]
        acc[pl.ds(keep, quarter), :] = total
        parents.append((offset, length))
        offset, length, slot = keep, quarter, slot + 3 * quarter

    last = digits[-1]
    me = member(last)
    segment = acc.at[pl.ds(offset, length)]
    copies = [start(device(last, d), segment, exchange.at[me]) for d in (1, 2, 3)]
    exchange[me] = acc[pl.ds(offset, length), :]
    for copy in copies:
        copy.wait()
    gathered[pl.ds(offset, length), :] = ((exchange[0] + exchange[1]) + exchange[2]) + exchange[3]

    for digit, (parent_offset, parent_length) in zip(reversed(digits[:-1]), reversed(parents)):
        part = gathered.at[pl.ds(offset, length)]
        copies = [start(device(digit, d), part, part) for d in (1, 2, 3)]
        for copy in copies:
            copy.wait()
        offset, length = parent_offset, parent_length
    o_ref[...] = gathered[...]


def allreduce_all(x):
    steps = partner_list(lax.axis_size("gx"), lax.axis_size("af"))
    assert len(steps) % 2 == 0
    digits = [steps[t:t + 2] for t in range(0, len(steps), 2)]
    last_rows = x.shape[0] // 4 ** (len(digits) - 1)
    assert last_rows % 8 == 0
    copies = 3 * (2 * len(digits) - 1)
    return pl.pallas_call(
        functools.partial(allreduce_kernel, digits),
        out_shape=jax.ShapeDtypeStruct(x.shape, x.dtype),
        in_specs=[pl.BlockSpec(memory_space=pltpu.VMEM)],
        out_specs=pl.BlockSpec(memory_space=pltpu.VMEM),
        scratch_shapes=[
            pltpu.VMEM(x.shape, x.dtype),
            pltpu.VMEM(x.shape, x.dtype),
            pltpu.VMEM((4, last_rows) + x.shape[1:], x.dtype),
            pltpu.VMEM(x.shape, x.dtype),
            pltpu.SemaphoreType.DMA((copies,)),
            pltpu.SemaphoreType.DMA((copies,)),
        ],
        compiler_params=pltpu.CompilerParams(collective_id=0, has_side_effects=True),
    )(x)


def panel_kernel(*refs):
    count = len(refs) // 2
    inputs, outputs = refs[:count], refs[count:]
    for source, target in zip(inputs, outputs):
        target[...] = source[...]
    rank = outputs[0].shape[0]

    def step(j, carry):
        columns, roots = [], []
        for ref in outputs:
            width = ref.shape[1]
            row = ref[pl.ds(j, 1), :]
            lanes = lax.broadcasted_iota(jnp.int32, (1, width), 1)
            pivot = jnp.sum(jnp.where(lanes == j, row, 0.0), axis=1, keepdims=True)
            root = jnp.sqrt(pivot)
            columns.append(jnp.where(lanes < j, 0.0, row / root))
            roots.append(root)

        def chunk(i, inner):
            rows = pl.ds(pl.multiple_of(i * 8, 8), 8)
            below = lax.broadcasted_iota(jnp.int32, (8, 1), 0) + i * 8 > j
            cols = lax.broadcasted_iota(jnp.int32, (8, rank), 1)
            for ref, column, root in zip(outputs, columns, roots):
                block = ref[rows, :]
                upper = jnp.sum(jnp.where(cols == j, block[:, :rank], 0.0), axis=1, keepdims=True)
                scale = jnp.where(below, upper / root, 0.0)
                ref[rows, :] = block - scale * column
            return inner

        lax.fori_loop(j // 8, rank // 8, chunk, 0)
        for ref, column in zip(outputs, columns):
            ref[pl.ds(j, 1), :] = column
        return carry

    lax.fori_loop(0, rank, step, 0)


def factor_panels(*panels):
    return pl.pallas_call(
        panel_kernel,
        out_shape=[jax.ShapeDtypeStruct(p.shape, p.dtype) for p in panels],
        in_specs=[pl.BlockSpec(memory_space=pltpu.VMEM)] * len(panels),
        out_specs=[pl.BlockSpec(memory_space=pltpu.VMEM)] * len(panels),
    )(*panels)


def group_kernel(kind, cycle, send_ref, o_ref, recv, send_sem, recv_sem):
    g = lax.axis_index("gx")
    a = lax.axis_index("af")
    size = send_ref.shape[0]
    if kind == "af":
        me = a

        def device(j):
            return (g, j)
    else:
        me = g // cycle

        def device(j):
            return (j * cycle + g % cycle, a)

    members = [(me + d) % size for d in range(1, size)]
    barrier = pltpu.get_barrier_semaphore()
    for j in members:
        pl.semaphore_signal(barrier, inc=1, device_id=device(j), device_id_type=MESH)
    pl.semaphore_wait(barrier, len(members))

    copies = []
    for n, j in enumerate(members):
        copy = pltpu.make_async_remote_copy(
            src_ref=send_ref.at[j],
            dst_ref=recv.at[n],
            send_sem=send_sem.at[n],
            recv_sem=recv_sem.at[n],
            device_id=device(j),
            device_id_type=MESH,
        )
        copy.start()
        copies.append(copy)
    for copy in copies:
        copy.wait()
    total = send_ref[me]
    for n in range(len(members)):
        total = total + recv[n]
    o_ref[...] = total


def group_sum(pieces, kind, cycle, collective_id):
    size = pieces.shape[0]
    piece = pieces.shape[1:]
    return pl.pallas_call(
        functools.partial(group_kernel, kind, cycle),
        out_shape=jax.ShapeDtypeStruct(piece, pieces.dtype),
        in_specs=[pl.BlockSpec(memory_space=pltpu.VMEM)],
        out_specs=pl.BlockSpec(memory_space=pltpu.VMEM),
        scratch_shapes=[
            pltpu.VMEM((size - 1,) + piece, pieces.dtype),
            pltpu.SemaphoreType.DMA((size - 1,)),
            pltpu.SemaphoreType.DMA((size - 1,)),
        ],
        compiler_params=pltpu.CompilerParams(collective_id=collective_id, has_side_effects=True),
    )(pieces)


def body(
    scalar_field, plane_sketch, second_sketch, third_sketch, mixing, plane_targets, plane_signs
):
    planes, rows, cells = scalar_field.shape
    rank_cols = mixing.shape[2]
    gx_index = lax.axis_index("gx")
    af_index = lax.axis_index("af")
    gx_size = lax.axis_size("gx")
    af_size = lax.axis_size("af")

    along_second = jnp.einsum("pjl,lk->pjk", scalar_field, third_sketch, precision=precise)
    partial_second = jnp.einsum(
        "pjk,pk->jk", along_second, plane_sketch[:, 0, :], precision=precise
    )
    along_third = jnp.einsum("pjl,jk->plk", scalar_field, second_sketch, precision=precise)
    partial_third = jnp.einsum("plk,pk->lk", along_third, plane_sketch[:, 1, :], precision=precise)

    range_second_block = jnp.dot(partial_second, mixing[0], precision=precise)
    range_third = jnp.dot(partial_third, mixing[1], precision=precise)
    full_rows = rows * af_size
    range_second = lax.dynamic_update_slice_in_dim(
        jnp.zeros((full_rows, rank_cols), jnp.float32), range_second_block, af_index * rows, 0
    )
    both = allreduce_all(jnp.concatenate([range_second, range_third], axis=0))

    ranges = both.reshape(2, full_rows, rank_cols)
    grams = jnp.einsum("nji,njk->nik", ranges, ranges, precision=precise)
    own_second = lax.dynamic_slice_in_dim(ranges[0], af_index * rows, rows, 0)
    panel_third, panel_second = factor_panels(
        jnp.concatenate([grams[1], ranges[1].T], axis=1),
        jnp.concatenate([grams[0], own_second.T], axis=1),
    )
    factor_third_all = panel_third[:, rank_cols:].T
    basis_second = panel_second[:, rank_cols:].T

    out_second = full_rows // (gx_size * af_size)
    assert rows == gx_size * out_second
    factor_second = lax.dynamic_slice_in_dim(basis_second, gx_index * out_second, out_second, 0)
    factor_third = lax.dynamic_slice_in_dim(
        factor_third_all, (gx_index * af_size + af_index) * out_second, out_second, 0
    )
    left_side = jnp.einsum("jr,pjl->prl", basis_second, scalar_field, precision=precise)
    projected = jnp.einsum("prl,ls->prs", left_side, factor_third_all, precision=precise)
    cycle = BLOCK // planes
    groups = gx_size // cycle
    assert planes * gx_size == BLOCKS * BLOCK and groups == BLOCKS
    own_targets = lax.dynamic_slice_in_dim(plane_targets, gx_index * planes, planes, 0)
    own_signs = lax.dynamic_slice_in_dim(plane_signs, gx_index * planes, planes, 0)
    sign_values = (2 * own_signs - 1).astype(jnp.float32)
    block_ids = jnp.arange(groups, dtype=jnp.int32)
    weights = jnp.sum(
        jnp.where(own_targets[None, :, :] == block_ids[:, None, None], sign_values[None, :, :], 0.0),
        axis=2,
    )
    slab = rank_cols // af_size
    pieces = projected.reshape(planes, af_size, slab, rank_cols).transpose(1, 0, 2, 3)
    summed = group_sum(pieces, "af", cycle, 1)
    contributions = weights[:, :, None, None] * summed[None]
    core_sketch = group_sum(contributions, "gx", cycle, 2)
    return (factor_second, factor_third, core_sketch)


def solution(mesh):
    in_specs = (P("gx", "af", None), P("gx", None, None), P("af", None), P(), P(), P(), P())
    out_specs = (P(("af", "gx"), None), P(("gx", "af"), None), P("gx", "af", None))
    return jax.shard_map(body, mesh=mesh, in_specs=in_specs, out_specs=out_specs, check_vma=False)
```

```python
import functools

import jax
import jax.numpy as jnp
from jax import lax
from jax.experimental import pallas as pl
from jax.experimental.pallas import tpu as pltpu
from jax.sharding import PartitionSpec as P

MESH = pl.DeviceIdType.MESH

BLOCK = 16
BLOCKS = 8


precise = lax.Precision.HIGHEST


def partner_list(gx_size, af_size):
    preferred = [("gx", 1), ("gx", 2), ("gx", 16), ("af", 1), ("gx", 4), ("gx", 32), ("af", 2), ("gx", 8)]
    sizes = {"gx": gx_size, "af": af_size}
    steps = [(axis, bit) for axis, bit in preferred if bit < sizes[axis]]
    for axis in ("gx", "af"):
        bit = 1
        while bit < sizes[axis]:
            if (axis, bit) not in steps:
                steps.append((axis, bit))
            bit *= 2
    return steps


def allreduce_kernel(digits, x_ref, o_ref, acc, recv, exchange, gathered, send_sem, recv_sem):
    index = {"gx": lax.axis_index("gx"), "af": lax.axis_index("af")}

    def bits_of(digit):
        return [(index[axis] // bit) % 2 for axis, bit in digit]

    def member(digit):
        own = bits_of(digit)
        return own[0] + 2 * own[1]

    def device(digit, d):
        values = dict(index)
        for t, ((axis, bit), own) in enumerate(zip(digit, bits_of(digit))):
            flip = (d >> t) & 1
            values[axis] = values[axis] + bit * flip * (1 - 2 * own)
        return (values["gx"], values["af"])

    barrier = pltpu.get_barrier_semaphore()
    for digit in digits:
        for d in (1, 2, 3):
            pl.semaphore_signal(barrier, inc=1, device_id=device(digit, d), device_id_type=MESH)
    pl.semaphore_wait(barrier, 3 * len(digits))

    counter = [0]

    def start(device_id, source, target):
        n = counter[0]
        counter[0] += 1
        copy = pltpu.make_async_remote_copy(
            src_ref=source,
            dst_ref=target,
            send_sem=send_sem.at[n],
            recv_sem=recv_sem.at[n],
            device_id=device_id,
            device_id_type=MESH,
        )
        copy.start()
        return copy

    def flipped(me, d):
        low, high = me % 2, me // 2
        low = low + (d & 1) * (1 - 2 * low)
        high = high + ((d >> 1) & 1) * (1 - 2 * high)
        return low + 2 * high

    acc[...] = x_ref[...]
    offset, length, slot = 0, acc.shape[0], 0
    parents = []
    for digit in digits[:-1]:
        me = member(digit)
        quarter = length // 4
        copies = []
        for d in (1, 2, 3):
            give = pl.multiple_of(offset + flipped(me, d) * quarter, 8)
            target = recv.at[pl.ds(slot + (d - 1) * quarter, quarter)]
            copies.append(start(device(digit, d), acc.at[pl.ds(give, quarter)], target))
        for copy in copies:
            copy.wait()
        keep = pl.multiple_of(offset + me * quarter, 8)
        total = acc[pl.ds(keep, quarter), :]
        for d in (1, 2, 3):
            total = total + recv[pl.ds(slot + (d - 1) * quarter, quarter), :]
        acc[pl.ds(keep, quarter), :] = total
        parents.append((offset, length))
        offset, length, slot = keep, quarter, slot + 3 * quarter

    last = digits[-1]
    me = member(last)
    segment = acc.at[pl.ds(offset, length)]
    copies = [start(device(last, d), segment, exchange.at[me]) for d in (1, 2, 3)]
    exchange[me] = acc[pl.ds(offset, length), :]
    for copy in copies:
        copy.wait()
    gathered[pl.ds(offset, length), :] = ((exchange[0] + exchange[1]) + exchange[2]) + exchange[3]

    for digit, (parent_offset, parent_length) in zip(reversed(digits[:-1]), reversed(parents)):
        part = gathered.at[pl.ds(offset, length)]
        copies = [start(device(digit, d), part, part) for d in (1, 2, 3)]
        for copy in copies:
            copy.wait()
        offset, length = parent_offset, parent_length
    o_ref[...] = gathered[...]


def allreduce_all(x):
    steps = partner_list(lax.axis_size("gx"), lax.axis_size("af"))
    assert len(steps) % 2 == 0
    digits = [steps[t:t + 2] for t in range(0, len(steps), 2)]
    last_rows = x.shape[0] // 4 ** (len(digits) - 1)
    assert last_rows % 8 == 0
    copies = 3 * (2 * len(digits) - 1)
    return pl.pallas_call(
        functools.partial(allreduce_kernel, digits),
        out_shape=jax.ShapeDtypeStruct(x.shape, x.dtype),
        in_specs=[pl.BlockSpec(memory_space=pltpu.VMEM)],
        out_specs=pl.BlockSpec(memory_space=pltpu.VMEM),
        scratch_shapes=[
            pltpu.VMEM(x.shape, x.dtype),
            pltpu.VMEM(x.shape, x.dtype),
            pltpu.VMEM((4, last_rows) + x.shape[1:], x.dtype),
            pltpu.VMEM(x.shape, x.dtype),
            pltpu.SemaphoreType.DMA((copies,)),
            pltpu.SemaphoreType.DMA((copies,)),
        ],
        compiler_params=pltpu.CompilerParams(collective_id=0, has_side_effects=True),
    )(x)


def panel_kernel(*refs):
    count = len(refs) // 2
    inputs, outputs = refs[:count], refs[count:]
    for source, target in zip(inputs, outputs):
        target[...] = source[...]
    rank = outputs[0].shape[0]

    def step(first, j, carry):
        for ref in outputs:
            width = ref.shape[1]
            row = ref[pl.ds(j, 1), :]
            lanes = lax.broadcasted_iota(jnp.int32, (1, width), 1)
            pivot = jnp.sum(jnp.where(lanes == j, row, 0.0), axis=1, keepdims=True)
            root = jnp.sqrt(pivot)
            column = jnp.where(lanes < j, 0.0, row / root)
            count = rank - first
            block = ref[pl.ds(first, count), :]
            cols = lax.broadcasted_iota(jnp.int32, (count, rank), 1)
            upper = jnp.sum(jnp.where(cols == j, block[:, :rank], 0.0), axis=1, keepdims=True)
            below = lax.broadcasted_iota(jnp.int32, (count, 1), 0) + first > j
            scale = jnp.where(below, upper / root, 0.0)
            ref[pl.ds(first, count), :] = block - scale * column
            ref[pl.ds(j, 1), :] = column
        return carry

    span = 16
    for first in range(0, rank, span):
        lax.fori_loop(first, first + span, functools.partial(step, first), 0)


def factor_panels(*panels):
    return pl.pallas_call(
        panel_kernel,
        out_shape=[jax.ShapeDtypeStruct(p.shape, p.dtype) for p in panels],
        in_specs=[pl.BlockSpec(memory_space=pltpu.VMEM)] * len(panels),
        out_specs=[pl.BlockSpec(memory_space=pltpu.VMEM)] * len(panels),
    )(*panels)


def group_kernel(kind, cycle, send_ref, o_ref, recv, send_sem, recv_sem):
    g = lax.axis_index("gx")
    a = lax.axis_index("af")
    size = send_ref.shape[0]
    if kind == "af":
        me = a

        def device(j):
            return (g, j)
    else:
        me = g // cycle

        def device(j):
            return (j * cycle + g % cycle, a)

    members = [(me + d) % size for d in range(1, size)]
    barrier = pltpu.get_barrier_semaphore()
    for j in members:
        pl.semaphore_signal(barrier, inc=1, device_id=device(j), device_id_type=MESH)
    pl.semaphore_wait(barrier, len(members))

    copies = []
    for n, j in enumerate(members):
        copy = pltpu.make_async_remote_copy(
            src_ref=send_ref.at[j],
            dst_ref=recv.at[n],
            send_sem=send_sem.at[n],
            recv_sem=recv_sem.at[n],
            device_id=device(j),
            device_id_type=MESH,
        )
        copy.start()
        copies.append(copy)
    for copy in copies:
        copy.wait()
    total = send_ref[me]
    for n in range(len(members)):
        total = total + recv[n]
    o_ref[...] = total


def group_sum(pieces, kind, cycle, collective_id):
    size = pieces.shape[0]
    piece = pieces.shape[1:]
    return pl.pallas_call(
        functools.partial(group_kernel, kind, cycle),
        out_shape=jax.ShapeDtypeStruct(piece, pieces.dtype),
        in_specs=[pl.BlockSpec(memory_space=pltpu.VMEM)],
        out_specs=pl.BlockSpec(memory_space=pltpu.VMEM),
        scratch_shapes=[
            pltpu.VMEM((size - 1,) + piece, pieces.dtype),
            pltpu.SemaphoreType.DMA((size - 1,)),
            pltpu.SemaphoreType.DMA((size - 1,)),
        ],
        compiler_params=pltpu.CompilerParams(collective_id=collective_id, has_side_effects=True),
    )(pieces)


def body(
    scalar_field, plane_sketch, second_sketch, third_sketch, mixing, plane_targets, plane_signs
):
    planes, rows, cells = scalar_field.shape
    rank_cols = mixing.shape[2]
    gx_index = lax.axis_index("gx")
    af_index = lax.axis_index("af")
    gx_size = lax.axis_size("gx")
    af_size = lax.axis_size("af")

    along_second = jnp.einsum("pjl,lk->pjk", scalar_field, third_sketch, precision=precise)
    partial_second = jnp.einsum(
        "pjk,pk->jk", along_second, plane_sketch[:, 0, :], precision=precise
    )
    along_third = jnp.einsum("pjl,jk->plk", scalar_field, second_sketch, precision=precise)
    partial_third = jnp.einsum("plk,pk->lk", along_third, plane_sketch[:, 1, :], precision=precise)

    range_second_block = jnp.dot(partial_second, mixing[0], precision=precise)
    range_third = jnp.dot(partial_third, mixing[1], precision=precise)
    full_rows = rows * af_size
    range_second = lax.dynamic_update_slice_in_dim(
        jnp.zeros((full_rows, rank_cols), jnp.float32), range_second_block, af_index * rows, 0
    )
    both = allreduce_all(jnp.concatenate([range_second, range_third], axis=0))

    ranges = both.reshape(2, full_rows, rank_cols)
    grams = jnp.einsum("nji,njk->nik", ranges, ranges, precision=precise)
    own_second = lax.dynamic_slice_in_dim(ranges[0], af_index * rows, rows, 0)
    panel_third, panel_second = factor_panels(
        jnp.concatenate([grams[1], ranges[1].T], axis=1),
        jnp.concatenate([grams[0], own_second.T], axis=1),
    )
    factor_third_all = panel_third[:, rank_cols:].T
    basis_second = panel_second[:, rank_cols:].T

    out_second = full_rows // (gx_size * af_size)
    assert rows == gx_size * out_second
    factor_second = lax.dynamic_slice_in_dim(basis_second, gx_index * out_second, out_second, 0)
    factor_third = lax.dynamic_slice_in_dim(
        factor_third_all, (gx_index * af_size + af_index) * out_second, out_second, 0
    )
    left_side = jnp.einsum("jr,pjl->prl", basis_second, scalar_field, precision=precise)
    projected = jnp.einsum("prl,ls->prs", left_side, factor_third_all, precision=precise)
    cycle = BLOCK // planes
    groups = gx_size // cycle
    assert planes * gx_size == BLOCKS * BLOCK and groups == BLOCKS
    own_targets = lax.dynamic_slice_in_dim(plane_targets, gx_index * planes, planes, 0)
    own_signs = lax.dynamic_slice_in_dim(plane_signs, gx_index * planes, planes, 0)
    sign_values = (2 * own_signs - 1).astype(jnp.float32)
    block_ids = jnp.arange(groups, dtype=jnp.int32)
    weights = jnp.sum(
        jnp.where(own_targets[None, :, :] == block_ids[:, None, None], sign_values[None, :, :], 0.0),
        axis=2,
    )
    slab = rank_cols // af_size
    pieces = projected.reshape(planes, af_size, slab, rank_cols).transpose(1, 0, 2, 3)
    summed = group_sum(pieces, "af", cycle, 1)
    contributions = weights[:, :, None, None] * summed[None]
    core_sketch = group_sum(contributions, "gx", cycle, 2)
    return (factor_second, factor_third, core_sketch)


def solution(mesh):
    in_specs = (P("gx", "af", None), P("gx", None, None), P("af", None), P(), P(), P(), P())
    out_specs = (P(("af", "gx"), None), P(("gx", "af"), None), P("gx", "af", None))
    return jax.shard_map(body, mesh=mesh, in_specs=in_specs, out_specs=out_specs, check_vma=False)
```

```python
import functools

import jax
import jax.numpy as jnp
from jax import lax
from jax.experimental import pallas as pl
from jax.experimental.pallas import tpu as pltpu
from jax.sharding import PartitionSpec as P

MESH = pl.DeviceIdType.MESH

BLOCK = 16
BLOCKS = 8


precise = lax.Precision.HIGHEST


def partner_list(gx_size, af_size):
    preferred = [("gx", 1), ("gx", 2), ("gx", 16), ("af", 1), ("gx", 4), ("gx", 32), ("af", 2), ("gx", 8)]
    sizes = {"gx": gx_size, "af": af_size}
    steps = [(axis, bit) for axis, bit in preferred if bit < sizes[axis]]
    for axis in ("gx", "af"):
        bit = 1
        while bit < sizes[axis]:
            if (axis, bit) not in steps:
                steps.append((axis, bit))
            bit *= 2
    return steps


def allreduce_kernel(digits, x_ref, o_ref, acc, recv, exchange, gathered, send_sem, recv_sem):
    index = {"gx": lax.axis_index("gx"), "af": lax.axis_index("af")}

    def bits_of(digit):
        return [(index[axis] // bit) % 2 for axis, bit in digit]

    def member(digit):
        own = bits_of(digit)
        return own[0] + 2 * own[1]

    def device(digit, d):
        values = dict(index)
        for t, ((axis, bit), own) in enumerate(zip(digit, bits_of(digit))):
            flip = (d >> t) & 1
            values[axis] = values[axis] + bit * flip * (1 - 2 * own)
        return (values["gx"], values["af"])

    barrier = pltpu.get_barrier_semaphore()
    for digit in digits:
        for d in (1, 2, 3):
            pl.semaphore_signal(barrier, inc=1, device_id=device(digit, d), device_id_type=MESH)
    pl.semaphore_wait(barrier, 3 * len(digits))

    counter = [0]

    def start(device_id, source, target):
        n = counter[0]
        counter[0] += 1
        copy = pltpu.make_async_remote_copy(
            src_ref=source,
            dst_ref=target,
            send_sem=send_sem.at[n],
            recv_sem=recv_sem.at[n],
            device_id=device_id,
            device_id_type=MESH,
        )
        copy.start()
        return copy

    def flipped(me, d):
        low, high = me % 2, me // 2
        low = low + (d & 1) * (1 - 2 * low)
        high = high + ((d >> 1) & 1) * (1 - 2 * high)
        return low + 2 * high

    acc[...] = x_ref[...]
    offset, length, slot = 0, acc.shape[0], 0
    parents = []
    for digit in digits[:-1]:
        me = member(digit)
        quarter = length // 4
        copies = []
        for d in (1, 2, 3):
            give = pl.multiple_of(offset + flipped(me, d) * quarter, 8)
            target = recv.at[pl.ds(slot + (d - 1) * quarter, quarter)]
            copies.append(start(device(digit, d), acc.at[pl.ds(give, quarter)], target))
        for copy in copies:
            copy.wait()
        keep = pl.multiple_of(offset + me * quarter, 8)
        total = acc[pl.ds(keep, quarter), :]
        for d in (1, 2, 3):
            total = total + recv[pl.ds(slot + (d - 1) * quarter, quarter), :]
        acc[pl.ds(keep, quarter), :] = total
        parents.append((offset, length))
        offset, length, slot = keep, quarter, slot + 3 * quarter

    last = digits[-1]
    me = member(last)
    segment = acc.at[pl.ds(offset, length)]
    copies = [start(device(last, d), segment, exchange.at[me]) for d in (1, 2, 3)]
    exchange[me] = acc[pl.ds(offset, length), :]
    for copy in copies:
        copy.wait()
    gathered[pl.ds(offset, length), :] = ((exchange[0] + exchange[1]) + exchange[2]) + exchange[3]

    for digit, (parent_offset, parent_length) in zip(reversed(digits[:-1]), reversed(parents)):
        part = gathered.at[pl.ds(offset, length)]
        copies = [start(device(digit, d), part, part) for d in (1, 2, 3)]
        for copy in copies:
            copy.wait()
        offset, length = parent_offset, parent_length
    o_ref[...] = gathered[...]


def allreduce_all(x):
    steps = partner_list(lax.axis_size("gx"), lax.axis_size("af"))
    assert len(steps) % 2 == 0
    digits = [steps[t:t + 2] for t in range(0, len(steps), 2)]
    last_rows = x.shape[0] // 4 ** (len(digits) - 1)
    assert last_rows % 8 == 0
    copies = 3 * (2 * len(digits) - 1)
    return pl.pallas_call(
        functools.partial(allreduce_kernel, digits),
        out_shape=jax.ShapeDtypeStruct(x.shape, x.dtype),
        in_specs=[pl.BlockSpec(memory_space=pltpu.VMEM)],
        out_specs=pl.BlockSpec(memory_space=pltpu.VMEM),
        scratch_shapes=[
            pltpu.VMEM(x.shape, x.dtype),
            pltpu.VMEM(x.shape, x.dtype),
            pltpu.VMEM((4, last_rows) + x.shape[1:], x.dtype),
            pltpu.VMEM(x.shape, x.dtype),
            pltpu.SemaphoreType.DMA((copies,)),
            pltpu.SemaphoreType.DMA((copies,)),
        ],
        compiler_params=pltpu.CompilerParams(collective_id=0, has_side_effects=True),
    )(x)


def panel_kernel(*refs):
    count = len(refs) // 2
    inputs, outputs = refs[:count], refs[count:]
    for source, target in zip(inputs, outputs):
        target[...] = source[...]
    rank = outputs[0].shape[0]

    def step(first, j, carry):
        for ref in outputs:
            width = ref.shape[1]
            row = ref[pl.ds(j, 1), :]
            lanes = lax.broadcasted_iota(jnp.int32, (1, width), 1)
            pivot = jnp.sum(jnp.where(lanes == j, row, 0.0), axis=1, keepdims=True)
            root = jnp.sqrt(pivot)
            column = jnp.where(lanes < j, 0.0, row / root)
            count = rank - first
            block = ref[pl.ds(first, count), :]
            cols = lax.broadcasted_iota(jnp.int32, (count, rank), 1)
            upper = jnp.sum(jnp.where(cols == j, block[:, :rank], 0.0), axis=1, keepdims=True)
            below = lax.broadcasted_iota(jnp.int32, (count, 1), 0) + first > j
            scale = jnp.where(below, upper / root, 0.0)
            ref[pl.ds(first, count), :] = block - scale * column
            ref[pl.ds(j, 1), :] = column
        return carry

    span = 16
    for first in range(0, rank, span):
        lax.fori_loop(first, first + span, functools.partial(step, first), 0)


def factor_panels(*panels):
    return pl.pallas_call(
        panel_kernel,
        out_shape=[jax.ShapeDtypeStruct(p.shape, p.dtype) for p in panels],
        in_specs=[pl.BlockSpec(memory_space=pltpu.VMEM)] * len(panels),
        out_specs=[pl.BlockSpec(memory_space=pltpu.VMEM)] * len(panels),
    )(*panels)


def core_kernel(cycle, pieces_ref, weights_ref, o_ref, first, staged, second, send_sem, recv_sem):
    g = lax.axis_index("gx")
    a = lax.axis_index("af")
    quarters, blocks = pieces_ref.shape[0], weights_ref.shape[0]
    k = g // cycle
    c = g % cycle
    peers = [(a + d) % quarters for d in range(1, quarters)]
    owners = [(k + d) % blocks for d in range(1, blocks)]

    def peer(j):
        return (g, j)

    def owner(j):
        return (j * cycle + c, a)

    barrier = pltpu.get_barrier_semaphore()
    for device in [peer(j) for j in peers] + [owner(j) for j in owners]:
        pl.semaphore_signal(barrier, inc=1, device_id=device, device_id_type=MESH)
    pl.semaphore_wait(barrier, len(peers) + len(owners))

    def start(n, source, target, device):
        copy = pltpu.make_async_remote_copy(
            src_ref=source,
            dst_ref=target,
            send_sem=send_sem.at[n],
            recv_sem=recv_sem.at[n],
            device_id=device,
            device_id_type=MESH,
        )
        copy.start()
        return copy

    copies = [start(n, pieces_ref.at[j], first.at[n], peer(j)) for n, j in enumerate(peers)]
    for copy in copies:
        copy.wait()
    total = pieces_ref[a]
    for n in range(len(peers)):
        total = total + first[n]
    for j in range(blocks):
        staged[j] = weights_ref[j] * total
    base = len(peers)
    copies = [
        start(base + n, staged.at[j], second.at[n], owner(j)) for n, j in enumerate(owners)
    ]
    for copy in copies:
        copy.wait()
    result = staged[k]
    for n in range(len(owners)):
        result = result + second[n]
    o_ref[...] = result


def core_exchange(pieces, weights, cycle):
    quarters, blocks = pieces.shape[0], weights.shape[0]
    piece = pieces.shape[1:]
    return pl.pallas_call(
        functools.partial(core_kernel, cycle),
        out_shape=jax.ShapeDtypeStruct(piece, pieces.dtype),
        in_specs=[pl.BlockSpec(memory_space=pltpu.VMEM)] * 2,
        out_specs=pl.BlockSpec(memory_space=pltpu.VMEM),
        scratch_shapes=[
            pltpu.VMEM((quarters - 1,) + piece, pieces.dtype),
            pltpu.VMEM((blocks,) + piece, pieces.dtype),
            pltpu.VMEM((blocks - 1,) + piece, pieces.dtype),
            pltpu.SemaphoreType.DMA((quarters + blocks - 2,)),
            pltpu.SemaphoreType.DMA((quarters + blocks - 2,)),
        ],
        compiler_params=pltpu.CompilerParams(collective_id=1, has_side_effects=True),
    )(pieces, weights)


def body(
    scalar_field, plane_sketch, second_sketch, third_sketch, mixing, plane_targets, plane_signs
):
    planes, rows, cells = scalar_field.shape
    rank_cols = mixing.shape[2]
    gx_index = lax.axis_index("gx")
    af_index = lax.axis_index("af")
    gx_size = lax.axis_size("gx")
    af_size = lax.axis_size("af")

    along_second = jnp.einsum("pjl,lk->pjk", scalar_field, third_sketch, precision=precise)
    partial_second = jnp.einsum(
        "pjk,pk->jk", along_second, plane_sketch[:, 0, :], precision=precise
    )
    along_third = jnp.einsum("pjl,jk->plk", scalar_field, second_sketch, precision=precise)
    partial_third = jnp.einsum("plk,pk->lk", along_third, plane_sketch[:, 1, :], precision=precise)

    range_second_block = jnp.dot(partial_second, mixing[0], precision=precise)
    range_third = jnp.dot(partial_third, mixing[1], precision=precise)
    full_rows = rows * af_size
    range_second = lax.dynamic_update_slice_in_dim(
        jnp.zeros((full_rows, rank_cols), jnp.float32), range_second_block, af_index * rows, 0
    )
    both = allreduce_all(jnp.concatenate([range_second, range_third], axis=0))

    ranges = both.reshape(2, full_rows, rank_cols)
    grams = jnp.einsum("nji,njk->nik", ranges, ranges, precision=precise)
    own_second = lax.dynamic_slice_in_dim(ranges[0], af_index * rows, rows, 0)
    panel_third, panel_second = factor_panels(
        jnp.concatenate([grams[1], ranges[1].T], axis=1),
        jnp.concatenate([grams[0], own_second.T], axis=1),
    )
    factor_third_all = panel_third[:, rank_cols:].T
    basis_second = panel_second[:, rank_cols:].T

    out_second = full_rows // (gx_size * af_size)
    assert rows == gx_size * out_second
    factor_second = lax.dynamic_slice_in_dim(basis_second, gx_index * out_second, out_second, 0)
    factor_third = lax.dynamic_slice_in_dim(
        factor_third_all, (gx_index * af_size + af_index) * out_second, out_second, 0
    )
    left_side = jnp.einsum("jr,pjl->prl", basis_second, scalar_field, precision=precise)
    projected = jnp.einsum("prl,ls->prs", left_side, factor_third_all, precision=precise)
    cycle = BLOCK // planes
    groups = gx_size // cycle
    assert planes * gx_size == BLOCKS * BLOCK and groups == BLOCKS
    own_targets = lax.dynamic_slice_in_dim(plane_targets, gx_index * planes, planes, 0)
    own_signs = lax.dynamic_slice_in_dim(plane_signs, gx_index * planes, planes, 0)
    sign_values = (2 * own_signs - 1).astype(jnp.float32)
    block_ids = jnp.arange(groups, dtype=jnp.int32)
    weights = jnp.sum(
        jnp.where(own_targets[None, :, :] == block_ids[:, None, None], sign_values[None, :, :], 0.0),
        axis=2,
    )
    slab = rank_cols // af_size
    pieces = projected.reshape(planes, af_size, slab, rank_cols).transpose(1, 0, 2, 3)
    lane_weights = jnp.broadcast_to(weights[:, :, None, None], (groups, planes, 1, rank_cols))
    core_sketch = core_exchange(pieces, lane_weights, cycle)
    return (factor_second, factor_third, core_sketch)


def solution(mesh):
    in_specs = (P("gx", "af", None), P("gx", None, None), P("af", None), P(), P(), P(), P())
    out_specs = (P(("af", "gx"), None), P(("gx", "af"), None), P("gx", "af", None))
    return jax.shard_map(body, mesh=mesh, in_specs=in_specs, out_specs=out_specs, check_vma=False)
```

```python
import functools

import jax
import jax.numpy as jnp
from jax import lax
from jax.experimental import pallas as pl
from jax.experimental.pallas import tpu as pltpu
from jax.sharding import PartitionSpec as P

MESH = pl.DeviceIdType.MESH

BLOCK = 16
BLOCKS = 8


precise = lax.Precision.HIGHEST


def partner_list(gx_size, af_size):
    preferred = [("gx", 1), ("gx", 2), ("gx", 16), ("af", 1), ("gx", 4), ("gx", 32), ("af", 2), ("gx", 8)]
    sizes = {"gx": gx_size, "af": af_size}
    steps = [(axis, bit) for axis, bit in preferred if bit < sizes[axis]]
    for axis in ("gx", "af"):
        bit = 1
        while bit < sizes[axis]:
            if (axis, bit) not in steps:
                steps.append((axis, bit))
            bit *= 2
    return steps


def allreduce_kernel(digits, x_ref, o_ref, acc, recv, exchange, gathered, send_sem, recv_sem):
    index = {"gx": lax.axis_index("gx"), "af": lax.axis_index("af")}

    def bits_of(digit):
        return [(index[axis] // bit) % 2 for axis, bit in digit]

    def member(digit):
        return sum(own * 2**t for t, own in enumerate(bits_of(digit)))

    def flipped(digit, d):
        return sum(
            (own + ((d >> t) & 1) * (1 - 2 * own)) * 2**t for t, own in enumerate(bits_of(digit))
        )

    def device(digit, d):
        values = dict(index)
        for t, ((axis, bit), own) in enumerate(zip(digit, bits_of(digit))):
            values[axis] = values[axis] + bit * ((d >> t) & 1) * (1 - 2 * own)
        return (values["gx"], values["af"])

    def others(digit):
        return range(1, 2 ** len(digit))

    barrier = pltpu.get_barrier_semaphore()
    for digit in digits:
        for d in others(digit):
            pl.semaphore_signal(barrier, inc=1, device_id=device(digit, d), device_id_type=MESH)
    pl.semaphore_wait(barrier, sum(len(others(digit)) for digit in digits))

    counter = [0]

    def start(device_id, source, target):
        n = counter[0]
        counter[0] += 1
        copy = pltpu.make_async_remote_copy(
            src_ref=source,
            dst_ref=target,
            send_sem=send_sem.at[n],
            recv_sem=recv_sem.at[n],
            device_id=device_id,
            device_id_type=MESH,
        )
        copy.start()
        return copy

    acc[...] = x_ref[...]
    offset, length, slot = 0, acc.shape[0], 0
    parents = []
    for digit in digits[:-1]:
        me = member(digit)
        part = length // 2 ** len(digit)
        copies = []
        for d in others(digit):
            give = pl.multiple_of(offset + flipped(digit, d) * part, 8)
            target = recv.at[pl.ds(slot + (d - 1) * part, part)]
            copies.append(start(device(digit, d), acc.at[pl.ds(give, part)], target))
        for copy in copies:
            copy.wait()
        keep = pl.multiple_of(offset + me * part, 8)
        total = acc[pl.ds(keep, part), :]
        for d in others(digit):
            total = total + recv[pl.ds(slot + (d - 1) * part, part), :]
        acc[pl.ds(keep, part), :] = total
        parents.append((offset, length))
        offset, length, slot = keep, part, slot + len(others(digit)) * part

    last = digits[-1]
    me = member(last)
    segment = acc.at[pl.ds(offset, length)]
    copies = [start(device(last, d), segment, exchange.at[me]) for d in others(last)]
    exchange[me] = acc[pl.ds(offset, length), :]
    for copy in copies:
        copy.wait()
    total = exchange[0]
    for q in range(1, 2 ** len(last)):
        total = total + exchange[q]
    gathered[pl.ds(offset, length), :] = total

    for digit, (parent_offset, parent_length) in zip(reversed(digits[:-1]), reversed(parents)):
        part = gathered.at[pl.ds(offset, length)]
        copies = [start(device(digit, d), part, part) for d in others(digit)]
        for copy in copies:
            copy.wait()
        offset, length = parent_offset, parent_length
    o_ref[...] = gathered[...]


def allreduce_all(x):
    steps = partner_list(lax.axis_size("gx"), lax.axis_size("af"))
    digits = [steps[t:t + 3] for t in range(0, len(steps), 3)]
    last_rows = x.shape[0]
    for digit in digits[:-1]:
        last_rows //= 2 ** len(digit)
    assert last_rows % 8 == 0
    copies = sum(2 * (2 ** len(digit) - 1) for digit in digits[:-1]) + 2 ** len(digits[-1]) - 1
    return pl.pallas_call(
        functools.partial(allreduce_kernel, digits),
        out_shape=jax.ShapeDtypeStruct(x.shape, x.dtype),
        in_specs=[pl.BlockSpec(memory_space=pltpu.VMEM)],
        out_specs=pl.BlockSpec(memory_space=pltpu.VMEM),
        scratch_shapes=[
            pltpu.VMEM(x.shape, x.dtype),
            pltpu.VMEM(x.shape, x.dtype),
            pltpu.VMEM((2 ** len(digits[-1]), last_rows) + x.shape[1:], x.dtype),
            pltpu.VMEM(x.shape, x.dtype),
            pltpu.SemaphoreType.DMA((copies,)),
            pltpu.SemaphoreType.DMA((copies,)),
        ],
        compiler_params=pltpu.CompilerParams(collective_id=0, has_side_effects=True),
    )(x)


def panel_kernel(*refs):
    count = len(refs) // 2
    inputs, outputs = refs[:count], refs[count:]
    for source, target in zip(inputs, outputs):
        target[...] = source[...]
    rank = outputs[0].shape[0]

    def step(first, j, carry):
        for ref in outputs:
            width = ref.shape[1]
            row = ref[pl.ds(j, 1), :]
            lanes = lax.broadcasted_iota(jnp.int32, (1, width), 1)
            pivot = jnp.sum(jnp.where(lanes == j, row, 0.0), axis=1, keepdims=True)
            root = jnp.sqrt(pivot)
            column = jnp.where(lanes < j, 0.0, row / root)
            count = rank - first
            block = ref[pl.ds(first, count), :]
            cols = lax.broadcasted_iota(jnp.int32, (count, rank), 1)
            upper = jnp.sum(jnp.where(cols == j, block[:, :rank], 0.0), axis=1, keepdims=True)
            below = lax.broadcasted_iota(jnp.int32, (count, 1), 0) + first > j
            scale = jnp.where(below, upper / root, 0.0)
            ref[pl.ds(first, count), :] = block - scale * column
            ref[pl.ds(j, 1), :] = column
        return carry

    span = 16
    for first in range(0, rank, span):
        lax.fori_loop(first, first + span, functools.partial(step, first), 0)


def factor_panels(*panels):
    return pl.pallas_call(
        panel_kernel,
        out_shape=[jax.ShapeDtypeStruct(p.shape, p.dtype) for p in panels],
        in_specs=[pl.BlockSpec(memory_space=pltpu.VMEM)] * len(panels),
        out_specs=[pl.BlockSpec(memory_space=pltpu.VMEM)] * len(panels),
    )(*panels)


def core_kernel(cycle, pieces_ref, weights_ref, o_ref, first, staged, second, send_sem, recv_sem):
    g = lax.axis_index("gx")
    a = lax.axis_index("af")
    quarters, blocks = pieces_ref.shape[0], weights_ref.shape[0]
    k = g // cycle
    c = g % cycle
    peers = [(a + d) % quarters for d in range(1, quarters)]
    owners = [(k + d) % blocks for d in range(1, blocks)]

    def peer(j):
        return (g, j)

    def owner(j):
        return (j * cycle + c, a)

    barrier = pltpu.get_barrier_semaphore()
    for device in [peer(j) for j in peers] + [owner(j) for j in owners]:
        pl.semaphore_signal(barrier, inc=1, device_id=device, device_id_type=MESH)
    pl.semaphore_wait(barrier, len(peers) + len(owners))

    def start(n, source, target, device):
        copy = pltpu.make_async_remote_copy(
            src_ref=source,
            dst_ref=target,
            send_sem=send_sem.at[n],
            recv_sem=recv_sem.at[n],
            device_id=device,
            device_id_type=MESH,
        )
        copy.start()
        return copy

    copies = [start(n, pieces_ref.at[j], first.at[n], peer(j)) for n, j in enumerate(peers)]
    for copy in copies:
        copy.wait()
    total = pieces_ref[a]
    for n in range(len(peers)):
        total = total + first[n]
    for j in range(blocks):
        staged[j] = weights_ref[j] * total
    base = len(peers)
    copies = [
        start(base + n, staged.at[j], second.at[n], owner(j)) for n, j in enumerate(owners)
    ]
    for copy in copies:
        copy.wait()
    result = staged[k]
    for n in range(len(owners)):
        result = result + second[n]
    o_ref[...] = result


def core_exchange(pieces, weights, cycle):
    quarters, blocks = pieces.shape[0], weights.shape[0]
    piece = pieces.shape[1:]
    return pl.pallas_call(
        functools.partial(core_kernel, cycle),
        out_shape=jax.ShapeDtypeStruct(piece, pieces.dtype),
        in_specs=[pl.BlockSpec(memory_space=pltpu.VMEM)] * 2,
        out_specs=pl.BlockSpec(memory_space=pltpu.VMEM),
        scratch_shapes=[
            pltpu.VMEM((quarters - 1,) + piece, pieces.dtype),
            pltpu.VMEM((blocks,) + piece, pieces.dtype),
            pltpu.VMEM((blocks - 1,) + piece, pieces.dtype),
            pltpu.SemaphoreType.DMA((quarters + blocks - 2,)),
            pltpu.SemaphoreType.DMA((quarters + blocks - 2,)),
        ],
        compiler_params=pltpu.CompilerParams(collective_id=1, has_side_effects=True),
    )(pieces, weights)


def body(
    scalar_field, plane_sketch, second_sketch, third_sketch, mixing, plane_targets, plane_signs
):
    planes, rows, cells = scalar_field.shape
    rank_cols = mixing.shape[2]
    gx_index = lax.axis_index("gx")
    af_index = lax.axis_index("af")
    gx_size = lax.axis_size("gx")
    af_size = lax.axis_size("af")

    along_second = jnp.einsum("pjl,lk->pjk", scalar_field, third_sketch, precision=precise)
    partial_second = jnp.einsum(
        "pjk,pk->jk", along_second, plane_sketch[:, 0, :], precision=precise
    )
    along_third = jnp.einsum("pjl,jk->plk", scalar_field, second_sketch, precision=precise)
    partial_third = jnp.einsum("plk,pk->lk", along_third, plane_sketch[:, 1, :], precision=precise)

    range_second_block = jnp.dot(partial_second, mixing[0], precision=precise)
    range_third = jnp.dot(partial_third, mixing[1], precision=precise)
    full_rows = rows * af_size
    range_second = lax.dynamic_update_slice_in_dim(
        jnp.zeros((full_rows, rank_cols), jnp.float32), range_second_block, af_index * rows, 0
    )
    both = allreduce_all(jnp.concatenate([range_second, range_third], axis=0))

    ranges = both.reshape(2, full_rows, rank_cols)
    grams = jnp.einsum("nji,njk->nik", ranges, ranges, precision=precise)
    own_second = lax.dynamic_slice_in_dim(ranges[0], af_index * rows, rows, 0)
    panel_third, panel_second = factor_panels(
        jnp.concatenate([grams[1], ranges[1].T], axis=1),
        jnp.concatenate([grams[0], own_second.T], axis=1),
    )
    factor_third_all = panel_third[:, rank_cols:].T
    basis_second = panel_second[:, rank_cols:].T

    out_second = full_rows // (gx_size * af_size)
    assert rows == gx_size * out_second
    factor_second = lax.dynamic_slice_in_dim(basis_second, gx_index * out_second, out_second, 0)
    factor_third = lax.dynamic_slice_in_dim(
        factor_third_all, (gx_index * af_size + af_index) * out_second, out_second, 0
    )
    left_side = jnp.einsum("jr,pjl->prl", basis_second, scalar_field, precision=precise)
    projected = jnp.einsum("prl,ls->prs", left_side, factor_third_all, precision=precise)
    cycle = BLOCK // planes
    groups = gx_size // cycle
    assert planes * gx_size == BLOCKS * BLOCK and groups == BLOCKS
    own_targets = lax.dynamic_slice_in_dim(plane_targets, gx_index * planes, planes, 0)
    own_signs = lax.dynamic_slice_in_dim(plane_signs, gx_index * planes, planes, 0)
    sign_values = (2 * own_signs - 1).astype(jnp.float32)
    block_ids = jnp.arange(groups, dtype=jnp.int32)
    weights = jnp.sum(
        jnp.where(own_targets[None, :, :] == block_ids[:, None, None], sign_values[None, :, :], 0.0),
        axis=2,
    )
    slab = rank_cols // af_size
    pieces = projected.reshape(planes, af_size, slab, rank_cols).transpose(1, 0, 2, 3)
    lane_weights = jnp.broadcast_to(weights[:, :, None, None], (groups, planes, 1, rank_cols))
    core_sketch = core_exchange(pieces, lane_weights, cycle)
    return (factor_second, factor_third, core_sketch)


def solution(mesh):
    in_specs = (P("gx", "af", None), P("gx", None, None), P("af", None), P(), P(), P(), P())
    out_specs = (P(("af", "gx"), None), P(("gx", "af"), None), P("gx", "af", None))
    return jax.shard_map(body, mesh=mesh, in_specs=in_specs, out_specs=out_specs, check_vma=False)
```

```python
import functools

import jax
import jax.numpy as jnp
from jax import lax
from jax.experimental import pallas as pl
from jax.experimental.pallas import tpu as pltpu
from jax.sharding import PartitionSpec as P

MESH = pl.DeviceIdType.MESH

BLOCK = 16
BLOCKS = 8


precise = lax.Precision.HIGHEST


def partner_list(gx_size, af_size):
    preferred = [("gx", 1), ("gx", 2), ("gx", 16), ("af", 1), ("gx", 4), ("gx", 32), ("af", 2), ("gx", 8)]
    sizes = {"gx": gx_size, "af": af_size}
    steps = [(axis, bit) for axis, bit in preferred if bit < sizes[axis]]
    for axis in ("gx", "af"):
        bit = 1
        while bit < sizes[axis]:
            if (axis, bit) not in steps:
                steps.append((axis, bit))
            bit *= 2
    return steps


def allreduce_kernel(digits, x_ref, o_ref, acc, recv, exchange, gathered, send_sem, recv_sem):
    index = {"gx": lax.axis_index("gx"), "af": lax.axis_index("af")}

    def bits_of(digit):
        return [(index[axis] // bit) % 2 for axis, bit in digit]

    def member(digit):
        return sum(own * 2**t for t, own in enumerate(bits_of(digit)))

    def flipped(digit, d):
        return sum(
            (own + ((d >> t) & 1) * (1 - 2 * own)) * 2**t for t, own in enumerate(bits_of(digit))
        )

    def device(digit, d):
        values = dict(index)
        for t, ((axis, bit), own) in enumerate(zip(digit, bits_of(digit))):
            values[axis] = values[axis] + bit * ((d >> t) & 1) * (1 - 2 * own)
        return (values["gx"], values["af"])

    def others(digit):
        return range(1, 2 ** len(digit))

    barrier = pltpu.get_barrier_semaphore()
    for digit in digits:
        for d in others(digit):
            pl.semaphore_signal(barrier, inc=1, device_id=device(digit, d), device_id_type=MESH)
    pl.semaphore_wait(barrier, sum(len(others(digit)) for digit in digits))

    counter = [0]

    def start(device_id, source, target):
        n = counter[0]
        counter[0] += 1
        copy = pltpu.make_async_remote_copy(
            src_ref=source,
            dst_ref=target,
            send_sem=send_sem.at[n],
            recv_sem=recv_sem.at[n],
            device_id=device_id,
            device_id_type=MESH,
        )
        copy.start()
        return copy

    acc[...] = x_ref[...]
    offset, length, slot = 0, acc.shape[0], 0
    parents = []
    for digit in digits[:-1]:
        me = member(digit)
        part = length // 2 ** len(digit)
        copies = []
        for d in others(digit):
            give = pl.multiple_of(offset + flipped(digit, d) * part, 8)
            target = recv.at[pl.ds(slot + (d - 1) * part, part)]
            copies.append(start(device(digit, d), acc.at[pl.ds(give, part)], target))
        for copy in copies:
            copy.wait()
        keep = pl.multiple_of(offset + me * part, 8)
        total = acc[pl.ds(keep, part), :]
        for d in others(digit):
            total = total + recv[pl.ds(slot + (d - 1) * part, part), :]
        acc[pl.ds(keep, part), :] = total
        parents.append((offset, length))
        offset, length, slot = keep, part, slot + len(others(digit)) * part

    last = digits[-1]
    me = member(last)
    segment = acc.at[pl.ds(offset, length)]
    copies = [start(device(last, d), segment, exchange.at[me]) for d in others(last)]
    exchange[me] = acc[pl.ds(offset, length), :]
    for copy in copies:
        copy.wait()
    total = exchange[0]
    for q in range(1, 2 ** len(last)):
        total = total + exchange[q]
    gathered[pl.ds(offset, length), :] = total

    for digit, (parent_offset, parent_length) in zip(reversed(digits[:-1]), reversed(parents)):
        part = gathered.at[pl.ds(offset, length)]
        copies = [start(device(digit, d), part, part) for d in others(digit)]
        for copy in copies:
            copy.wait()
        offset, length = parent_offset, parent_length
    o_ref[...] = gathered[...]


def allreduce_all(x):
    steps = partner_list(lax.axis_size("gx"), lax.axis_size("af"))
    digits = [steps[t:t + 3] for t in range(0, len(steps), 3)]
    last_rows = x.shape[0]
    for digit in digits[:-1]:
        last_rows //= 2 ** len(digit)
    assert last_rows % 8 == 0
    copies = sum(2 * (2 ** len(digit) - 1) for digit in digits[:-1]) + 2 ** len(digits[-1]) - 1
    return pl.pallas_call(
        functools.partial(allreduce_kernel, digits),
        out_shape=jax.ShapeDtypeStruct(x.shape, x.dtype),
        in_specs=[pl.BlockSpec(memory_space=pltpu.VMEM)],
        out_specs=pl.BlockSpec(memory_space=pltpu.VMEM),
        scratch_shapes=[
            pltpu.VMEM(x.shape, x.dtype),
            pltpu.VMEM(x.shape, x.dtype),
            pltpu.VMEM((2 ** len(digits[-1]), last_rows) + x.shape[1:], x.dtype),
            pltpu.VMEM(x.shape, x.dtype),
            pltpu.SemaphoreType.DMA((copies,)),
            pltpu.SemaphoreType.DMA((copies,)),
        ],
        compiler_params=pltpu.CompilerParams(collective_id=0, has_side_effects=True),
    )(x)


def panel_kernel(*refs):
    count = len(refs) // 2
    inputs, outputs = refs[:count], refs[count:]
    for source, target in zip(inputs, outputs):
        target[...] = source[...]
    rank = outputs[0].shape[0]

    def step(first, j, carry):
        for ref in outputs:
            width = ref.shape[1]
            row = ref[pl.ds(j, 1), :]
            lanes = lax.broadcasted_iota(jnp.int32, (1, width), 1)
            square_lanes = lax.broadcasted_iota(jnp.int32, (1, rank), 1)
            pivot = jnp.sum(
                jnp.where(square_lanes == j, row[:, :rank], 0.0), axis=1, keepdims=True
            )
            inverse = 1.0 / jnp.sqrt(pivot)
            column = jnp.where(lanes < j, 0.0, row * inverse)
            count = rank - first
            block = ref[pl.ds(first, count), :]
            cols = lax.broadcasted_iota(jnp.int32, (count, rank), 1)
            upper = jnp.sum(jnp.where(cols == j, block[:, :rank], 0.0), axis=1, keepdims=True)
            below = lax.broadcasted_iota(jnp.int32, (count, 1), 0) + first > j
            scale = jnp.where(below, upper * inverse, 0.0)
            ref[pl.ds(first, count), :] = block - scale * column
            ref[pl.ds(j, 1), :] = column
        return carry

    span = 16
    for first in range(0, rank, span):
        lax.fori_loop(first, first + span, functools.partial(step, first), 0, unroll=2)


def factor_panels(*panels):
    return pl.pallas_call(
        panel_kernel,
        out_shape=[jax.ShapeDtypeStruct(p.shape, p.dtype) for p in panels],
        in_specs=[pl.BlockSpec(memory_space=pltpu.VMEM)] * len(panels),
        out_specs=[pl.BlockSpec(memory_space=pltpu.VMEM)] * len(panels),
    )(*panels)


def core_kernel(cycle, pieces_ref, weights_ref, o_ref, first, staged, second, send_sem, recv_sem):
    g = lax.axis_index("gx")
    a = lax.axis_index("af")
    quarters, blocks = pieces_ref.shape[0], weights_ref.shape[0]
    k = g // cycle
    c = g % cycle
    peers = [(a + d) % quarters for d in range(1, quarters)]
    owners = [(k + d) % blocks for d in range(1, blocks)]

    def peer(j):
        return (g, j)

    def owner(j):
        return (j * cycle + c, a)

    barrier = pltpu.get_barrier_semaphore()
    for device in [peer(j) for j in peers] + [owner(j) for j in owners]:
        pl.semaphore_signal(barrier, inc=1, device_id=device, device_id_type=MESH)
    pl.semaphore_wait(barrier, len(peers) + len(owners))

    def start(n, source, target, device):
        copy = pltpu.make_async_remote_copy(
            src_ref=source,
            dst_ref=target,
            send_sem=send_sem.at[n],
            recv_sem=recv_sem.at[n],
            device_id=device,
            device_id_type=MESH,
        )
        copy.start()
        return copy

    copies = [start(n, pieces_ref.at[j], first.at[n], peer(j)) for n, j in enumerate(peers)]
    for copy in copies:
        copy.wait()
    total = pieces_ref[a]
    for n in range(len(peers)):
        total = total + first[n]
    for j in range(blocks):
        staged[j] = weights_ref[j] * total
    base = len(peers)
    copies = [
        start(base + n, staged.at[j], second.at[n], owner(j)) for n, j in enumerate(owners)
    ]
    for copy in copies:
        copy.wait()
    result = staged[k]
    for n in range(len(owners)):
        result = result + second[n]
    o_ref[...] = result


def core_exchange(pieces, weights, cycle):
    quarters, blocks = pieces.shape[0], weights.shape[0]
    piece = pieces.shape[1:]
    return pl.pallas_call(
        functools.partial(core_kernel, cycle),
        out_shape=jax.ShapeDtypeStruct(piece, pieces.dtype),
        in_specs=[pl.BlockSpec(memory_space=pltpu.VMEM)] * 2,
        out_specs=pl.BlockSpec(memory_space=pltpu.VMEM),
        scratch_shapes=[
            pltpu.VMEM((quarters - 1,) + piece, pieces.dtype),
            pltpu.VMEM((blocks,) + piece, pieces.dtype),
            pltpu.VMEM((blocks - 1,) + piece, pieces.dtype),
            pltpu.SemaphoreType.DMA((quarters + blocks - 2,)),
            pltpu.SemaphoreType.DMA((quarters + blocks - 2,)),
        ],
        compiler_params=pltpu.CompilerParams(collective_id=1, has_side_effects=True),
    )(pieces, weights)


def body(
    scalar_field, plane_sketch, second_sketch, third_sketch, mixing, plane_targets, plane_signs
):
    planes, rows, cells = scalar_field.shape
    rank_cols = mixing.shape[2]
    gx_index = lax.axis_index("gx")
    af_index = lax.axis_index("af")
    gx_size = lax.axis_size("gx")
    af_size = lax.axis_size("af")

    along_second = jnp.einsum("pjl,lk->pjk", scalar_field, third_sketch, precision=precise)
    partial_second = jnp.einsum(
        "pjk,pk->jk", along_second, plane_sketch[:, 0, :], precision=precise
    )
    along_third = jnp.einsum("pjl,jk->plk", scalar_field, second_sketch, precision=precise)
    partial_third = jnp.einsum("plk,pk->lk", along_third, plane_sketch[:, 1, :], precision=precise)

    range_second_block = jnp.dot(partial_second, mixing[0], precision=precise)
    range_third = jnp.dot(partial_third, mixing[1], precision=precise)
    full_rows = rows * af_size
    range_second = lax.dynamic_update_slice_in_dim(
        jnp.zeros((full_rows, rank_cols), jnp.float32), range_second_block, af_index * rows, 0
    )
    both = allreduce_all(jnp.concatenate([range_second, range_third], axis=0))

    ranges = both.reshape(2, full_rows, rank_cols)
    grams = jnp.einsum("nji,njk->nik", ranges, ranges, precision=precise)
    own_second = lax.dynamic_slice_in_dim(ranges[0], af_index * rows, rows, 0)
    panel_third, panel_second = factor_panels(
        jnp.concatenate([grams[1], ranges[1].T], axis=1),
        jnp.concatenate([grams[0], own_second.T], axis=1),
    )
    factor_third_all = panel_third[:, rank_cols:].T
    basis_second = panel_second[:, rank_cols:].T

    out_second = full_rows // (gx_size * af_size)
    assert rows == gx_size * out_second
    factor_second = lax.dynamic_slice_in_dim(basis_second, gx_index * out_second, out_second, 0)
    factor_third = lax.dynamic_slice_in_dim(
        factor_third_all, (gx_index * af_size + af_index) * out_second, out_second, 0
    )
    left_side = jnp.einsum("jr,pjl->prl", basis_second, scalar_field, precision=precise)
    projected = jnp.einsum("prl,ls->prs", left_side, factor_third_all, precision=precise)
    cycle = BLOCK // planes
    groups = gx_size // cycle
    assert planes * gx_size == BLOCKS * BLOCK and groups == BLOCKS
    own_targets = lax.dynamic_slice_in_dim(plane_targets, gx_index * planes, planes, 0)
    own_signs = lax.dynamic_slice_in_dim(plane_signs, gx_index * planes, planes, 0)
    sign_values = (2 * own_signs - 1).astype(jnp.float32)
    block_ids = jnp.arange(groups, dtype=jnp.int32)
    weights = jnp.sum(
        jnp.where(own_targets[None, :, :] == block_ids[:, None, None], sign_values[None, :, :], 0.0),
        axis=2,
    )
    slab = rank_cols // af_size
    pieces = projected.reshape(planes, af_size, slab, rank_cols).transpose(1, 0, 2, 3)
    lane_weights = jnp.broadcast_to(weights[:, :, None, None], (groups, planes, 1, rank_cols))
    core_sketch = core_exchange(pieces, lane_weights, cycle)
    return (factor_second, factor_third, core_sketch)


def solution(mesh):
    in_specs = (P("gx", "af", None), P("gx", None, None), P("af", None), P(), P(), P(), P())
    out_specs = (P(("af", "gx"), None), P(("gx", "af"), None), P("gx", "af", None))
    return jax.shard_map(body, mesh=mesh, in_specs=in_specs, out_specs=out_specs, check_vma=False)
```

```python
import functools

import jax
import jax.numpy as jnp
from jax import lax
from jax.experimental import pallas as pl
from jax.experimental.pallas import tpu as pltpu
from jax.sharding import PartitionSpec as P

MESH = pl.DeviceIdType.MESH

BLOCK = 16
BLOCKS = 8


precise = lax.Precision.HIGHEST


def partner_list(gx_size, af_size):
    preferred = [("gx", 1), ("gx", 2), ("gx", 16), ("af", 1), ("gx", 4), ("gx", 32), ("af", 2), ("gx", 8)]
    sizes = {"gx": gx_size, "af": af_size}
    steps = [(axis, bit) for axis, bit in preferred if bit < sizes[axis]]
    for axis in ("gx", "af"):
        bit = 1
        while bit < sizes[axis]:
            if (axis, bit) not in steps:
                steps.append((axis, bit))
            bit *= 2
    return steps


def allreduce_kernel(digits, x_ref, o_ref, acc, recv, exchange, gathered, send_sem, recv_sem):
    index = {"gx": lax.axis_index("gx"), "af": lax.axis_index("af")}

    def bits_of(digit):
        return [(index[axis] // bit) % 2 for axis, bit in digit]

    def member(digit):
        return sum(own * 2**t for t, own in enumerate(bits_of(digit)))

    def flipped(digit, d):
        return sum(
            (own + ((d >> t) & 1) * (1 - 2 * own)) * 2**t for t, own in enumerate(bits_of(digit))
        )

    def device(digit, d):
        values = dict(index)
        for t, ((axis, bit), own) in enumerate(zip(digit, bits_of(digit))):
            values[axis] = values[axis] + bit * ((d >> t) & 1) * (1 - 2 * own)
        return (values["gx"], values["af"])

    def others(digit):
        return range(1, 2 ** len(digit))

    barrier = pltpu.get_barrier_semaphore()
    for digit in digits:
        for d in others(digit):
            pl.semaphore_signal(barrier, inc=1, device_id=device(digit, d), device_id_type=MESH)
    pl.semaphore_wait(barrier, sum(len(others(digit)) for digit in digits))

    counter = [0]

    def start(device_id, source, target):
        n = counter[0]
        counter[0] += 1
        copy = pltpu.make_async_remote_copy(
            src_ref=source,
            dst_ref=target,
            send_sem=send_sem.at[n],
            recv_sem=recv_sem.at[n],
            device_id=device_id,
            device_id_type=MESH,
        )
        copy.start()
        return copy

    acc[...] = x_ref[...]
    offset, length, slot = 0, acc.shape[0], 0
    parents = []
    for digit in digits[:-1]:
        me = member(digit)
        part = length // 2 ** len(digit)
        copies = []
        for d in others(digit):
            give = pl.multiple_of(offset + flipped(digit, d) * part, 8)
            target = recv.at[pl.ds(slot + (d - 1) * part, part)]
            copies.append(start(device(digit, d), acc.at[pl.ds(give, part)], target))
        for copy in copies:
            copy.wait()
        keep = pl.multiple_of(offset + me * part, 8)
        total = acc[pl.ds(keep, part), :]
        for d in others(digit):
            total = total + recv[pl.ds(slot + (d - 1) * part, part), :]
        acc[pl.ds(keep, part), :] = total
        parents.append((offset, length))
        offset, length, slot = keep, part, slot + len(others(digit)) * part

    last = digits[-1]
    me = member(last)
    segment = acc.at[pl.ds(offset, length)]
    copies = [start(device(last, d), segment, exchange.at[me]) for d in others(last)]
    exchange[me] = acc[pl.ds(offset, length), :]
    for copy in copies:
        copy.wait()
    total = exchange[0]
    for q in range(1, 2 ** len(last)):
        total = total + exchange[q]
    gathered[pl.ds(offset, length), :] = total

    for digit, (parent_offset, parent_length) in zip(reversed(digits[:-1]), reversed(parents)):
        part = gathered.at[pl.ds(offset, length)]
        copies = [start(device(digit, d), part, part) for d in others(digit)]
        for copy in copies:
            copy.wait()
        offset, length = parent_offset, parent_length
    o_ref[...] = gathered[...]


def allreduce_all(x):
    steps = partner_list(lax.axis_size("gx"), lax.axis_size("af"))
    digits = [steps[t:t + 3] for t in range(0, len(steps), 3)]
    last_rows = x.shape[0]
    for digit in digits[:-1]:
        last_rows //= 2 ** len(digit)
    assert last_rows % 8 == 0
    copies = sum(2 * (2 ** len(digit) - 1) for digit in digits[:-1]) + 2 ** len(digits[-1]) - 1
    return pl.pallas_call(
        functools.partial(allreduce_kernel, digits),
        out_shape=jax.ShapeDtypeStruct(x.shape, x.dtype),
        in_specs=[pl.BlockSpec(memory_space=pltpu.VMEM)],
        out_specs=pl.BlockSpec(memory_space=pltpu.VMEM),
        scratch_shapes=[
            pltpu.VMEM(x.shape, x.dtype),
            pltpu.VMEM(x.shape, x.dtype),
            pltpu.VMEM((2 ** len(digits[-1]), last_rows) + x.shape[1:], x.dtype),
            pltpu.VMEM(x.shape, x.dtype),
            pltpu.SemaphoreType.DMA((copies,)),
            pltpu.SemaphoreType.DMA((copies,)),
        ],
        compiler_params=pltpu.CompilerParams(collective_id=0, has_side_effects=True),
    )(x)


def panel_kernel(both_ref, third_ref, second_ref):
    outputs = (third_ref, second_ref)
    rank = third_ref.shape[0]
    half = both_ref.shape[0] // 2
    own_rows = second_ref.shape[1] - rank
    for target, ranged in ((third_ref, both_ref[half:, :]), (second_ref, both_ref[:half, :])):
        flipped = ranged.T
        target[:, :rank] = jnp.dot(
            flipped, ranged, precision=lax.Precision.HIGHEST, preferred_element_type=jnp.float32
        )
    third_ref[:, rank:] = both_ref[half:, :].T
    start = pl.multiple_of(lax.axis_index("af") * own_rows, 8)
    second_ref[:, rank:] = both_ref[pl.ds(start, own_rows), :].T

    def step(first, j, carry):
        for ref in outputs:
            width = ref.shape[1]
            row = ref[pl.ds(j, 1), :]
            lanes = lax.broadcasted_iota(jnp.int32, (1, width), 1)
            square_lanes = lax.broadcasted_iota(jnp.int32, (1, rank), 1)
            pivot = jnp.sum(
                jnp.where(square_lanes == j, row[:, :rank], 0.0), axis=1, keepdims=True
            )
            inverse = 1.0 / jnp.sqrt(pivot)
            column = jnp.where(lanes < j, 0.0, row * inverse)
            count = rank - first
            block = ref[pl.ds(first, count), :]
            cols = lax.broadcasted_iota(jnp.int32, (count, rank), 1)
            upper = jnp.sum(jnp.where(cols == j, block[:, :rank], 0.0), axis=1, keepdims=True)
            below = lax.broadcasted_iota(jnp.int32, (count, 1), 0) + first > j
            scale = jnp.where(below, upper * inverse, 0.0)
            ref[pl.ds(first, count), :] = block - scale * column
            ref[pl.ds(j, 1), :] = column
        return carry

    span = 16
    for first in range(0, rank, span):
        lax.fori_loop(first, first + span, functools.partial(step, first), 0, unroll=2)


def factor_panels(both, rows):
    rank = both.shape[1]
    half = both.shape[0] // 2
    return pl.pallas_call(
        panel_kernel,
        out_shape=[
            jax.ShapeDtypeStruct((rank, rank + half), both.dtype),
            jax.ShapeDtypeStruct((rank, rank + rows), both.dtype),
        ],
        in_specs=[pl.BlockSpec(memory_space=pltpu.VMEM)],
        out_specs=[pl.BlockSpec(memory_space=pltpu.VMEM)] * 2,
    )(both)


def core_kernel(cycle, pieces_ref, weights_ref, o_ref, first, staged, second, send_sem, recv_sem):
    g = lax.axis_index("gx")
    a = lax.axis_index("af")
    quarters, blocks = pieces_ref.shape[0], weights_ref.shape[0]
    k = g // cycle
    c = g % cycle
    peers = [(a + d) % quarters for d in range(1, quarters)]
    owners = [(k + d) % blocks for d in range(1, blocks)]

    def peer(j):
        return (g, j)

    def owner(j):
        return (j * cycle + c, a)

    barrier = pltpu.get_barrier_semaphore()
    for device in [peer(j) for j in peers] + [owner(j) for j in owners]:
        pl.semaphore_signal(barrier, inc=1, device_id=device, device_id_type=MESH)
    pl.semaphore_wait(barrier, len(peers) + len(owners))

    def start(n, source, target, device):
        copy = pltpu.make_async_remote_copy(
            src_ref=source,
            dst_ref=target,
            send_sem=send_sem.at[n],
            recv_sem=recv_sem.at[n],
            device_id=device,
            device_id_type=MESH,
        )
        copy.start()
        return copy

    copies = [start(n, pieces_ref.at[j], first.at[n], peer(j)) for n, j in enumerate(peers)]
    for copy in copies:
        copy.wait()
    total = pieces_ref[a]
    for n in range(len(peers)):
        total = total + first[n]
    for j in range(blocks):
        staged[j] = weights_ref[j] * total
    base = len(peers)
    copies = [
        start(base + n, staged.at[j], second.at[n], owner(j)) for n, j in enumerate(owners)
    ]
    for copy in copies:
        copy.wait()
    result = staged[k]
    for n in range(len(owners)):
        result = result + second[n]
    o_ref[...] = result


def core_exchange(pieces, weights, cycle):
    quarters, blocks = pieces.shape[0], weights.shape[0]
    piece = pieces.shape[1:]
    return pl.pallas_call(
        functools.partial(core_kernel, cycle),
        out_shape=jax.ShapeDtypeStruct(piece, pieces.dtype),
        in_specs=[pl.BlockSpec(memory_space=pltpu.VMEM)] * 2,
        out_specs=pl.BlockSpec(memory_space=pltpu.VMEM),
        scratch_shapes=[
            pltpu.VMEM((quarters - 1,) + piece, pieces.dtype),
            pltpu.VMEM((blocks,) + piece, pieces.dtype),
            pltpu.VMEM((blocks - 1,) + piece, pieces.dtype),
            pltpu.SemaphoreType.DMA((quarters + blocks - 2,)),
            pltpu.SemaphoreType.DMA((quarters + blocks - 2,)),
        ],
        compiler_params=pltpu.CompilerParams(collective_id=1, has_side_effects=True),
    )(pieces, weights)


def body(
    scalar_field, plane_sketch, second_sketch, third_sketch, mixing, plane_targets, plane_signs
):
    planes, rows, cells = scalar_field.shape
    rank_cols = mixing.shape[2]
    gx_index = lax.axis_index("gx")
    af_index = lax.axis_index("af")
    gx_size = lax.axis_size("gx")
    af_size = lax.axis_size("af")

    along_second = jnp.einsum("pjl,lk->pjk", scalar_field, third_sketch, precision=precise)
    partial_second = jnp.einsum(
        "pjk,pk->jk", along_second, plane_sketch[:, 0, :], precision=precise
    )
    along_third = jnp.einsum("pjl,jk->plk", scalar_field, second_sketch, precision=precise)
    partial_third = jnp.einsum("plk,pk->lk", along_third, plane_sketch[:, 1, :], precision=precise)

    range_second_block = jnp.dot(partial_second, mixing[0], precision=precise)
    range_third = jnp.dot(partial_third, mixing[1], precision=precise)
    full_rows = rows * af_size
    range_second = lax.dynamic_update_slice_in_dim(
        jnp.zeros((full_rows, rank_cols), jnp.float32), range_second_block, af_index * rows, 0
    )
    both = allreduce_all(jnp.concatenate([range_second, range_third], axis=0))

    panel_third, panel_second = factor_panels(both, rows)
    factor_third_all = panel_third[:, rank_cols:].T
    basis_second = panel_second[:, rank_cols:].T

    out_second = full_rows // (gx_size * af_size)
    assert rows == gx_size * out_second
    factor_second = lax.dynamic_slice_in_dim(basis_second, gx_index * out_second, out_second, 0)
    factor_third = lax.dynamic_slice_in_dim(
        factor_third_all, (gx_index * af_size + af_index) * out_second, out_second, 0
    )
    left_side = jnp.einsum("jr,pjl->prl", basis_second, scalar_field, precision=precise)
    projected = jnp.einsum("prl,ls->prs", left_side, factor_third_all, precision=precise)
    cycle = BLOCK // planes
    groups = gx_size // cycle
    assert planes * gx_size == BLOCKS * BLOCK and groups == BLOCKS
    own_targets = lax.dynamic_slice_in_dim(plane_targets, gx_index * planes, planes, 0)
    own_signs = lax.dynamic_slice_in_dim(plane_signs, gx_index * planes, planes, 0)
    sign_values = (2 * own_signs - 1).astype(jnp.float32)
    block_ids = jnp.arange(groups, dtype=jnp.int32)
    weights = jnp.sum(
        jnp.where(own_targets[None, :, :] == block_ids[:, None, None], sign_values[None, :, :], 0.0),
        axis=2,
    )
    slab = rank_cols // af_size
    pieces = projected.reshape(planes, af_size, slab, rank_cols).transpose(1, 0, 2, 3)
    lane_weights = jnp.broadcast_to(weights[:, :, None, None], (groups, planes, 1, rank_cols))
    core_sketch = core_exchange(pieces, lane_weights, cycle)
    return (factor_second, factor_third, core_sketch)


def solution(mesh):
    in_specs = (P("gx", "af", None), P("gx", None, None), P("af", None), P(), P(), P(), P())
    out_specs = (P(("af", "gx"), None), P(("gx", "af"), None), P("gx", "af", None))
    return jax.shard_map(body, mesh=mesh, in_specs=in_specs, out_specs=out_specs, check_vma=False)
```

```python
import functools

import jax
import jax.numpy as jnp
from jax import lax
from jax.experimental import pallas as pl
from jax.experimental.pallas import tpu as pltpu
from jax.sharding import PartitionSpec as P

MESH = pl.DeviceIdType.MESH

BLOCK = 16
BLOCKS = 8


precise = lax.Precision.HIGHEST


def partner_list(gx_size, af_size):
    preferred = [("gx", 1), ("gx", 2), ("gx", 16), ("af", 1), ("gx", 4), ("gx", 32), ("af", 2), ("gx", 8)]
    sizes = {"gx": gx_size, "af": af_size}
    steps = [(axis, bit) for axis, bit in preferred if bit < sizes[axis]]
    for axis in ("gx", "af"):
        bit = 1
        while bit < sizes[axis]:
            if (axis, bit) not in steps:
                steps.append((axis, bit))
            bit *= 2
    return steps


def allreduce_kernel(digits, x_ref, o_ref, acc, recv, exchange, gathered, send_sem, recv_sem):
    index = {"gx": lax.axis_index("gx"), "af": lax.axis_index("af")}

    def bits_of(digit):
        return [(index[axis] // bit) % 2 for axis, bit in digit]

    def member(digit):
        return sum(own * 2**t for t, own in enumerate(bits_of(digit)))

    def flipped(digit, d):
        return sum(
            (own + ((d >> t) & 1) * (1 - 2 * own)) * 2**t for t, own in enumerate(bits_of(digit))
        )

    def device(digit, d):
        values = dict(index)
        for t, ((axis, bit), own) in enumerate(zip(digit, bits_of(digit))):
            values[axis] = values[axis] + bit * ((d >> t) & 1) * (1 - 2 * own)
        return (values["gx"], values["af"])

    def others(digit):
        return range(1, 2 ** len(digit))

    barrier = pltpu.get_barrier_semaphore()
    for digit in digits:
        for d in others(digit):
            pl.semaphore_signal(barrier, inc=1, device_id=device(digit, d), device_id_type=MESH)
    pl.semaphore_wait(barrier, sum(len(others(digit)) for digit in digits))

    counter = [0]

    def start(device_id, source, target):
        n = counter[0]
        counter[0] += 1
        copy = pltpu.make_async_remote_copy(
            src_ref=source,
            dst_ref=target,
            send_sem=send_sem.at[n],
            recv_sem=recv_sem.at[n],
            device_id=device_id,
            device_id_type=MESH,
        )
        copy.start()
        return copy

    acc[...] = x_ref[...]
    offset, length, slot = 0, acc.shape[0], 0
    parents = []
    for digit in digits[:-1]:
        me = member(digit)
        part = length // 2 ** len(digit)
        copies = []
        for d in others(digit):
            give = pl.multiple_of(offset + flipped(digit, d) * part, 8)
            target = recv.at[pl.ds(slot + (d - 1) * part, part)]
            copies.append(start(device(digit, d), acc.at[pl.ds(give, part)], target))
        for copy in copies:
            copy.wait()
        keep = pl.multiple_of(offset + me * part, 8)
        total = acc[pl.ds(keep, part), :]
        for d in others(digit):
            total = total + recv[pl.ds(slot + (d - 1) * part, part), :]
        acc[pl.ds(keep, part), :] = total
        parents.append((offset, length))
        offset, length, slot = keep, part, slot + len(others(digit)) * part

    last = digits[-1]
    me = member(last)
    segment = acc.at[pl.ds(offset, length)]
    copies = [start(device(last, d), segment, exchange.at[me]) for d in others(last)]
    exchange[me] = acc[pl.ds(offset, length), :]
    for copy in copies:
        copy.wait()
    total = exchange[0]
    for q in range(1, 2 ** len(last)):
        total = total + exchange[q]
    gathered[pl.ds(offset, length), :] = total

    for digit, (parent_offset, parent_length) in zip(reversed(digits[:-1]), reversed(parents)):
        part = gathered.at[pl.ds(offset, length)]
        copies = [start(device(digit, d), part, part) for d in others(digit)]
        for copy in copies:
            copy.wait()
        offset, length = parent_offset, parent_length
    o_ref[...] = gathered[...]


def allreduce_all(x):
    steps = partner_list(lax.axis_size("gx"), lax.axis_size("af"))
    digits = [steps[t:t + 3] for t in range(0, len(steps), 3)]
    last_rows = x.shape[0]
    for digit in digits[:-1]:
        last_rows //= 2 ** len(digit)
    assert last_rows % 8 == 0
    copies = sum(2 * (2 ** len(digit) - 1) for digit in digits[:-1]) + 2 ** len(digits[-1]) - 1
    return pl.pallas_call(
        functools.partial(allreduce_kernel, digits),
        out_shape=jax.ShapeDtypeStruct(x.shape, x.dtype),
        in_specs=[pl.BlockSpec(memory_space=pltpu.VMEM)],
        out_specs=pl.BlockSpec(memory_space=pltpu.VMEM),
        scratch_shapes=[
            pltpu.VMEM(x.shape, x.dtype),
            pltpu.VMEM(x.shape, x.dtype),
            pltpu.VMEM((2 ** len(digits[-1]), last_rows) + x.shape[1:], x.dtype),
            pltpu.VMEM(x.shape, x.dtype),
            pltpu.SemaphoreType.DMA((copies,)),
            pltpu.SemaphoreType.DMA((copies,)),
        ],
        compiler_params=pltpu.CompilerParams(collective_id=0, has_side_effects=True),
    )(x)


def panel_kernel(both_ref, third_ref, second_ref):
    outputs = (third_ref, second_ref)
    rank = third_ref.shape[0]
    half = both_ref.shape[0] // 2
    own_rows = second_ref.shape[1] - rank
    for target, ranged in ((third_ref, both_ref[half:, :]), (second_ref, both_ref[:half, :])):
        flipped = ranged.T
        target[:, :rank] = jnp.dot(
            flipped, ranged, precision=lax.Precision.HIGHEST, preferred_element_type=jnp.float32
        )
    third_ref[:, rank:] = both_ref[half:, :].T
    start = pl.multiple_of(lax.axis_index("af") * own_rows, 8)
    second_ref[:, rank:] = both_ref[pl.ds(start, own_rows), :].T

    def step(first, j, carry):
        for ref in outputs:
            width = ref.shape[1]
            row = ref[pl.ds(j, 1), :]
            lanes = lax.broadcasted_iota(jnp.int32, (1, width), 1)
            square_lanes = lax.broadcasted_iota(jnp.int32, (1, rank), 1)
            pivot = jnp.sum(
                jnp.where(square_lanes == j, row[:, :rank], 0.0), axis=1, keepdims=True
            )
            inverse = 1.0 / jnp.sqrt(pivot)
            column = jnp.where(lanes < j, 0.0, row * inverse)
            count = rank - first
            block = ref[pl.ds(first, count), :]
            cols = lax.broadcasted_iota(jnp.int32, (count, rank), 1)
            upper = jnp.sum(jnp.where(cols == j, block[:, :rank], 0.0), axis=1, keepdims=True)
            below = lax.broadcasted_iota(jnp.int32, (count, 1), 0) + first > j
            scale = jnp.where(below, upper * inverse, 0.0)
            ref[pl.ds(first, count), :] = block - scale * column
            ref[pl.ds(j, 1), :] = column
        return carry

    span = 16
    for first in range(0, rank, span):
        lax.fori_loop(first, first + span, functools.partial(step, first), 0, unroll=2)


def factor_panels(both, rows):
    rank = both.shape[1]
    half = both.shape[0] // 2
    return pl.pallas_call(
        panel_kernel,
        out_shape=[
            jax.ShapeDtypeStruct((rank, rank + half), both.dtype),
            jax.ShapeDtypeStruct((rank, rank + rows), both.dtype),
        ],
        in_specs=[pl.BlockSpec(memory_space=pltpu.VMEM)],
        out_specs=[pl.BlockSpec(memory_space=pltpu.VMEM)] * 2,
    )(both)


def core_kernel(
    cycle, field_ref, left_ref, right_ref, weights_ref, o_ref,
    pieces_ref, first, staged, second, send_sem, recv_sem,
):
    g = lax.axis_index("gx")
    a = lax.axis_index("af")
    quarters, planes, slab = pieces_ref.shape[:3]
    blocks = weights_ref.shape[0]
    rank = right_ref.shape[0]
    for p in range(planes):
        left = jnp.dot(
            left_ref[:, rank:], field_ref[p],
            precision=lax.Precision.HIGHEST, preferred_element_type=jnp.float32,
        )
        projected = lax.dot_general(
            left, right_ref[:, rank:], (((1,), (1,)), ((), ())),
            precision=lax.Precision.HIGHEST, preferred_element_type=jnp.float32,
        )
        for q in range(quarters):
            pieces_ref[q, p] = projected[q * slab:(q + 1) * slab, :]
    k = g // cycle
    c = g % cycle
    peers = [(a + d) % quarters for d in range(1, quarters)]
    owners = [(k + d) % blocks for d in range(1, blocks)]

    def peer(j):
        return (g, j)

    def owner(j):
        return (j * cycle + c, a)

    barrier = pltpu.get_barrier_semaphore()
    for device in [peer(j) for j in peers] + [owner(j) for j in owners]:
        pl.semaphore_signal(barrier, inc=1, device_id=device, device_id_type=MESH)
    pl.semaphore_wait(barrier, len(peers) + len(owners))

    def start(n, source, target, device):
        copy = pltpu.make_async_remote_copy(
            src_ref=source,
            dst_ref=target,
            send_sem=send_sem.at[n],
            recv_sem=recv_sem.at[n],
            device_id=device,
            device_id_type=MESH,
        )
        copy.start()
        return copy

    copies = [start(n, pieces_ref.at[j], first.at[n], peer(j)) for n, j in enumerate(peers)]
    for copy in copies:
        copy.wait()
    total = pieces_ref[a]
    for n in range(len(peers)):
        total = total + first[n]
    for j in range(blocks):
        staged[j] = weights_ref[j] * total
    base = len(peers)
    copies = [
        start(base + n, staged.at[j], second.at[n], owner(j)) for n, j in enumerate(owners)
    ]
    for copy in copies:
        copy.wait()
    result = staged[k]
    for n in range(len(owners)):
        result = result + second[n]
    o_ref[...] = result


def core_exchange(field, left, right, weights, cycle, quarters):
    planes, rank = field.shape[0], right.shape[0]
    blocks = weights.shape[0]
    piece = (planes, rank // quarters, rank)
    dtype = field.dtype
    return pl.pallas_call(
        functools.partial(core_kernel, cycle),
        out_shape=jax.ShapeDtypeStruct(piece, dtype),
        in_specs=[pl.BlockSpec(memory_space=pltpu.VMEM)] * 4,
        out_specs=pl.BlockSpec(memory_space=pltpu.VMEM),
        scratch_shapes=[
            pltpu.VMEM((quarters,) + piece, dtype),
            pltpu.VMEM((quarters - 1,) + piece, dtype),
            pltpu.VMEM((blocks,) + piece, dtype),
            pltpu.VMEM((blocks - 1,) + piece, dtype),
            pltpu.SemaphoreType.DMA((quarters + blocks - 2,)),
            pltpu.SemaphoreType.DMA((quarters + blocks - 2,)),
        ],
        compiler_params=pltpu.CompilerParams(collective_id=1, has_side_effects=True),
    )(field, left, right, weights)


def body(
    scalar_field, plane_sketch, second_sketch, third_sketch, mixing, plane_targets, plane_signs
):
    planes, rows, cells = scalar_field.shape
    rank_cols = mixing.shape[2]
    gx_index = lax.axis_index("gx")
    af_index = lax.axis_index("af")
    gx_size = lax.axis_size("gx")
    af_size = lax.axis_size("af")

    along_second = jnp.einsum("pjl,lk->pjk", scalar_field, third_sketch, precision=precise)
    partial_second = jnp.einsum(
        "pjk,pk->jk", along_second, plane_sketch[:, 0, :], precision=precise
    )
    along_third = jnp.einsum("pjl,jk->plk", scalar_field, second_sketch, precision=precise)
    partial_third = jnp.einsum("plk,pk->lk", along_third, plane_sketch[:, 1, :], precision=precise)

    range_second_block = jnp.dot(partial_second, mixing[0], precision=precise)
    range_third = jnp.dot(partial_third, mixing[1], precision=precise)
    full_rows = rows * af_size
    range_second = lax.dynamic_update_slice_in_dim(
        jnp.zeros((full_rows, rank_cols), jnp.float32), range_second_block, af_index * rows, 0
    )
    both = allreduce_all(jnp.concatenate([range_second, range_third], axis=0))

    panel_third, panel_second = factor_panels(both, rows)
    factor_third_all = panel_third[:, rank_cols:].T
    basis_second = panel_second[:, rank_cols:].T

    out_second = full_rows // (gx_size * af_size)
    assert rows == gx_size * out_second
    factor_second = lax.dynamic_slice_in_dim(basis_second, gx_index * out_second, out_second, 0)
    factor_third = lax.dynamic_slice_in_dim(
        factor_third_all, (gx_index * af_size + af_index) * out_second, out_second, 0
    )
    cycle = BLOCK // planes
    groups = gx_size // cycle
    assert planes * gx_size == BLOCKS * BLOCK and groups == BLOCKS
    own_targets = lax.dynamic_slice_in_dim(plane_targets, gx_index * planes, planes, 0)
    own_signs = lax.dynamic_slice_in_dim(plane_signs, gx_index * planes, planes, 0)
    sign_values = (2 * own_signs - 1).astype(jnp.float32)
    block_ids = jnp.arange(groups, dtype=jnp.int32)
    weights = jnp.sum(
        jnp.where(own_targets[None, :, :] == block_ids[:, None, None], sign_values[None, :, :], 0.0),
        axis=2,
    )
    lane_weights = jnp.broadcast_to(weights[:, :, None, None], (groups, planes, 1, rank_cols))
    core_sketch = core_exchange(
        scalar_field, panel_second, panel_third, lane_weights, cycle, af_size
    )
    return (factor_second, factor_third, core_sketch)


def solution(mesh):
    in_specs = (P("gx", "af", None), P("gx", None, None), P("af", None), P(), P(), P(), P())
    out_specs = (P(("af", "gx"), None), P(("gx", "af"), None), P("gx", "af", None))
    return jax.shard_map(body, mesh=mesh, in_specs=in_specs, out_specs=out_specs, check_vma=False)
```

```python
import functools

import jax
import jax.numpy as jnp
from jax import lax
from jax.experimental import pallas as pl
from jax.experimental.pallas import tpu as pltpu
from jax.sharding import PartitionSpec as P

MESH = pl.DeviceIdType.MESH

BLOCK = 16
BLOCKS = 8


precise = lax.Precision.HIGHEST


def partner_list(gx_size, af_size):
    preferred = [("gx", 1), ("gx", 2), ("gx", 16), ("af", 1), ("gx", 4), ("gx", 32), ("af", 2), ("gx", 8)]
    sizes = {"gx": gx_size, "af": af_size}
    steps = [(axis, bit) for axis, bit in preferred if bit < sizes[axis]]
    for axis in ("gx", "af"):
        bit = 1
        while bit < sizes[axis]:
            if (axis, bit) not in steps:
                steps.append((axis, bit))
            bit *= 2
    return steps


def allreduce_kernel(digits, x_ref, o_ref, acc, recv, exchange, gathered, send_sem, recv_sem):
    index = {"gx": lax.axis_index("gx"), "af": lax.axis_index("af")}

    def bits_of(digit):
        return [(index[axis] // bit) % 2 for axis, bit in digit]

    def member(digit):
        return sum(own * 2**t for t, own in enumerate(bits_of(digit)))

    def flipped(digit, d):
        return sum(
            (own + ((d >> t) & 1) * (1 - 2 * own)) * 2**t for t, own in enumerate(bits_of(digit))
        )

    def device(digit, d):
        values = dict(index)
        for t, ((axis, bit), own) in enumerate(zip(digit, bits_of(digit))):
            values[axis] = values[axis] + bit * ((d >> t) & 1) * (1 - 2 * own)
        return (values["gx"], values["af"])

    def others(digit):
        return range(1, 2 ** len(digit))

    barrier = pltpu.get_barrier_semaphore()
    for digit in digits:
        for d in others(digit):
            pl.semaphore_signal(barrier, inc=1, device_id=device(digit, d), device_id_type=MESH)
    pl.semaphore_wait(barrier, sum(len(others(digit)) for digit in digits))

    counter = [0]

    def start(device_id, source, target):
        n = counter[0]
        counter[0] += 1
        copy = pltpu.make_async_remote_copy(
            src_ref=source,
            dst_ref=target,
            send_sem=send_sem.at[n],
            recv_sem=recv_sem.at[n],
            device_id=device_id,
            device_id_type=MESH,
        )
        copy.start()
        return copy

    acc[...] = x_ref[...]
    offset, length, slot = 0, acc.shape[0], 0
    parents = []
    for digit in digits[:-1]:
        me = member(digit)
        part = length // 2 ** len(digit)
        copies = []
        for d in others(digit):
            give = pl.multiple_of(offset + flipped(digit, d) * part, 8)
            target = recv.at[pl.ds(slot + (d - 1) * part, part)]
            copies.append(start(device(digit, d), acc.at[pl.ds(give, part)], target))
        for copy in copies:
            copy.wait()
        keep = pl.multiple_of(offset + me * part, 8)
        total = acc[pl.ds(keep, part), :]
        for d in others(digit):
            total = total + recv[pl.ds(slot + (d - 1) * part, part), :]
        acc[pl.ds(keep, part), :] = total
        parents.append((offset, length))
        offset, length, slot = keep, part, slot + len(others(digit)) * part

    last = digits[-1]
    me = member(last)
    segment = acc.at[pl.ds(offset, length)]
    copies = [start(device(last, d), segment, exchange.at[me]) for d in others(last)]
    exchange[me] = acc[pl.ds(offset, length), :]
    for copy in copies:
        copy.wait()
    total = exchange[0]
    for q in range(1, 2 ** len(last)):
        total = total + exchange[q]
    gathered[pl.ds(offset, length), :] = total

    for digit, (parent_offset, parent_length) in zip(reversed(digits[:-1]), reversed(parents)):
        part = gathered.at[pl.ds(offset, length)]
        copies = [start(device(digit, d), part, part) for d in others(digit)]
        for copy in copies:
            copy.wait()
        offset, length = parent_offset, parent_length
    o_ref[...] = gathered[...]


def allreduce_all(x):
    steps = partner_list(lax.axis_size("gx"), lax.axis_size("af"))
    digits = [steps[t:t + 3] for t in range(0, len(steps), 3)]
    last_rows = x.shape[0]
    for digit in digits[:-1]:
        last_rows //= 2 ** len(digit)
    assert last_rows % 8 == 0
    copies = sum(2 * (2 ** len(digit) - 1) for digit in digits[:-1]) + 2 ** len(digits[-1]) - 1
    return pl.pallas_call(
        functools.partial(allreduce_kernel, digits),
        out_shape=jax.ShapeDtypeStruct(x.shape, x.dtype),
        in_specs=[pl.BlockSpec(memory_space=pltpu.VMEM)],
        out_specs=pl.BlockSpec(memory_space=pltpu.VMEM),
        scratch_shapes=[
            pltpu.VMEM(x.shape, x.dtype),
            pltpu.VMEM(x.shape, x.dtype),
            pltpu.VMEM((2 ** len(digits[-1]), last_rows) + x.shape[1:], x.dtype),
            pltpu.VMEM(x.shape, x.dtype),
            pltpu.SemaphoreType.DMA((copies,)),
            pltpu.SemaphoreType.DMA((copies,)),
        ],
        compiler_params=pltpu.CompilerParams(collective_id=0, has_side_effects=True),
    )(x)


def panel_kernel(both_ref, third_ref, second_ref):
    outputs = (third_ref, second_ref)
    rank = third_ref.shape[0]
    half = both_ref.shape[0] // 2
    own_rows = second_ref.shape[1] - rank
    for target, ranged in ((third_ref, both_ref[half:, :]), (second_ref, both_ref[:half, :])):
        flipped = ranged.T
        target[:, :rank] = jnp.dot(
            flipped, ranged, precision=lax.Precision.HIGHEST, preferred_element_type=jnp.float32
        )
    third_ref[:, rank:] = both_ref[half:, :].T
    start = pl.multiple_of(lax.axis_index("af") * own_rows, 8)
    second_ref[:, rank:] = both_ref[pl.ds(start, own_rows), :].T

    def step(first, j, carry):
        for ref in outputs:
            width = ref.shape[1]
            row = ref[pl.ds(j, 1), :]
            lanes = lax.broadcasted_iota(jnp.int32, (1, width), 1)
            square_lanes = lax.broadcasted_iota(jnp.int32, (1, rank), 1)
            pivot = jnp.sum(
                jnp.where(square_lanes == j, row[:, :rank], 0.0), axis=1, keepdims=True
            )
            inverse = 1.0 / jnp.sqrt(pivot)
            column = jnp.where(lanes < j, 0.0, row * inverse)
            count = rank - first
            block = ref[pl.ds(first, count), :]
            cols = lax.broadcasted_iota(jnp.int32, (count, rank), 1)
            upper = jnp.sum(jnp.where(cols == j, block[:, :rank], 0.0), axis=1, keepdims=True)
            below = lax.broadcasted_iota(jnp.int32, (count, 1), 0) + first > j
            scale = jnp.where(below, upper * inverse, 0.0)
            ref[pl.ds(first, count), :] = block - scale * column
            ref[pl.ds(j, 1), :] = column
        return carry

    span = 16
    for first in range(0, rank, span):
        lax.fori_loop(first, first + span, functools.partial(step, first), 0, unroll=2)


def factor_panels(both, rows):
    rank = both.shape[1]
    half = both.shape[0] // 2
    return pl.pallas_call(
        panel_kernel,
        out_shape=[
            jax.ShapeDtypeStruct((rank, rank + half), both.dtype),
            jax.ShapeDtypeStruct((rank, rank + rows), both.dtype),
        ],
        in_specs=[pl.BlockSpec(memory_space=pltpu.VMEM)],
        out_specs=[pl.BlockSpec(memory_space=pltpu.VMEM)] * 2,
    )(both)


def core_kernel(
    cycle, blocks, field_ref, left_ref, right_ref, targets_ref, signs_ref, o_ref,
    pieces_ref, first, staged, second, send_sem, recv_sem,
):
    g = lax.axis_index("gx")
    a = lax.axis_index("af")
    quarters, planes, slab = pieces_ref.shape[:3]
    rank = right_ref.shape[0]
    for p in range(planes):
        left = jnp.dot(
            left_ref[:, rank:], field_ref[p],
            precision=lax.Precision.HIGHEST, preferred_element_type=jnp.float32,
        )
        projected = lax.dot_general(
            left, right_ref[:, rank:], (((1,), (1,)), ((), ())),
            precision=lax.Precision.HIGHEST, preferred_element_type=jnp.float32,
        )
        for q in range(quarters):
            pieces_ref[q, p] = projected[q * slab:(q + 1) * slab, :]
    k = g // cycle
    c = g % cycle
    peers = [(a + d) % quarters for d in range(1, quarters)]
    owners = [(k + d) % blocks for d in range(1, blocks)]

    def peer(j):
        return (g, j)

    def owner(j):
        return (j * cycle + c, a)

    barrier = pltpu.get_barrier_semaphore()
    for device in [peer(j) for j in peers] + [owner(j) for j in owners]:
        pl.semaphore_signal(barrier, inc=1, device_id=device, device_id_type=MESH)
    pl.semaphore_wait(barrier, len(peers) + len(owners))

    def start(n, source, target, device):
        copy = pltpu.make_async_remote_copy(
            src_ref=source,
            dst_ref=target,
            send_sem=send_sem.at[n],
            recv_sem=recv_sem.at[n],
            device_id=device,
            device_id_type=MESH,
        )
        copy.start()
        return copy

    copies = [start(n, pieces_ref.at[j], first.at[n], peer(j)) for n, j in enumerate(peers)]
    for copy in copies:
        copy.wait()
    total = pieces_ref[a]
    for n in range(len(peers)):
        total = total + first[n]
    for p in range(planes):
        plane = g * planes + p
        for j in range(blocks):
            weight = 0
            for t in range(targets_ref.shape[1]):
                sign = 2 * signs_ref[plane, t] - 1
                weight = weight + jnp.where(targets_ref[plane, t] == j, sign, 0)
            staged[j, p] = weight.astype(jnp.float32) * total[p]
    base = len(peers)
    copies = [
        start(base + n, staged.at[j], second.at[n], owner(j)) for n, j in enumerate(owners)
    ]
    for copy in copies:
        copy.wait()
    result = staged[k]
    for n in range(len(owners)):
        result = result + second[n]
    o_ref[...] = result


def core_exchange(field, left, right, targets, signs, cycle, quarters, blocks):
    planes, rank = field.shape[0], right.shape[0]
    piece = (planes, rank // quarters, rank)
    dtype = field.dtype
    return pl.pallas_call(
        functools.partial(core_kernel, cycle, blocks),
        out_shape=jax.ShapeDtypeStruct(piece, dtype),
        in_specs=[pl.BlockSpec(memory_space=pltpu.VMEM)] * 3
        + [pl.BlockSpec(memory_space=pltpu.SMEM)] * 2,
        out_specs=pl.BlockSpec(memory_space=pltpu.VMEM),
        scratch_shapes=[
            pltpu.VMEM((quarters,) + piece, dtype),
            pltpu.VMEM((quarters - 1,) + piece, dtype),
            pltpu.VMEM((blocks,) + piece, dtype),
            pltpu.VMEM((blocks - 1,) + piece, dtype),
            pltpu.SemaphoreType.DMA((quarters + blocks - 2,)),
            pltpu.SemaphoreType.DMA((quarters + blocks - 2,)),
        ],
        compiler_params=pltpu.CompilerParams(collective_id=1, has_side_effects=True),
    )(field, left, right, targets, signs)


def body(
    scalar_field, plane_sketch, second_sketch, third_sketch, mixing, plane_targets, plane_signs
):
    planes, rows, cells = scalar_field.shape
    rank_cols = mixing.shape[2]
    gx_index = lax.axis_index("gx")
    af_index = lax.axis_index("af")
    gx_size = lax.axis_size("gx")
    af_size = lax.axis_size("af")

    along_second = jnp.einsum("pjl,lk->pjk", scalar_field, third_sketch, precision=precise)
    partial_second = jnp.einsum(
        "pjk,pk->jk", along_second, plane_sketch[:, 0, :], precision=precise
    )
    along_third = jnp.einsum("pjl,jk->plk", scalar_field, second_sketch, precision=precise)
    partial_third = jnp.einsum("plk,pk->lk", along_third, plane_sketch[:, 1, :], precision=precise)

    range_second_block = jnp.dot(partial_second, mixing[0], precision=precise)
    range_third = jnp.dot(partial_third, mixing[1], precision=precise)
    full_rows = rows * af_size
    range_second = lax.dynamic_update_slice_in_dim(
        jnp.zeros((full_rows, rank_cols), jnp.float32), range_second_block, af_index * rows, 0
    )
    both = allreduce_all(jnp.concatenate([range_second, range_third], axis=0))

    panel_third, panel_second = factor_panels(both, rows)
    factor_third_all = panel_third[:, rank_cols:].T
    basis_second = panel_second[:, rank_cols:].T

    out_second = full_rows // (gx_size * af_size)
    assert rows == gx_size * out_second
    factor_second = lax.dynamic_slice_in_dim(basis_second, gx_index * out_second, out_second, 0)
    factor_third = lax.dynamic_slice_in_dim(
        factor_third_all, (gx_index * af_size + af_index) * out_second, out_second, 0
    )
    cycle = BLOCK // planes
    groups = gx_size // cycle
    assert planes * gx_size == BLOCKS * BLOCK and groups == BLOCKS
    core_sketch = core_exchange(
        scalar_field, panel_second, panel_third, plane_targets, plane_signs, cycle, af_size, groups
    )
    return (factor_second, factor_third, core_sketch)


def solution(mesh):
    in_specs = (P("gx", "af", None), P("gx", None, None), P("af", None), P(), P(), P(), P())
    out_specs = (P(("af", "gx"), None), P(("gx", "af"), None), P("gx", "af", None))
    return jax.shard_map(body, mesh=mesh, in_specs=in_specs, out_specs=out_specs, check_vma=False)
```

```python
import functools

import jax
import jax.numpy as jnp
from jax import lax
from jax.experimental import pallas as pl
from jax.experimental.pallas import tpu as pltpu
from jax.sharding import PartitionSpec as P

MESH = pl.DeviceIdType.MESH

BLOCK = 16
BLOCKS = 8


precise = lax.Precision.HIGHEST


def partner_list(gx_size, af_size):
    preferred = [("gx", 1), ("gx", 2), ("gx", 16), ("af", 1), ("gx", 4), ("gx", 32), ("af", 2), ("gx", 8)]
    sizes = {"gx": gx_size, "af": af_size}
    steps = [(axis, bit) for axis, bit in preferred if bit < sizes[axis]]
    for axis in ("gx", "af"):
        bit = 1
        while bit < sizes[axis]:
            if (axis, bit) not in steps:
                steps.append((axis, bit))
            bit *= 2
    return steps


def allreduce_kernel(digits, block_ref, third_ref, o_ref, acc, recv, exchange, gathered, send_sem, recv_sem):
    index = {"gx": lax.axis_index("gx"), "af": lax.axis_index("af")}

    def bits_of(digit):
        return [(index[axis] // bit) % 2 for axis, bit in digit]

    def member(digit):
        return sum(own * 2**t for t, own in enumerate(bits_of(digit)))

    def flipped(digit, d):
        return sum(
            (own + ((d >> t) & 1) * (1 - 2 * own)) * 2**t for t, own in enumerate(bits_of(digit))
        )

    def device(digit, d):
        values = dict(index)
        for t, ((axis, bit), own) in enumerate(zip(digit, bits_of(digit))):
            values[axis] = values[axis] + bit * ((d >> t) & 1) * (1 - 2 * own)
        return (values["gx"], values["af"])

    def others(digit):
        return range(1, 2 ** len(digit))

    barrier = pltpu.get_barrier_semaphore()
    for digit in digits:
        for d in others(digit):
            pl.semaphore_signal(barrier, inc=1, device_id=device(digit, d), device_id_type=MESH)
    pl.semaphore_wait(barrier, sum(len(others(digit)) for digit in digits))

    counter = [0]

    def start(device_id, source, target):
        n = counter[0]
        counter[0] += 1
        copy = pltpu.make_async_remote_copy(
            src_ref=source,
            dst_ref=target,
            send_sem=send_sem.at[n],
            recv_sem=recv_sem.at[n],
            device_id=device_id,
            device_id_type=MESH,
        )
        copy.start()
        return copy

    half = third_ref.shape[0]
    block_rows = block_ref.shape[0]
    acc[pl.ds(0, half), :] = jnp.zeros((half,) + acc.shape[1:], acc.dtype)
    acc[pl.ds(pl.multiple_of(index["af"] * block_rows, 8), block_rows), :] = block_ref[...]
    acc[pl.ds(half, half), :] = third_ref[...]
    offset, length, slot = 0, acc.shape[0], 0
    parents = []
    for digit in digits[:-1]:
        me = member(digit)
        part = length // 2 ** len(digit)
        copies = []
        for d in others(digit):
            give = pl.multiple_of(offset + flipped(digit, d) * part, 8)
            target = recv.at[pl.ds(slot + (d - 1) * part, part)]
            copies.append(start(device(digit, d), acc.at[pl.ds(give, part)], target))
        for copy in copies:
            copy.wait()
        keep = pl.multiple_of(offset + me * part, 8)
        total = acc[pl.ds(keep, part), :]
        for d in others(digit):
            total = total + recv[pl.ds(slot + (d - 1) * part, part), :]
        acc[pl.ds(keep, part), :] = total
        parents.append((offset, length))
        offset, length, slot = keep, part, slot + len(others(digit)) * part

    last = digits[-1]
    me = member(last)
    segment = acc.at[pl.ds(offset, length)]
    copies = [start(device(last, d), segment, exchange.at[me]) for d in others(last)]
    exchange[me] = acc[pl.ds(offset, length), :]
    for copy in copies:
        copy.wait()
    total = exchange[0]
    for q in range(1, 2 ** len(last)):
        total = total + exchange[q]
    gathered[pl.ds(offset, length), :] = total

    for digit, (parent_offset, parent_length) in zip(reversed(digits[:-1]), reversed(parents)):
        part = gathered.at[pl.ds(offset, length)]
        copies = [start(device(digit, d), part, part) for d in others(digit)]
        for copy in copies:
            copy.wait()
        offset, length = parent_offset, parent_length
    o_ref[...] = gathered[...]


def allreduce_all(block, third):
    x = jax.ShapeDtypeStruct((2 * third.shape[0],) + third.shape[1:], third.dtype)
    steps = partner_list(lax.axis_size("gx"), lax.axis_size("af"))
    digits = [steps[t:t + 3] for t in range(0, len(steps), 3)]
    last_rows = x.shape[0]
    for digit in digits[:-1]:
        last_rows //= 2 ** len(digit)
    assert last_rows % 8 == 0
    copies = sum(2 * (2 ** len(digit) - 1) for digit in digits[:-1]) + 2 ** len(digits[-1]) - 1
    return pl.pallas_call(
        functools.partial(allreduce_kernel, digits),
        out_shape=jax.ShapeDtypeStruct(x.shape, x.dtype),
        in_specs=[pl.BlockSpec(memory_space=pltpu.VMEM)] * 2,
        out_specs=pl.BlockSpec(memory_space=pltpu.VMEM),
        scratch_shapes=[
            pltpu.VMEM(x.shape, x.dtype),
            pltpu.VMEM(x.shape, x.dtype),
            pltpu.VMEM((2 ** len(digits[-1]), last_rows) + x.shape[1:], x.dtype),
            pltpu.VMEM(x.shape, x.dtype),
            pltpu.SemaphoreType.DMA((copies,)),
            pltpu.SemaphoreType.DMA((copies,)),
        ],
        compiler_params=pltpu.CompilerParams(collective_id=0, has_side_effects=True),
    )(block, third)


def panel_kernel(both_ref, third_ref, second_ref):
    outputs = (third_ref, second_ref)
    rank = third_ref.shape[0]
    half = both_ref.shape[0] // 2
    own_rows = second_ref.shape[1] - rank
    for target, ranged in ((third_ref, both_ref[half:, :]), (second_ref, both_ref[:half, :])):
        flipped = ranged.T
        target[:, :rank] = jnp.dot(
            flipped, ranged, precision=lax.Precision.HIGHEST, preferred_element_type=jnp.float32
        )
    third_ref[:, rank:] = both_ref[half:, :].T
    start = pl.multiple_of(lax.axis_index("af") * own_rows, 8)
    second_ref[:, rank:] = both_ref[pl.ds(start, own_rows), :].T

    def step(first, j, carry):
        for ref in outputs:
            width = ref.shape[1]
            row = ref[pl.ds(j, 1), :]
            lanes = lax.broadcasted_iota(jnp.int32, (1, width), 1)
            square_lanes = lax.broadcasted_iota(jnp.int32, (1, rank), 1)
            pivot = jnp.sum(
                jnp.where(square_lanes == j, row[:, :rank], 0.0), axis=1, keepdims=True
            )
            inverse = 1.0 / jnp.sqrt(pivot)
            column = jnp.where(lanes < j, 0.0, row * inverse)
            count = rank - first
            block = ref[pl.ds(first, count), :]
            cols = lax.broadcasted_iota(jnp.int32, (count, rank), 1)
            upper = jnp.sum(jnp.where(cols == j, block[:, :rank], 0.0), axis=1, keepdims=True)
            below = lax.broadcasted_iota(jnp.int32, (count, 1), 0) + first > j
            scale = jnp.where(below, upper * inverse, 0.0)
            ref[pl.ds(first, count), :] = block - scale * column
            ref[pl.ds(j, 1), :] = column
        return carry

    span = 16
    for first in range(0, rank, span):
        lax.fori_loop(first, first + span, functools.partial(step, first), 0, unroll=2)


def factor_panels(both, rows):
    rank = both.shape[1]
    half = both.shape[0] // 2
    return pl.pallas_call(
        panel_kernel,
        out_shape=[
            jax.ShapeDtypeStruct((rank, rank + half), both.dtype),
            jax.ShapeDtypeStruct((rank, rank + rows), both.dtype),
        ],
        in_specs=[pl.BlockSpec(memory_space=pltpu.VMEM)],
        out_specs=[pl.BlockSpec(memory_space=pltpu.VMEM)] * 2,
    )(both)


def core_kernel(
    cycle, field_ref, left_ref, right_ref, weights_ref, o_ref,
    pieces_ref, first, staged, second, send_sem, recv_sem,
):
    g = lax.axis_index("gx")
    a = lax.axis_index("af")
    quarters, planes, slab = pieces_ref.shape[:3]
    blocks = weights_ref.shape[0]
    rank = right_ref.shape[0]
    for p in range(planes):
        left = jnp.dot(
            left_ref[:, rank:], field_ref[p],
            precision=lax.Precision.HIGHEST, preferred_element_type=jnp.float32,
        )
        projected = lax.dot_general(
            left, right_ref[:, rank:], (((1,), (1,)), ((), ())),
            precision=lax.Precision.HIGHEST, preferred_element_type=jnp.float32,
        )
        for q in range(quarters):
            pieces_ref[q, p] = projected[q * slab:(q + 1) * slab, :]
    k = g // cycle
    c = g % cycle
    peers = [(a + d) % quarters for d in range(1, quarters)]
    owners = [(k + d) % blocks for d in range(1, blocks)]

    def peer(j):
        return (g, j)

    def owner(j):
        return (j * cycle + c, a)

    barrier = pltpu.get_barrier_semaphore()
    for device in [peer(j) for j in peers] + [owner(j) for j in owners]:
        pl.semaphore_signal(barrier, inc=1, device_id=device, device_id_type=MESH)
    pl.semaphore_wait(barrier, len(peers) + len(owners))

    def start(n, source, target, device):
        copy = pltpu.make_async_remote_copy(
            src_ref=source,
            dst_ref=target,
            send_sem=send_sem.at[n],
            recv_sem=recv_sem.at[n],
            device_id=device,
            device_id_type=MESH,
        )
        copy.start()
        return copy

    copies = [start(n, pieces_ref.at[j], first.at[n], peer(j)) for n, j in enumerate(peers)]
    for copy in copies:
        copy.wait()
    total = pieces_ref[a]
    for n in range(len(peers)):
        total = total + first[n]
    for j in range(blocks):
        staged[j] = weights_ref[j] * total
    base = len(peers)
    copies = [
        start(base + n, staged.at[j], second.at[n], owner(j)) for n, j in enumerate(owners)
    ]
    for copy in copies:
        copy.wait()
    result = staged[k]
    for n in range(len(owners)):
        result = result + second[n]
    o_ref[...] = result


def core_exchange(field, left, right, weights, cycle, quarters):
    planes, rank = field.shape[0], right.shape[0]
    blocks = weights.shape[0]
    piece = (planes, rank // quarters, rank)
    dtype = field.dtype
    return pl.pallas_call(
        functools.partial(core_kernel, cycle),
        out_shape=jax.ShapeDtypeStruct(piece, dtype),
        in_specs=[pl.BlockSpec(memory_space=pltpu.VMEM)] * 4,
        out_specs=pl.BlockSpec(memory_space=pltpu.VMEM),
        scratch_shapes=[
            pltpu.VMEM((quarters,) + piece, dtype),
            pltpu.VMEM((quarters - 1,) + piece, dtype),
            pltpu.VMEM((blocks,) + piece, dtype),
            pltpu.VMEM((blocks - 1,) + piece, dtype),
            pltpu.SemaphoreType.DMA((quarters + blocks - 2,)),
            pltpu.SemaphoreType.DMA((quarters + blocks - 2,)),
        ],
        compiler_params=pltpu.CompilerParams(collective_id=1, has_side_effects=True),
    )(field, left, right, weights)


def body(
    scalar_field, plane_sketch, second_sketch, third_sketch, mixing, plane_targets, plane_signs
):
    planes, rows, cells = scalar_field.shape
    rank_cols = mixing.shape[2]
    gx_index = lax.axis_index("gx")
    af_index = lax.axis_index("af")
    gx_size = lax.axis_size("gx")
    af_size = lax.axis_size("af")

    along_second = jnp.einsum("pjl,lk->pjk", scalar_field, third_sketch, precision=precise)
    partial_second = jnp.einsum(
        "pjk,pk->jk", along_second, plane_sketch[:, 0, :], precision=precise
    )
    along_third = jnp.einsum("pjl,jk->plk", scalar_field, second_sketch, precision=precise)
    partial_third = jnp.einsum("plk,pk->lk", along_third, plane_sketch[:, 1, :], precision=precise)

    range_second_block = jnp.dot(partial_second, mixing[0], precision=precise)
    range_third = jnp.dot(partial_third, mixing[1], precision=precise)
    full_rows = rows * af_size
    both = allreduce_all(range_second_block, range_third)

    panel_third, panel_second = factor_panels(both, rows)
    factor_third_all = panel_third[:, rank_cols:].T
    basis_second = panel_second[:, rank_cols:].T

    out_second = full_rows // (gx_size * af_size)
    assert rows == gx_size * out_second
    factor_second = lax.dynamic_slice_in_dim(basis_second, gx_index * out_second, out_second, 0)
    factor_third = lax.dynamic_slice_in_dim(
        factor_third_all, (gx_index * af_size + af_index) * out_second, out_second, 0
    )
    cycle = BLOCK // planes
    groups = gx_size // cycle
    assert planes * gx_size == BLOCKS * BLOCK and groups == BLOCKS
    own_targets = lax.dynamic_slice_in_dim(plane_targets, gx_index * planes, planes, 0)
    own_signs = lax.dynamic_slice_in_dim(plane_signs, gx_index * planes, planes, 0)
    sign_values = (2 * own_signs - 1).astype(jnp.float32)
    block_ids = jnp.arange(groups, dtype=jnp.int32)
    weights = jnp.sum(
        jnp.where(own_targets[None, :, :] == block_ids[:, None, None], sign_values[None, :, :], 0.0),
        axis=2,
    )
    lane_weights = jnp.broadcast_to(weights[:, :, None, None], (groups, planes, 1, rank_cols))
    core_sketch = core_exchange(
        scalar_field, panel_second, panel_third, lane_weights, cycle, af_size
    )
    return (factor_second, factor_third, core_sketch)


def solution(mesh):
    in_specs = (P("gx", "af", None), P("gx", None, None), P("af", None), P(), P(), P(), P())
    out_specs = (P(("af", "gx"), None), P(("gx", "af"), None), P("gx", "af", None))
    return jax.shard_map(body, mesh=mesh, in_specs=in_specs, out_specs=out_specs, check_vma=False)
```

```python
import functools

import jax
import jax.numpy as jnp
from jax import lax
from jax.experimental import pallas as pl
from jax.experimental.pallas import tpu as pltpu
from jax.sharding import PartitionSpec as P

MESH = pl.DeviceIdType.MESH

BLOCK = 16
BLOCKS = 8


precise = lax.Precision.HIGHEST


def partner_list(gx_size, af_size):
    preferred = [("gx", 1), ("gx", 2), ("af", 1), ("gx", 16), ("gx", 4), ("af", 2), ("gx", 32), ("gx", 8)]
    sizes = {"gx": gx_size, "af": af_size}
    steps = [(axis, bit) for axis, bit in preferred if bit < sizes[axis]]
    for axis in ("gx", "af"):
        bit = 1
        while bit < sizes[axis]:
            if (axis, bit) not in steps:
                steps.append((axis, bit))
            bit *= 2
    return steps


def allreduce_kernel(digits, x_ref, o_ref, acc, recv, exchange, gathered, send_sem, recv_sem):
    index = {"gx": lax.axis_index("gx"), "af": lax.axis_index("af")}

    def bits_of(digit):
        return [(index[axis] // bit) % 2 for axis, bit in digit]

    def member(digit):
        return sum(own * 2**t for t, own in enumerate(bits_of(digit)))

    def flipped(digit, d):
        return sum(
            (own + ((d >> t) & 1) * (1 - 2 * own)) * 2**t for t, own in enumerate(bits_of(digit))
        )

    def device(digit, d):
        values = dict(index)
        for t, ((axis, bit), own) in enumerate(zip(digit, bits_of(digit))):
            values[axis] = values[axis] + bit * ((d >> t) & 1) * (1 - 2 * own)
        return (values["gx"], values["af"])

    def others(digit):
        return range(1, 2 ** len(digit))

    barrier = pltpu.get_barrier_semaphore()
    for digit in digits:
        for d in others(digit):
            pl.semaphore_signal(barrier, inc=1, device_id=device(digit, d), device_id_type=MESH)
    pl.semaphore_wait(barrier, sum(len(others(digit)) for digit in digits))

    counter = [0]

    def start(device_id, source, target):
        n = counter[0]
        counter[0] += 1
        copy = pltpu.make_async_remote_copy(
            src_ref=source,
            dst_ref=target,
            send_sem=send_sem.at[n],
            recv_sem=recv_sem.at[n],
            device_id=device_id,
            device_id_type=MESH,
        )
        copy.start()
        return copy

    acc[...] = x_ref[...]
    offset, length, slot = 0, acc.shape[0], 0
    parents = []
    for digit in digits[:-1]:
        me = member(digit)
        part = length // 2 ** len(digit)
        copies = []
        for d in others(digit):
            give = pl.multiple_of(offset + flipped(digit, d) * part, 8)
            target = recv.at[pl.ds(slot + (d - 1) * part, part)]
            copies.append(start(device(digit, d), acc.at[pl.ds(give, part)], target))
        for copy in copies:
            copy.wait()
        keep = pl.multiple_of(offset + me * part, 8)
        total = acc[pl.ds(keep, part), :]
        for d in others(digit):
            total = total + recv[pl.ds(slot + (d - 1) * part, part), :]
        acc[pl.ds(keep, part), :] = total
        parents.append((offset, length))
        offset, length, slot = keep, part, slot + len(others(digit)) * part

    last = digits[-1]
    me = member(last)
    segment = acc.at[pl.ds(offset, length)]
    copies = [start(device(last, d), segment, exchange.at[me]) for d in others(last)]
    exchange[me] = acc[pl.ds(offset, length), :]
    for copy in copies:
        copy.wait()
    total = exchange[0]
    for q in range(1, 2 ** len(last)):
        total = total + exchange[q]
    gathered[pl.ds(offset, length), :] = total

    for digit, (parent_offset, parent_length) in zip(reversed(digits[:-1]), reversed(parents)):
        part = gathered.at[pl.ds(offset, length)]
        copies = [start(device(digit, d), part, part) for d in others(digit)]
        for copy in copies:
            copy.wait()
        offset, length = parent_offset, parent_length
    o_ref[...] = gathered[...]


def allreduce_all(x):
    steps = partner_list(lax.axis_size("gx"), lax.axis_size("af"))
    digits = [steps[t:t + 3] for t in range(0, len(steps), 3)]
    last_rows = x.shape[0]
    for digit in digits[:-1]:
        last_rows //= 2 ** len(digit)
    assert last_rows % 8 == 0
    copies = sum(2 * (2 ** len(digit) - 1) for digit in digits[:-1]) + 2 ** len(digits[-1]) - 1
    return pl.pallas_call(
        functools.partial(allreduce_kernel, digits),
        out_shape=jax.ShapeDtypeStruct(x.shape, x.dtype),
        in_specs=[pl.BlockSpec(memory_space=pltpu.VMEM)],
        out_specs=pl.BlockSpec(memory_space=pltpu.VMEM),
        scratch_shapes=[
            pltpu.VMEM(x.shape, x.dtype),
            pltpu.VMEM(x.shape, x.dtype),
            pltpu.VMEM((2 ** len(digits[-1]), last_rows) + x.shape[1:], x.dtype),
            pltpu.VMEM(x.shape, x.dtype),
            pltpu.SemaphoreType.DMA((copies,)),
            pltpu.SemaphoreType.DMA((copies,)),
        ],
        compiler_params=pltpu.CompilerParams(collective_id=0, has_side_effects=True),
    )(x)


def panel_kernel(both_ref, third_ref, second_ref):
    outputs = (third_ref, second_ref)
    rank = third_ref.shape[0]
    half = both_ref.shape[0] // 2
    own_rows = second_ref.shape[1] - rank
    for target, ranged in ((third_ref, both_ref[half:, :]), (second_ref, both_ref[:half, :])):
        flipped = ranged.T
        target[:, :rank] = jnp.dot(
            flipped, ranged, precision=lax.Precision.HIGHEST, preferred_element_type=jnp.float32
        )
    third_ref[:, rank:] = both_ref[half:, :].T
    start = pl.multiple_of(lax.axis_index("af") * own_rows, 8)
    second_ref[:, rank:] = both_ref[pl.ds(start, own_rows), :].T

    def step(first, j, carry):
        for ref in outputs:
            width = ref.shape[1]
            row = ref[pl.ds(j, 1), :]
            lanes = lax.broadcasted_iota(jnp.int32, (1, width), 1)
            square_lanes = lax.broadcasted_iota(jnp.int32, (1, rank), 1)
            pivot = jnp.sum(
                jnp.where(square_lanes == j, row[:, :rank], 0.0), axis=1, keepdims=True
            )
            inverse = 1.0 / jnp.sqrt(pivot)
            column = jnp.where(lanes < j, 0.0, row * inverse)
            count = rank - first
            block = ref[pl.ds(first, count), :]
            cols = lax.broadcasted_iota(jnp.int32, (count, rank), 1)
            upper = jnp.sum(jnp.where(cols == j, block[:, :rank], 0.0), axis=1, keepdims=True)
            below = lax.broadcasted_iota(jnp.int32, (count, 1), 0) + first > j
            scale = jnp.where(below, upper * inverse, 0.0)
            ref[pl.ds(first, count), :] = block - scale * column
            ref[pl.ds(j, 1), :] = column
        return carry

    span = 16
    for first in range(0, rank, span):
        lax.fori_loop(first, first + span, functools.partial(step, first), 0, unroll=2)


def factor_panels(both, rows):
    rank = both.shape[1]
    half = both.shape[0] // 2
    return pl.pallas_call(
        panel_kernel,
        out_shape=[
            jax.ShapeDtypeStruct((rank, rank + half), both.dtype),
            jax.ShapeDtypeStruct((rank, rank + rows), both.dtype),
        ],
        in_specs=[pl.BlockSpec(memory_space=pltpu.VMEM)],
        out_specs=[pl.BlockSpec(memory_space=pltpu.VMEM)] * 2,
    )(both)


def core_kernel(
    cycle, field_ref, left_ref, right_ref, weights_ref, o_ref,
    pieces_ref, first, staged, second, send_sem, recv_sem,
):
    g = lax.axis_index("gx")
    a = lax.axis_index("af")
    quarters, planes, slab = pieces_ref.shape[:3]
    blocks = weights_ref.shape[0]
    rank = right_ref.shape[0]
    for p in range(planes):
        left = jnp.dot(
            left_ref[:, rank:], field_ref[p],
            precision=lax.Precision.HIGHEST, preferred_element_type=jnp.float32,
        )
        projected = lax.dot_general(
            left, right_ref[:, rank:], (((1,), (1,)), ((), ())),
            precision=lax.Precision.HIGHEST, preferred_element_type=jnp.float32,
        )
        for q in range(quarters):
            pieces_ref[q, p] = projected[q * slab:(q + 1) * slab, :]
    k = g // cycle
    c = g % cycle
    peers = [(a + d) % quarters for d in range(1, quarters)]
    owners = [(k + d) % blocks for d in range(1, blocks)]

    def peer(j):
        return (g, j)

    def owner(j):
        return (j * cycle + c, a)

    barrier = pltpu.get_barrier_semaphore()
    for device in [peer(j) for j in peers] + [owner(j) for j in owners]:
        pl.semaphore_signal(barrier, inc=1, device_id=device, device_id_type=MESH)
    pl.semaphore_wait(barrier, len(peers) + len(owners))

    def start(n, source, target, device):
        copy = pltpu.make_async_remote_copy(
            src_ref=source,
            dst_ref=target,
            send_sem=send_sem.at[n],
            recv_sem=recv_sem.at[n],
            device_id=device,
            device_id_type=MESH,
        )
        copy.start()
        return copy

    copies = [start(n, pieces_ref.at[j], first.at[n], peer(j)) for n, j in enumerate(peers)]
    for copy in copies:
        copy.wait()
    total = pieces_ref[a]
    for n in range(len(peers)):
        total = total + first[n]
    for j in range(blocks):
        staged[j] = weights_ref[j] * total
    base = len(peers)
    copies = [
        start(base + n, staged.at[j], second.at[n], owner(j)) for n, j in enumerate(owners)
    ]
    for copy in copies:
        copy.wait()
    result = staged[k]
    for n in range(len(owners)):
        result = result + second[n]
    o_ref[...] = result


def core_exchange(field, left, right, weights, cycle, quarters):
    planes, rank = field.shape[0], right.shape[0]
    blocks = weights.shape[0]
    piece = (planes, rank // quarters, rank)
    dtype = field.dtype
    return pl.pallas_call(
        functools.partial(core_kernel, cycle),
        out_shape=jax.ShapeDtypeStruct(piece, dtype),
        in_specs=[pl.BlockSpec(memory_space=pltpu.VMEM)] * 4,
        out_specs=pl.BlockSpec(memory_space=pltpu.VMEM),
        scratch_shapes=[
            pltpu.VMEM((quarters,) + piece, dtype),
            pltpu.VMEM((quarters - 1,) + piece, dtype),
            pltpu.VMEM((blocks,) + piece, dtype),
            pltpu.VMEM((blocks - 1,) + piece, dtype),
            pltpu.SemaphoreType.DMA((quarters + blocks - 2,)),
            pltpu.SemaphoreType.DMA((quarters + blocks - 2,)),
        ],
        compiler_params=pltpu.CompilerParams(collective_id=1, has_side_effects=True),
    )(field, left, right, weights)


def body(
    scalar_field, plane_sketch, second_sketch, third_sketch, mixing, plane_targets, plane_signs
):
    planes, rows, cells = scalar_field.shape
    rank_cols = mixing.shape[2]
    gx_index = lax.axis_index("gx")
    af_index = lax.axis_index("af")
    gx_size = lax.axis_size("gx")
    af_size = lax.axis_size("af")

    along_second = jnp.einsum("pjl,lk->pjk", scalar_field, third_sketch, precision=precise)
    partial_second = jnp.einsum(
        "pjk,pk->jk", along_second, plane_sketch[:, 0, :], precision=precise
    )
    along_third = jnp.einsum("pjl,jk->plk", scalar_field, second_sketch, precision=precise)
    partial_third = jnp.einsum("plk,pk->lk", along_third, plane_sketch[:, 1, :], precision=precise)

    range_second_block = jnp.dot(partial_second, mixing[0], precision=precise)
    range_third = jnp.dot(partial_third, mixing[1], precision=precise)
    full_rows = rows * af_size
    range_second = lax.dynamic_update_slice_in_dim(
        jnp.zeros((full_rows, rank_cols), jnp.float32), range_second_block, af_index * rows, 0
    )
    both = allreduce_all(jnp.concatenate([range_second, range_third], axis=0))

    panel_third, panel_second = factor_panels(both, rows)
    factor_third_all = panel_third[:, rank_cols:].T
    basis_second = panel_second[:, rank_cols:].T

    out_second = full_rows // (gx_size * af_size)
    assert rows == gx_size * out_second
    factor_second = lax.dynamic_slice_in_dim(basis_second, gx_index * out_second, out_second, 0)
    factor_third = lax.dynamic_slice_in_dim(
        factor_third_all, (gx_index * af_size + af_index) * out_second, out_second, 0
    )
    cycle = BLOCK // planes
    groups = gx_size // cycle
    assert planes * gx_size == BLOCKS * BLOCK and groups == BLOCKS
    own_targets = lax.dynamic_slice_in_dim(plane_targets, gx_index * planes, planes, 0)
    own_signs = lax.dynamic_slice_in_dim(plane_signs, gx_index * planes, planes, 0)
    sign_values = (2 * own_signs - 1).astype(jnp.float32)
    block_ids = jnp.arange(groups, dtype=jnp.int32)
    weights = jnp.sum(
        jnp.where(own_targets[None, :, :] == block_ids[:, None, None], sign_values[None, :, :], 0.0),
        axis=2,
    )
    lane_weights = jnp.broadcast_to(weights[:, :, None, None], (groups, planes, 1, rank_cols))
    core_sketch = core_exchange(
        scalar_field, panel_second, panel_third, lane_weights, cycle, af_size
    )
    return (factor_second, factor_third, core_sketch)


def solution(mesh):
    in_specs = (P("gx", "af", None), P("gx", None, None), P("af", None), P(), P(), P(), P())
    out_specs = (P(("af", "gx"), None), P(("gx", "af"), None), P("gx", "af", None))
    return jax.shard_map(body, mesh=mesh, in_specs=in_specs, out_specs=out_specs, check_vma=False)
```

```python
import functools

import jax
import jax.numpy as jnp
from jax import lax
from jax.experimental import pallas as pl
from jax.experimental.pallas import tpu as pltpu
from jax.sharding import PartitionSpec as P

MESH = pl.DeviceIdType.MESH

BLOCK = 16
BLOCKS = 8


precise = lax.Precision.HIGHEST


def partner_list(gx_size, af_size):
    preferred = [("gx", 1), ("gx", 2), ("af", 1), ("gx", 16), ("gx", 4), ("af", 2), ("gx", 32), ("gx", 8)]
    sizes = {"gx": gx_size, "af": af_size}
    steps = [(axis, bit) for axis, bit in preferred if bit < sizes[axis]]
    for axis in ("gx", "af"):
        bit = 1
        while bit < sizes[axis]:
            if (axis, bit) not in steps:
                steps.append((axis, bit))
            bit *= 2
    return steps


def allreduce_kernel(digits, x_ref, o_ref, acc, recv, exchange, gathered, send_sem, recv_sem):
    index = {"gx": lax.axis_index("gx"), "af": lax.axis_index("af")}

    def bits_of(digit):
        return [(index[axis] // bit) % 2 for axis, bit in digit]

    def member(digit):
        return sum(own * 2**t for t, own in enumerate(bits_of(digit)))

    def flipped(digit, d):
        return sum(
            (own + ((d >> t) & 1) * (1 - 2 * own)) * 2**t for t, own in enumerate(bits_of(digit))
        )

    def device(digit, d):
        values = dict(index)
        for t, ((axis, bit), own) in enumerate(zip(digit, bits_of(digit))):
            values[axis] = values[axis] + bit * ((d >> t) & 1) * (1 - 2 * own)
        return (values["gx"], values["af"])

    def others(digit):
        return range(1, 2 ** len(digit))

    barrier = pltpu.get_barrier_semaphore()
    for digit in digits:
        for d in others(digit):
            pl.semaphore_signal(barrier, inc=1, device_id=device(digit, d), device_id_type=MESH)
    pl.semaphore_wait(barrier, sum(len(others(digit)) for digit in digits))

    counter = [0]

    def start(device_id, source, target):
        n = counter[0]
        counter[0] += 1
        copy = pltpu.make_async_remote_copy(
            src_ref=source,
            dst_ref=target,
            send_sem=send_sem.at[n],
            recv_sem=recv_sem.at[n],
            device_id=device_id,
            device_id_type=MESH,
        )
        copy.start()
        return copy

    acc[...] = x_ref[...]
    offset, length, slot = 0, acc.shape[0], 0
    parents = []
    for digit in digits[:-1]:
        me = member(digit)
        part = length // 2 ** len(digit)
        copies = []
        for d in others(digit):
            give = pl.multiple_of(offset + flipped(digit, d) * part, 8)
            target = recv.at[pl.ds(slot + (d - 1) * part, part)]
            copies.append(start(device(digit, d), acc.at[pl.ds(give, part)], target))
        for copy in copies:
            copy.wait()
        keep = pl.multiple_of(offset + me * part, 8)
        total = acc[pl.ds(keep, part), :]
        for d in others(digit):
            total = total + recv[pl.ds(slot + (d - 1) * part, part), :]
        acc[pl.ds(keep, part), :] = total
        parents.append((offset, length))
        offset, length, slot = keep, part, slot + len(others(digit)) * part

    last = digits[-1]
    me = member(last)
    segment = acc.at[pl.ds(offset, length)]
    copies = [start(device(last, d), segment, exchange.at[me]) for d in others(last)]
    exchange[me] = acc[pl.ds(offset, length), :]
    for copy in copies:
        copy.wait()
    total = exchange[0]
    for q in range(1, 2 ** len(last)):
        total = total + exchange[q]
    gathered[pl.ds(offset, length), :] = total

    for digit, (parent_offset, parent_length) in zip(reversed(digits[:-1]), reversed(parents)):
        part = gathered.at[pl.ds(offset, length)]
        copies = [start(device(digit, d), part, part) for d in others(digit)]
        for copy in copies:
            copy.wait()
        offset, length = parent_offset, parent_length
    o_ref[...] = gathered[...]


def allreduce_all(x):
    steps = partner_list(lax.axis_size("gx"), lax.axis_size("af"))
    digits = [steps[t:t + 3] for t in range(0, len(steps), 3)]
    last_rows = x.shape[0]
    for digit in digits[:-1]:
        last_rows //= 2 ** len(digit)
    assert last_rows % 8 == 0
    copies = sum(2 * (2 ** len(digit) - 1) for digit in digits[:-1]) + 2 ** len(digits[-1]) - 1
    return pl.pallas_call(
        functools.partial(allreduce_kernel, digits),
        out_shape=jax.ShapeDtypeStruct(x.shape, x.dtype),
        in_specs=[pl.BlockSpec(memory_space=pltpu.VMEM)],
        out_specs=pl.BlockSpec(memory_space=pltpu.VMEM),
        scratch_shapes=[
            pltpu.VMEM(x.shape, x.dtype),
            pltpu.VMEM(x.shape, x.dtype),
            pltpu.VMEM((2 ** len(digits[-1]), last_rows) + x.shape[1:], x.dtype),
            pltpu.VMEM(x.shape, x.dtype),
            pltpu.SemaphoreType.DMA((copies,)),
            pltpu.SemaphoreType.DMA((copies,)),
        ],
        compiler_params=pltpu.CompilerParams(collective_id=0, has_side_effects=True),
    )(x)


def panel_kernel(both_ref, third_ref, second_ref):
    outputs = (third_ref, second_ref)
    rank = third_ref.shape[0]
    half = both_ref.shape[0] // 2
    own_rows = second_ref.shape[1] - rank
    for target, ranged in ((third_ref, both_ref[half:, :]), (second_ref, both_ref[:half, :])):
        flipped = ranged.T
        target[:, :rank] = jnp.dot(
            flipped, ranged, precision=lax.Precision.HIGHEST, preferred_element_type=jnp.float32
        )
    third_ref[:, rank:] = both_ref[half:, :].T
    start = pl.multiple_of(lax.axis_index("af") * own_rows, 8)
    second_ref[:, rank:] = both_ref[pl.ds(start, own_rows), :].T

    def step(first, j, carry):
        for ref in outputs:
            width = ref.shape[1]
            row = ref[pl.ds(j, 1), :]
            lanes = lax.broadcasted_iota(jnp.int32, (1, width), 1)
            square_lanes = lax.broadcasted_iota(jnp.int32, (1, rank), 1)
            pivot = jnp.sum(
                jnp.where(square_lanes == j, row[:, :rank], 0.0), axis=1, keepdims=True
            )
            inverse = 1.0 / jnp.sqrt(pivot)
            column = jnp.where(lanes < j, 0.0, row * inverse)
            count = rank - first
            block = ref[pl.ds(first, count), :]
            cols = lax.broadcasted_iota(jnp.int32, (count, rank), 1)
            upper = jnp.sum(jnp.where(cols == j, block[:, :rank], 0.0), axis=1, keepdims=True)
            below = lax.broadcasted_iota(jnp.int32, (count, 1), 0) + first > j
            scale = jnp.where(below, upper * inverse, 0.0)
            ref[pl.ds(first, count), :] = block - scale * column
            ref[pl.ds(j, 1), :] = column
        return carry

    span = 16
    for first in range(0, rank, span):
        lax.fori_loop(first, first + span, functools.partial(step, first), 0, unroll=2)


def factor_panels(both, rows):
    rank = both.shape[1]
    half = both.shape[0] // 2
    return pl.pallas_call(
        panel_kernel,
        out_shape=[
            jax.ShapeDtypeStruct((rank, rank + half), both.dtype),
            jax.ShapeDtypeStruct((rank, rank + rows), both.dtype),
        ],
        in_specs=[pl.BlockSpec(memory_space=pltpu.VMEM)],
        out_specs=[pl.BlockSpec(memory_space=pltpu.VMEM)] * 2,
    )(both)


def core_kernel(
    cycle, field_ref, left_ref, right_ref, weights_ref, o_ref,
    pieces_ref, first, staged, second, send_sem, recv_sem,
):
    g = lax.axis_index("gx")
    a = lax.axis_index("af")
    quarters, planes, slab = pieces_ref.shape[:3]
    blocks = weights_ref.shape[0]
    rank = right_ref.shape[0]
    for p in range(planes):
        left = jnp.dot(
            left_ref[:, rank:], field_ref[p],
            precision=lax.Precision.HIGHEST, preferred_element_type=jnp.float32,
        )
        projected = lax.dot_general(
            left, right_ref[:, rank:], (((1,), (1,)), ((), ())),
            precision=lax.Precision.HIGHEST, preferred_element_type=jnp.float32,
        )
        for q in range(quarters):
            pieces_ref[q, p] = projected[q * slab:(q + 1) * slab, :]
    k = g // cycle
    c = g % cycle
    peers = [(a + d) % quarters for d in range(1, quarters)]
    owners = [(k + d) % blocks for d in range(1, blocks)]

    def peer(j):
        return (g, j)

    def owner(j):
        return (j * cycle + c, a)

    barrier = pltpu.get_barrier_semaphore()
    for device in [peer(j) for j in peers] + [owner(j) for j in owners]:
        pl.semaphore_signal(barrier, inc=1, device_id=device, device_id_type=MESH)
    pl.semaphore_wait(barrier, len(peers) + len(owners))

    def start(n, source, target, device):
        copy = pltpu.make_async_remote_copy(
            src_ref=source,
            dst_ref=target,
            send_sem=send_sem.at[n],
            recv_sem=recv_sem.at[n],
            device_id=device,
            device_id_type=MESH,
        )
        copy.start()
        return copy

    copies = [start(n, pieces_ref.at[j], first.at[n], peer(j)) for n, j in enumerate(peers)]
    for copy in copies:
        copy.wait()
    total = pieces_ref[a]
    for n in range(len(peers)):
        total = total + first[n]
    for j in range(blocks):
        staged[j] = weights_ref[j] * total
    base = len(peers)
    copies = [
        start(base + n, staged.at[j], second.at[n], owner(j)) for n, j in enumerate(owners)
    ]
    for copy in copies:
        copy.wait()
    result = staged[k]
    for n in range(len(owners)):
        result = result + second[n]
    o_ref[...] = result


def core_exchange(field, left, right, weights, cycle, quarters):
    planes, rank = field.shape[0], right.shape[0]
    blocks = weights.shape[0]
    piece = (planes, rank // quarters, rank)
    dtype = field.dtype
    return pl.pallas_call(
        functools.partial(core_kernel, cycle),
        out_shape=jax.ShapeDtypeStruct(piece, dtype),
        in_specs=[pl.BlockSpec(memory_space=pltpu.VMEM)] * 4,
        out_specs=pl.BlockSpec(memory_space=pltpu.VMEM),
        scratch_shapes=[
            pltpu.VMEM((quarters,) + piece, dtype),
            pltpu.VMEM((quarters - 1,) + piece, dtype),
            pltpu.VMEM((blocks,) + piece, dtype),
            pltpu.VMEM((blocks - 1,) + piece, dtype),
            pltpu.SemaphoreType.DMA((quarters + blocks - 2,)),
            pltpu.SemaphoreType.DMA((quarters + blocks - 2,)),
        ],
        compiler_params=pltpu.CompilerParams(collective_id=1, has_side_effects=True),
    )(field, left, right, weights)


def body(
    scalar_field, plane_sketch, second_sketch, third_sketch, mixing, plane_targets, plane_signs
):
    planes, rows, cells = scalar_field.shape
    rank_cols = mixing.shape[2]
    gx_index = lax.axis_index("gx")
    af_index = lax.axis_index("af")
    gx_size = lax.axis_size("gx")
    af_size = lax.axis_size("af")

    along_second = jnp.einsum("pjl,lk->pjk", scalar_field, third_sketch, precision=precise)
    partial_second = jnp.einsum(
        "pjk,pk->jk", along_second, plane_sketch[:, 0, :], precision=precise
    )
    along_third = jnp.einsum("pjl,jk->plk", scalar_field, second_sketch, precision=precise)
    partial_third = jnp.einsum("plk,pk->lk", along_third, plane_sketch[:, 1, :], precision=precise)

    range_second_block = jnp.dot(partial_second, mixing[0], precision=precise)
    range_third = jnp.dot(partial_third, mixing[1], precision=precise)
    full_rows = rows * af_size
    range_second = lax.dynamic_update_slice_in_dim(
        jnp.zeros((full_rows, rank_cols), jnp.float32), range_second_block, af_index * rows, 0
    )
    both = allreduce_all(jnp.concatenate([range_second, range_third], axis=0))

    panel_third, panel_second = factor_panels(both, rows)
    out_second = full_rows // (gx_size * af_size)
    assert rows == gx_size * out_second
    factor_second = lax.dynamic_slice_in_dim(
        panel_second, rank_cols + gx_index * out_second, out_second, 1
    ).T
    factor_third = lax.dynamic_slice_in_dim(
        panel_third, rank_cols + (gx_index * af_size + af_index) * out_second, out_second, 1
    ).T
    cycle = BLOCK // planes
    groups = gx_size // cycle
    assert planes * gx_size == BLOCKS * BLOCK and groups == BLOCKS
    own_targets = lax.dynamic_slice_in_dim(plane_targets, gx_index * planes, planes, 0)
    own_signs = lax.dynamic_slice_in_dim(plane_signs, gx_index * planes, planes, 0)
    sign_values = (2 * own_signs - 1).astype(jnp.float32)
    block_ids = jnp.arange(groups, dtype=jnp.int32)
    weights = jnp.sum(
        jnp.where(own_targets[None, :, :] == block_ids[:, None, None], sign_values[None, :, :], 0.0),
        axis=2,
    )
    lane_weights = jnp.broadcast_to(weights[:, :, None, None], (groups, planes, 1, rank_cols))
    core_sketch = core_exchange(
        scalar_field, panel_second, panel_third, lane_weights, cycle, af_size
    )
    return (factor_second, factor_third, core_sketch)


def solution(mesh):
    in_specs = (P("gx", "af", None), P("gx", None, None), P("af", None), P(), P(), P(), P())
    out_specs = (P(("af", "gx"), None), P(("gx", "af"), None), P("gx", "af", None))
    return jax.shard_map(body, mesh=mesh, in_specs=in_specs, out_specs=out_specs, check_vma=False)
```

```python
import functools

import jax
import jax.numpy as jnp
from jax import lax
from jax.experimental import pallas as pl
from jax.experimental.pallas import tpu as pltpu
from jax.sharding import PartitionSpec as P

MESH = pl.DeviceIdType.MESH

BLOCK = 16
BLOCKS = 8


precise = lax.Precision.HIGHEST


def partner_list(gx_size, af_size):
    preferred = [("gx", 1), ("gx", 2), ("af", 1), ("gx", 16), ("gx", 4), ("af", 2), ("gx", 32), ("gx", 8)]
    sizes = {"gx": gx_size, "af": af_size}
    steps = [(axis, bit) for axis, bit in preferred if bit < sizes[axis]]
    for axis in ("gx", "af"):
        bit = 1
        while bit < sizes[axis]:
            if (axis, bit) not in steps:
                steps.append((axis, bit))
            bit *= 2
    return steps


def allreduce_kernel(digits, x_ref, o_ref, acc, recv, exchange, gathered, send_sem, recv_sem):
    index = {"gx": lax.axis_index("gx"), "af": lax.axis_index("af")}

    def bits_of(digit):
        return [(index[axis] // bit) % 2 for axis, bit in digit]

    def member(digit):
        return sum(own * 2**t for t, own in enumerate(bits_of(digit)))

    def flipped(digit, d):
        return sum(
            (own + ((d >> t) & 1) * (1 - 2 * own)) * 2**t for t, own in enumerate(bits_of(digit))
        )

    def device(digit, d):
        values = dict(index)
        for t, ((axis, bit), own) in enumerate(zip(digit, bits_of(digit))):
            values[axis] = values[axis] + bit * ((d >> t) & 1) * (1 - 2 * own)
        return (values["gx"], values["af"])

    def others(digit):
        return range(1, 2 ** len(digit))

    barrier = pltpu.get_barrier_semaphore()
    for digit in digits:
        for d in others(digit):
            pl.semaphore_signal(barrier, inc=1, device_id=device(digit, d), device_id_type=MESH)
    pl.semaphore_wait(barrier, sum(len(others(digit)) for digit in digits))

    counter = [0]

    def start(device_id, source, target):
        n = counter[0]
        counter[0] += 1
        copy = pltpu.make_async_remote_copy(
            src_ref=source,
            dst_ref=target,
            send_sem=send_sem.at[n],
            recv_sem=recv_sem.at[n],
            device_id=device_id,
            device_id_type=MESH,
        )
        copy.start()
        return copy

    acc[...] = x_ref[...]
    offset, length, slot = 0, acc.shape[0], 0
    parents = []
    for digit in digits[:-1]:
        me = member(digit)
        part = length // 2 ** len(digit)
        copies = []
        for d in others(digit):
            give = pl.multiple_of(offset + flipped(digit, d) * part, 8)
            target = recv.at[pl.ds(slot + (d - 1) * part, part)]
            copies.append(start(device(digit, d), acc.at[pl.ds(give, part)], target))
        for copy in copies:
            copy.wait()
        keep = pl.multiple_of(offset + me * part, 8)
        total = acc[pl.ds(keep, part), :]
        for d in others(digit):
            total = total + recv[pl.ds(slot + (d - 1) * part, part), :]
        acc[pl.ds(keep, part), :] = total
        parents.append((offset, length))
        offset, length, slot = keep, part, slot + len(others(digit)) * part

    last = digits[-1]
    me = member(last)
    segment = acc.at[pl.ds(offset, length)]
    copies = [start(device(last, d), segment, exchange.at[me]) for d in others(last)]
    exchange[me] = acc[pl.ds(offset, length), :]
    for copy in copies:
        copy.wait()
    total = exchange[0]
    for q in range(1, 2 ** len(last)):
        total = total + exchange[q]
    gathered[pl.ds(offset, length), :] = total

    for digit, (parent_offset, parent_length) in zip(reversed(digits[:-1]), reversed(parents)):
        part = gathered.at[pl.ds(offset, length)]
        copies = [start(device(digit, d), part, part) for d in others(digit)]
        for copy in copies:
            copy.wait()
        offset, length = parent_offset, parent_length
    o_ref[...] = gathered[...]


def allreduce_all(x):
    steps = partner_list(lax.axis_size("gx"), lax.axis_size("af"))
    digits = [steps[t:t + 3] for t in range(0, len(steps), 3)]
    last_rows = x.shape[0]
    for digit in digits[:-1]:
        last_rows //= 2 ** len(digit)
    assert last_rows % 8 == 0
    copies = sum(2 * (2 ** len(digit) - 1) for digit in digits[:-1]) + 2 ** len(digits[-1]) - 1
    return pl.pallas_call(
        functools.partial(allreduce_kernel, digits),
        out_shape=jax.ShapeDtypeStruct(x.shape, x.dtype),
        in_specs=[pl.BlockSpec(memory_space=pltpu.VMEM)],
        out_specs=pl.BlockSpec(memory_space=pltpu.VMEM),
        scratch_shapes=[
            pltpu.VMEM(x.shape, x.dtype),
            pltpu.VMEM(x.shape, x.dtype),
            pltpu.VMEM((2 ** len(digits[-1]), last_rows) + x.shape[1:], x.dtype),
            pltpu.VMEM(x.shape, x.dtype),
            pltpu.SemaphoreType.DMA((copies,)),
            pltpu.SemaphoreType.DMA((copies,)),
        ],
        compiler_params=pltpu.CompilerParams(collective_id=0, has_side_effects=True),
    )(x)


def panel_kernel(both_ref, third_ref, second_ref):
    outputs = (third_ref, second_ref)
    rank = third_ref.shape[0]
    half = both_ref.shape[0] // 2
    own_rows = second_ref.shape[1] - rank
    for target, ranged in ((third_ref, both_ref[half:, :]), (second_ref, both_ref[:half, :])):
        flipped = ranged.T
        target[:, :rank] = jnp.dot(
            flipped, ranged, precision=lax.Precision.HIGHEST, preferred_element_type=jnp.float32
        )
    third_ref[:, rank:] = both_ref[half:, :].T
    start = pl.multiple_of(lax.axis_index("af") * own_rows, 8)
    second_ref[:, rank:] = both_ref[pl.ds(start, own_rows), :].T

    def step(first, j, carry):
        for ref in outputs:
            width = ref.shape[1]
            row = ref[pl.ds(j, 1), :]
            lanes = lax.broadcasted_iota(jnp.int32, (1, width), 1)
            square_lanes = lax.broadcasted_iota(jnp.int32, (1, rank), 1)
            pivot = jnp.sum(
                jnp.where(square_lanes == j, row[:, :rank], 0.0), axis=1, keepdims=True
            )
            inverse = 1.0 / jnp.sqrt(pivot)
            column = jnp.where(lanes < j, 0.0, row * inverse)
            count = rank - first
            block = ref[pl.ds(first, count), :]
            cols = lax.broadcasted_iota(jnp.int32, (count, rank), 1)
            upper = jnp.sum(jnp.where(cols == j, block[:, :rank], 0.0), axis=1, keepdims=True)
            below = lax.broadcasted_iota(jnp.int32, (count, 1), 0) + first > j
            scale = jnp.where(below, upper * inverse, 0.0)
            ref[pl.ds(first, count), :] = block - scale * column
            ref[pl.ds(j, 1), :] = column
        return carry

    span = 16
    for first in range(0, rank, span):
        lax.fori_loop(first, first + span, functools.partial(step, first), 0, unroll=4)


def factor_panels(both, rows):
    rank = both.shape[1]
    half = both.shape[0] // 2
    return pl.pallas_call(
        panel_kernel,
        out_shape=[
            jax.ShapeDtypeStruct((rank, rank + half), both.dtype),
            jax.ShapeDtypeStruct((rank, rank + rows), both.dtype),
        ],
        in_specs=[pl.BlockSpec(memory_space=pltpu.VMEM)],
        out_specs=[pl.BlockSpec(memory_space=pltpu.VMEM)] * 2,
    )(both)


def core_kernel(
    cycle, field_ref, left_ref, right_ref, weights_ref, o_ref,
    pieces_ref, first, staged, second, send_sem, recv_sem,
):
    g = lax.axis_index("gx")
    a = lax.axis_index("af")
    quarters, planes, slab = pieces_ref.shape[:3]
    blocks = weights_ref.shape[0]
    rank = right_ref.shape[0]
    for p in range(planes):
        left = jnp.dot(
            left_ref[:, rank:], field_ref[p],
            precision=lax.Precision.HIGHEST, preferred_element_type=jnp.float32,
        )
        projected = lax.dot_general(
            left, right_ref[:, rank:], (((1,), (1,)), ((), ())),
            precision=lax.Precision.HIGHEST, preferred_element_type=jnp.float32,
        )
        for q in range(quarters):
            pieces_ref[q, p] = projected[q * slab:(q + 1) * slab, :]
    k = g // cycle
    c = g % cycle
    peers = [(a + d) % quarters for d in range(1, quarters)]
    owners = [(k + d) % blocks for d in range(1, blocks)]

    def peer(j):
        return (g, j)

    def owner(j):
        return (j * cycle + c, a)

    barrier = pltpu.get_barrier_semaphore()
    for device in [peer(j) for j in peers] + [owner(j) for j in owners]:
        pl.semaphore_signal(barrier, inc=1, device_id=device, device_id_type=MESH)
    pl.semaphore_wait(barrier, len(peers) + len(owners))

    def start(n, source, target, device):
        copy = pltpu.make_async_remote_copy(
            src_ref=source,
            dst_ref=target,
            send_sem=send_sem.at[n],
            recv_sem=recv_sem.at[n],
            device_id=device,
            device_id_type=MESH,
        )
        copy.start()
        return copy

    copies = [start(n, pieces_ref.at[j], first.at[n], peer(j)) for n, j in enumerate(peers)]
    for copy in copies:
        copy.wait()
    total = pieces_ref[a]
    for n in range(len(peers)):
        total = total + first[n]
    for j in range(blocks):
        staged[j] = weights_ref[j] * total
    base = len(peers)
    copies = [
        start(base + n, staged.at[j], second.at[n], owner(j)) for n, j in enumerate(owners)
    ]
    for copy in copies:
        copy.wait()
    result = staged[k]
    for n in range(len(owners)):
        result = result + second[n]
    o_ref[...] = result


def core_exchange(field, left, right, weights, cycle, quarters):
    planes, rank = field.shape[0], right.shape[0]
    blocks = weights.shape[0]
    piece = (planes, rank // quarters, rank)
    dtype = field.dtype
    return pl.pallas_call(
        functools.partial(core_kernel, cycle),
        out_shape=jax.ShapeDtypeStruct(piece, dtype),
        in_specs=[pl.BlockSpec(memory_space=pltpu.VMEM)] * 4,
        out_specs=pl.BlockSpec(memory_space=pltpu.VMEM),
        scratch_shapes=[
            pltpu.VMEM((quarters,) + piece, dtype),
            pltpu.VMEM((quarters - 1,) + piece, dtype),
            pltpu.VMEM((blocks,) + piece, dtype),
            pltpu.VMEM((blocks - 1,) + piece, dtype),
            pltpu.SemaphoreType.DMA((quarters + blocks - 2,)),
            pltpu.SemaphoreType.DMA((quarters + blocks - 2,)),
        ],
        compiler_params=pltpu.CompilerParams(collective_id=1, has_side_effects=True),
    )(field, left, right, weights)


def body(
    scalar_field, plane_sketch, second_sketch, third_sketch, mixing, plane_targets, plane_signs
):
    planes, rows, cells = scalar_field.shape
    rank_cols = mixing.shape[2]
    gx_index = lax.axis_index("gx")
    af_index = lax.axis_index("af")
    gx_size = lax.axis_size("gx")
    af_size = lax.axis_size("af")

    along_second = jnp.einsum("pjl,lk->pjk", scalar_field, third_sketch, precision=precise)
    partial_second = jnp.einsum(
        "pjk,pk->jk", along_second, plane_sketch[:, 0, :], precision=precise
    )
    along_third = jnp.einsum("pjl,jk->plk", scalar_field, second_sketch, precision=precise)
    partial_third = jnp.einsum("plk,pk->lk", along_third, plane_sketch[:, 1, :], precision=precise)

    range_second_block = jnp.dot(partial_second, mixing[0], precision=precise)
    range_third = jnp.dot(partial_third, mixing[1], precision=precise)
    full_rows = rows * af_size
    range_second = lax.dynamic_update_slice_in_dim(
        jnp.zeros((full_rows, rank_cols), jnp.float32), range_second_block, af_index * rows, 0
    )
    both = allreduce_all(jnp.concatenate([range_second, range_third], axis=0))

    panel_third, panel_second = factor_panels(both, rows)
    factor_third_all = panel_third[:, rank_cols:].T
    basis_second = panel_second[:, rank_cols:].T

    out_second = full_rows // (gx_size * af_size)
    assert rows == gx_size * out_second
    factor_second = lax.dynamic_slice_in_dim(basis_second, gx_index * out_second, out_second, 0)
    factor_third = lax.dynamic_slice_in_dim(
        factor_third_all, (gx_index * af_size + af_index) * out_second, out_second, 0
    )
    cycle = BLOCK // planes
    groups = gx_size // cycle
    assert planes * gx_size == BLOCKS * BLOCK and groups == BLOCKS
    own_targets = lax.dynamic_slice_in_dim(plane_targets, gx_index * planes, planes, 0)
    own_signs = lax.dynamic_slice_in_dim(plane_signs, gx_index * planes, planes, 0)
    sign_values = (2 * own_signs - 1).astype(jnp.float32)
    block_ids = jnp.arange(groups, dtype=jnp.int32)
    weights = jnp.sum(
        jnp.where(own_targets[None, :, :] == block_ids[:, None, None], sign_values[None, :, :], 0.0),
        axis=2,
    )
    lane_weights = jnp.broadcast_to(weights[:, :, None, None], (groups, planes, 1, rank_cols))
    core_sketch = core_exchange(
        scalar_field, panel_second, panel_third, lane_weights, cycle, af_size
    )
    return (factor_second, factor_third, core_sketch)


def solution(mesh):
    in_specs = (P("gx", "af", None), P("gx", None, None), P("af", None), P(), P(), P(), P())
    out_specs = (P(("af", "gx"), None), P(("gx", "af"), None), P("gx", "af", None))
    return jax.shard_map(body, mesh=mesh, in_specs=in_specs, out_specs=out_specs, check_vma=False)
```

```python
import functools

import jax
import jax.numpy as jnp
from jax import lax
from jax.experimental import pallas as pl
from jax.experimental.pallas import tpu as pltpu
from jax.sharding import PartitionSpec as P

MESH = pl.DeviceIdType.MESH

BLOCK = 16
BLOCKS = 8


precise = lax.Precision.HIGHEST


def partner_list(gx_size, af_size):
    preferred = [("gx", 1), ("gx", 2), ("af", 1), ("gx", 16), ("gx", 4), ("af", 2), ("gx", 32), ("gx", 8)]
    sizes = {"gx": gx_size, "af": af_size}
    steps = [(axis, bit) for axis, bit in preferred if bit < sizes[axis]]
    for axis in ("gx", "af"):
        bit = 1
        while bit < sizes[axis]:
            if (axis, bit) not in steps:
                steps.append((axis, bit))
            bit *= 2
    return steps


def allreduce_kernel(digits, x_ref, third_ref, second_ref, acc, recv, exchange, gathered, send_sem, recv_sem):
    index = {"gx": lax.axis_index("gx"), "af": lax.axis_index("af")}

    def bits_of(digit):
        return [(index[axis] // bit) % 2 for axis, bit in digit]

    def member(digit):
        return sum(own * 2**t for t, own in enumerate(bits_of(digit)))

    def flipped(digit, d):
        return sum(
            (own + ((d >> t) & 1) * (1 - 2 * own)) * 2**t for t, own in enumerate(bits_of(digit))
        )

    def device(digit, d):
        values = dict(index)
        for t, ((axis, bit), own) in enumerate(zip(digit, bits_of(digit))):
            values[axis] = values[axis] + bit * ((d >> t) & 1) * (1 - 2 * own)
        return (values["gx"], values["af"])

    def others(digit):
        return range(1, 2 ** len(digit))

    barrier = pltpu.get_barrier_semaphore()
    for digit in digits:
        for d in others(digit):
            pl.semaphore_signal(barrier, inc=1, device_id=device(digit, d), device_id_type=MESH)
    pl.semaphore_wait(barrier, sum(len(others(digit)) for digit in digits))

    counter = [0]

    def start(device_id, source, target):
        n = counter[0]
        counter[0] += 1
        copy = pltpu.make_async_remote_copy(
            src_ref=source,
            dst_ref=target,
            send_sem=send_sem.at[n],
            recv_sem=recv_sem.at[n],
            device_id=device_id,
            device_id_type=MESH,
        )
        copy.start()
        return copy

    acc[...] = x_ref[...]
    offset, length, slot = 0, acc.shape[0], 0
    parents = []
    for digit in digits[:-1]:
        me = member(digit)
        part = length // 2 ** len(digit)
        copies = []
        for d in others(digit):
            give = pl.multiple_of(offset + flipped(digit, d) * part, 8)
            target = recv.at[pl.ds(slot + (d - 1) * part, part)]
            copies.append(start(device(digit, d), acc.at[pl.ds(give, part)], target))
        for copy in copies:
            copy.wait()
        keep = pl.multiple_of(offset + me * part, 8)
        total = acc[pl.ds(keep, part), :]
        for d in others(digit):
            total = total + recv[pl.ds(slot + (d - 1) * part, part), :]
        acc[pl.ds(keep, part), :] = total
        parents.append((offset, length))
        offset, length, slot = keep, part, slot + len(others(digit)) * part

    last = digits[-1]
    me = member(last)
    segment = acc.at[pl.ds(offset, length)]
    copies = [start(device(last, d), segment, exchange.at[me]) for d in others(last)]
    exchange[me] = acc[pl.ds(offset, length), :]
    for copy in copies:
        copy.wait()
    total = exchange[0]
    for q in range(1, 2 ** len(last)):
        total = total + exchange[q]
    gathered[pl.ds(offset, length), :] = total

    for digit, (parent_offset, parent_length) in zip(reversed(digits[:-1]), reversed(parents)):
        part = gathered.at[pl.ds(offset, length)]
        copies = [start(device(digit, d), part, part) for d in others(digit)]
        for copy in copies:
            copy.wait()
        offset, length = parent_offset, parent_length
    panel_kernel(gathered, third_ref, second_ref)


def allreduce_all(x, rows):
    rank = x.shape[1]
    half = x.shape[0] // 2
    steps = partner_list(lax.axis_size("gx"), lax.axis_size("af"))
    digits = [steps[t:t + 3] for t in range(0, len(steps), 3)]
    last_rows = x.shape[0]
    for digit in digits[:-1]:
        last_rows //= 2 ** len(digit)
    assert last_rows % 8 == 0
    copies = sum(2 * (2 ** len(digit) - 1) for digit in digits[:-1]) + 2 ** len(digits[-1]) - 1
    return pl.pallas_call(
        functools.partial(allreduce_kernel, digits),
        out_shape=[
            jax.ShapeDtypeStruct((rank, rank + half), x.dtype),
            jax.ShapeDtypeStruct((rank, rank + rows), x.dtype),
        ],
        in_specs=[pl.BlockSpec(memory_space=pltpu.VMEM)],
        out_specs=[pl.BlockSpec(memory_space=pltpu.VMEM)] * 2,
        scratch_shapes=[
            pltpu.VMEM(x.shape, x.dtype),
            pltpu.VMEM(x.shape, x.dtype),
            pltpu.VMEM((2 ** len(digits[-1]), last_rows) + x.shape[1:], x.dtype),
            pltpu.VMEM(x.shape, x.dtype),
            pltpu.SemaphoreType.DMA((copies,)),
            pltpu.SemaphoreType.DMA((copies,)),
        ],
        compiler_params=pltpu.CompilerParams(collective_id=0, has_side_effects=True),
    )(x)


def panel_kernel(both_ref, third_ref, second_ref):
    outputs = (third_ref, second_ref)
    rank = third_ref.shape[0]
    half = both_ref.shape[0] // 2
    own_rows = second_ref.shape[1] - rank
    for target, ranged in ((third_ref, both_ref[half:, :]), (second_ref, both_ref[:half, :])):
        flipped = ranged.T
        target[:, :rank] = jnp.dot(
            flipped, ranged, precision=lax.Precision.HIGHEST, preferred_element_type=jnp.float32
        )
    third_ref[:, rank:] = both_ref[half:, :].T
    start = pl.multiple_of(lax.axis_index("af") * own_rows, 8)
    second_ref[:, rank:] = both_ref[pl.ds(start, own_rows), :].T

    def step(first, j, carry):
        for ref in outputs:
            width = ref.shape[1]
            row = ref[pl.ds(j, 1), :]
            lanes = lax.broadcasted_iota(jnp.int32, (1, width), 1)
            square_lanes = lax.broadcasted_iota(jnp.int32, (1, rank), 1)
            pivot = jnp.sum(
                jnp.where(square_lanes == j, row[:, :rank], 0.0), axis=1, keepdims=True
            )
            inverse = 1.0 / jnp.sqrt(pivot)
            column = jnp.where(lanes < j, 0.0, row * inverse)
            count = rank - first
            block = ref[pl.ds(first, count), :]
            cols = lax.broadcasted_iota(jnp.int32, (count, rank), 1)
            upper = jnp.sum(jnp.where(cols == j, block[:, :rank], 0.0), axis=1, keepdims=True)
            below = lax.broadcasted_iota(jnp.int32, (count, 1), 0) + first > j
            scale = jnp.where(below, upper * inverse, 0.0)
            ref[pl.ds(first, count), :] = block - scale * column
            ref[pl.ds(j, 1), :] = column
        return carry

    span = 16
    for first in range(0, rank, span):
        lax.fori_loop(first, first + span, functools.partial(step, first), 0, unroll=4)


def core_kernel(
    cycle, field_ref, left_ref, right_ref, weights_ref, o_ref,
    pieces_ref, first, staged, second, send_sem, recv_sem,
):
    g = lax.axis_index("gx")
    a = lax.axis_index("af")
    quarters, planes, slab = pieces_ref.shape[:3]
    blocks = weights_ref.shape[0]
    rank = right_ref.shape[0]
    for p in range(planes):
        left = jnp.dot(
            left_ref[:, rank:], field_ref[p],
            precision=lax.Precision.HIGHEST, preferred_element_type=jnp.float32,
        )
        projected = lax.dot_general(
            left, right_ref[:, rank:], (((1,), (1,)), ((), ())),
            precision=lax.Precision.HIGHEST, preferred_element_type=jnp.float32,
        )
        for q in range(quarters):
            pieces_ref[q, p] = projected[q * slab:(q + 1) * slab, :]
    k = g // cycle
    c = g % cycle
    peers = [(a + d) % quarters for d in range(1, quarters)]
    owners = [(k + d) % blocks for d in range(1, blocks)]

    def peer(j):
        return (g, j)

    def owner(j):
        return (j * cycle + c, a)

    barrier = pltpu.get_barrier_semaphore()
    for device in [peer(j) for j in peers] + [owner(j) for j in owners]:
        pl.semaphore_signal(barrier, inc=1, device_id=device, device_id_type=MESH)
    pl.semaphore_wait(barrier, len(peers) + len(owners))

    def start(n, source, target, device):
        copy = pltpu.make_async_remote_copy(
            src_ref=source,
            dst_ref=target,
            send_sem=send_sem.at[n],
            recv_sem=recv_sem.at[n],
            device_id=device,
            device_id_type=MESH,
        )
        copy.start()
        return copy

    copies = [start(n, pieces_ref.at[j], first.at[n], peer(j)) for n, j in enumerate(peers)]
    for copy in copies:
        copy.wait()
    total = pieces_ref[a]
    for n in range(len(peers)):
        total = total + first[n]
    for j in range(blocks):
        staged[j] = weights_ref[j] * total
    base = len(peers)
    copies = [
        start(base + n, staged.at[j], second.at[n], owner(j)) for n, j in enumerate(owners)
    ]
    for copy in copies:
        copy.wait()
    result = staged[k]
    for n in range(len(owners)):
        result = result + second[n]
    o_ref[...] = result


def core_exchange(field, left, right, weights, cycle, quarters):
    planes, rank = field.shape[0], right.shape[0]
    blocks = weights.shape[0]
    piece = (planes, rank // quarters, rank)
    dtype = field.dtype
    return pl.pallas_call(
        functools.partial(core_kernel, cycle),
        out_shape=jax.ShapeDtypeStruct(piece, dtype),
        in_specs=[pl.BlockSpec(memory_space=pltpu.VMEM)] * 4,
        out_specs=pl.BlockSpec(memory_space=pltpu.VMEM),
        scratch_shapes=[
            pltpu.VMEM((quarters,) + piece, dtype),
            pltpu.VMEM((quarters - 1,) + piece, dtype),
            pltpu.VMEM((blocks,) + piece, dtype),
            pltpu.VMEM((blocks - 1,) + piece, dtype),
            pltpu.SemaphoreType.DMA((quarters + blocks - 2,)),
            pltpu.SemaphoreType.DMA((quarters + blocks - 2,)),
        ],
        compiler_params=pltpu.CompilerParams(collective_id=1, has_side_effects=True),
    )(field, left, right, weights)


def body(
    scalar_field, plane_sketch, second_sketch, third_sketch, mixing, plane_targets, plane_signs
):
    planes, rows, cells = scalar_field.shape
    rank_cols = mixing.shape[2]
    gx_index = lax.axis_index("gx")
    af_index = lax.axis_index("af")
    gx_size = lax.axis_size("gx")
    af_size = lax.axis_size("af")

    along_second = jnp.einsum("pjl,lk->pjk", scalar_field, third_sketch, precision=precise)
    partial_second = jnp.einsum(
        "pjk,pk->jk", along_second, plane_sketch[:, 0, :], precision=precise
    )
    along_third = jnp.einsum("pjl,jk->plk", scalar_field, second_sketch, precision=precise)
    partial_third = jnp.einsum("plk,pk->lk", along_third, plane_sketch[:, 1, :], precision=precise)

    range_second_block = jnp.dot(partial_second, mixing[0], precision=precise)
    range_third = jnp.dot(partial_third, mixing[1], precision=precise)
    full_rows = rows * af_size
    range_second = lax.dynamic_update_slice_in_dim(
        jnp.zeros((full_rows, rank_cols), jnp.float32), range_second_block, af_index * rows, 0
    )
    panel_third, panel_second = allreduce_all(
        jnp.concatenate([range_second, range_third], axis=0), rows
    )
    factor_third_all = panel_third[:, rank_cols:].T
    basis_second = panel_second[:, rank_cols:].T

    out_second = full_rows // (gx_size * af_size)
    assert rows == gx_size * out_second
    factor_second = lax.dynamic_slice_in_dim(basis_second, gx_index * out_second, out_second, 0)
    factor_third = lax.dynamic_slice_in_dim(
        factor_third_all, (gx_index * af_size + af_index) * out_second, out_second, 0
    )
    cycle = BLOCK // planes
    groups = gx_size // cycle
    assert planes * gx_size == BLOCKS * BLOCK and groups == BLOCKS
    own_targets = lax.dynamic_slice_in_dim(plane_targets, gx_index * planes, planes, 0)
    own_signs = lax.dynamic_slice_in_dim(plane_signs, gx_index * planes, planes, 0)
    sign_values = (2 * own_signs - 1).astype(jnp.float32)
    block_ids = jnp.arange(groups, dtype=jnp.int32)
    weights = jnp.sum(
        jnp.where(own_targets[None, :, :] == block_ids[:, None, None], sign_values[None, :, :], 0.0),
        axis=2,
    )
    lane_weights = jnp.broadcast_to(weights[:, :, None, None], (groups, planes, 1, rank_cols))
    core_sketch = core_exchange(
        scalar_field, panel_second, panel_third, lane_weights, cycle, af_size
    )
    return (factor_second, factor_third, core_sketch)


def solution(mesh):
    in_specs = (P("gx", "af", None), P("gx", None, None), P("af", None), P(), P(), P(), P())
    out_specs = (P(("af", "gx"), None), P(("gx", "af"), None), P("gx", "af", None))
    return jax.shard_map(body, mesh=mesh, in_specs=in_specs, out_specs=out_specs, check_vma=False)
```

```python
import functools

import jax
import jax.numpy as jnp
from jax import lax
from jax.experimental import pallas as pl
from jax.experimental.pallas import tpu as pltpu
from jax.sharding import PartitionSpec as P

MESH = pl.DeviceIdType.MESH

BLOCK = 16
BLOCKS = 8


precise = lax.Precision.HIGHEST


def partner_list(gx_size, af_size):
    preferred = [("gx", 1), ("gx", 2), ("af", 1), ("gx", 16), ("gx", 4), ("af", 2), ("gx", 32), ("gx", 8)]
    sizes = {"gx": gx_size, "af": af_size}
    steps = [(axis, bit) for axis, bit in preferred if bit < sizes[axis]]
    for axis in ("gx", "af"):
        bit = 1
        while bit < sizes[axis]:
            if (axis, bit) not in steps:
                steps.append((axis, bit))
            bit *= 2
    return steps


def allreduce_kernel(
    digits, cycle, x_ref, field_ref, weights_ref, third_ref, second_ref, core_ref,
    acc, recv, exchange, gathered, send_sem, recv_sem,
    pieces, first, staged, second, core_send, core_recv,
):
    index = {"gx": lax.axis_index("gx"), "af": lax.axis_index("af")}

    def bits_of(digit):
        return [(index[axis] // bit) % 2 for axis, bit in digit]

    def member(digit):
        return sum(own * 2**t for t, own in enumerate(bits_of(digit)))

    def flipped(digit, d):
        return sum(
            (own + ((d >> t) & 1) * (1 - 2 * own)) * 2**t for t, own in enumerate(bits_of(digit))
        )

    def device(digit, d):
        values = dict(index)
        for t, ((axis, bit), own) in enumerate(zip(digit, bits_of(digit))):
            values[axis] = values[axis] + bit * ((d >> t) & 1) * (1 - 2 * own)
        return (values["gx"], values["af"])

    def others(digit):
        return range(1, 2 ** len(digit))

    barrier = pltpu.get_barrier_semaphore()
    for digit in digits:
        for d in others(digit):
            pl.semaphore_signal(barrier, inc=1, device_id=device(digit, d), device_id_type=MESH)
    quarters, blocks = pieces.shape[0], weights_ref.shape[0]
    k, c = index["gx"] // cycle, index["gx"] % cycle
    core_devices = [(index["gx"], (index["af"] + d) % quarters) for d in range(1, quarters)]
    core_devices += [(((k + d) % blocks) * cycle + c, index["af"]) for d in range(1, blocks)]
    for core_device in core_devices:
        pl.semaphore_signal(barrier, inc=1, device_id=core_device, device_id_type=MESH)
    pl.semaphore_wait(barrier, sum(len(others(digit)) for digit in digits) + len(core_devices))

    counter = [0]

    def start(device_id, source, target):
        n = counter[0]
        counter[0] += 1
        copy = pltpu.make_async_remote_copy(
            src_ref=source,
            dst_ref=target,
            send_sem=send_sem.at[n],
            recv_sem=recv_sem.at[n],
            device_id=device_id,
            device_id_type=MESH,
        )
        copy.start()
        return copy

    acc[...] = x_ref[...]
    offset, length, slot = 0, acc.shape[0], 0
    parents = []
    for digit in digits[:-1]:
        me = member(digit)
        part = length // 2 ** len(digit)
        copies = []
        for d in others(digit):
            give = pl.multiple_of(offset + flipped(digit, d) * part, 8)
            target = recv.at[pl.ds(slot + (d - 1) * part, part)]
            copies.append(start(device(digit, d), acc.at[pl.ds(give, part)], target))
        for copy in copies:
            copy.wait()
        keep = pl.multiple_of(offset + me * part, 8)
        total = acc[pl.ds(keep, part), :]
        for d in others(digit):
            total = total + recv[pl.ds(slot + (d - 1) * part, part), :]
        acc[pl.ds(keep, part), :] = total
        parents.append((offset, length))
        offset, length, slot = keep, part, slot + len(others(digit)) * part

    last = digits[-1]
    me = member(last)
    segment = acc.at[pl.ds(offset, length)]
    copies = [start(device(last, d), segment, exchange.at[me]) for d in others(last)]
    exchange[me] = acc[pl.ds(offset, length), :]
    for copy in copies:
        copy.wait()
    total = exchange[0]
    for q in range(1, 2 ** len(last)):
        total = total + exchange[q]
    gathered[pl.ds(offset, length), :] = total

    for digit, (parent_offset, parent_length) in zip(reversed(digits[:-1]), reversed(parents)):
        part = gathered.at[pl.ds(offset, length)]
        copies = [start(device(digit, d), part, part) for d in others(digit)]
        for copy in copies:
            copy.wait()
        offset, length = parent_offset, parent_length
    panel_kernel(gathered, third_ref, second_ref)
    core_kernel(
        cycle, field_ref, second_ref, third_ref, weights_ref, core_ref,
        pieces, first, staged, second, core_send, core_recv, enter=False,
    )


def allreduce_all(x, rows, field, weights, cycle, quarters):
    planes, blocks = field.shape[0], weights.shape[0]
    rank = x.shape[1]
    half = x.shape[0] // 2
    steps = partner_list(lax.axis_size("gx"), lax.axis_size("af"))
    digits = [steps[t:t + 3] for t in range(0, len(steps), 3)]
    last_rows = x.shape[0]
    for digit in digits[:-1]:
        last_rows //= 2 ** len(digit)
    assert last_rows % 8 == 0
    copies = sum(2 * (2 ** len(digit) - 1) for digit in digits[:-1]) + 2 ** len(digits[-1]) - 1
    piece = (planes, rank // quarters, rank)
    return pl.pallas_call(
        functools.partial(allreduce_kernel, digits, cycle),
        out_shape=[
            jax.ShapeDtypeStruct((rank, rank + half), x.dtype),
            jax.ShapeDtypeStruct((rank, rank + rows), x.dtype),
            jax.ShapeDtypeStruct(piece, x.dtype),
        ],
        in_specs=[pl.BlockSpec(memory_space=pltpu.VMEM)] * 3,
        out_specs=[pl.BlockSpec(memory_space=pltpu.VMEM)] * 3,
        scratch_shapes=[
            pltpu.VMEM(x.shape, x.dtype),
            pltpu.VMEM(x.shape, x.dtype),
            pltpu.VMEM((2 ** len(digits[-1]), last_rows) + x.shape[1:], x.dtype),
            pltpu.VMEM(x.shape, x.dtype),
            pltpu.SemaphoreType.DMA((copies,)),
            pltpu.SemaphoreType.DMA((copies,)),
            pltpu.VMEM((quarters,) + piece, x.dtype),
            pltpu.VMEM((quarters - 1,) + piece, x.dtype),
            pltpu.VMEM((blocks,) + piece, x.dtype),
            pltpu.VMEM((blocks - 1,) + piece, x.dtype),
            pltpu.SemaphoreType.DMA((quarters + blocks - 2,)),
            pltpu.SemaphoreType.DMA((quarters + blocks - 2,)),
        ],
        compiler_params=pltpu.CompilerParams(collective_id=0, has_side_effects=True),
    )(x, field, weights)


def panel_kernel(both_ref, third_ref, second_ref):
    outputs = (third_ref, second_ref)
    rank = third_ref.shape[0]
    half = both_ref.shape[0] // 2
    own_rows = second_ref.shape[1] - rank
    for target, ranged in ((third_ref, both_ref[half:, :]), (second_ref, both_ref[:half, :])):
        flipped = ranged.T
        target[:, :rank] = jnp.dot(
            flipped, ranged, precision=lax.Precision.HIGHEST, preferred_element_type=jnp.float32
        )
    third_ref[:, rank:] = both_ref[half:, :].T
    start = pl.multiple_of(lax.axis_index("af") * own_rows, 8)
    second_ref[:, rank:] = both_ref[pl.ds(start, own_rows), :].T

    def step(first, j, carry):
        for ref in outputs:
            width = ref.shape[1]
            row = ref[pl.ds(j, 1), :]
            lanes = lax.broadcasted_iota(jnp.int32, (1, width), 1)
            square_lanes = lax.broadcasted_iota(jnp.int32, (1, rank), 1)
            pivot = jnp.sum(
                jnp.where(square_lanes == j, row[:, :rank], 0.0), axis=1, keepdims=True
            )
            inverse = 1.0 / jnp.sqrt(pivot)
            column = jnp.where(lanes < j, 0.0, row * inverse)
            count = rank - first
            block = ref[pl.ds(first, count), :]
            cols = lax.broadcasted_iota(jnp.int32, (count, rank), 1)
            upper = jnp.sum(jnp.where(cols == j, block[:, :rank], 0.0), axis=1, keepdims=True)
            below = lax.broadcasted_iota(jnp.int32, (count, 1), 0) + first > j
            scale = jnp.where(below, upper * inverse, 0.0)
            ref[pl.ds(first, count), :] = block - scale * column
            ref[pl.ds(j, 1), :] = column
        return carry

    span = 16
    for first in range(0, rank, span):
        lax.fori_loop(first, first + span, functools.partial(step, first), 0, unroll=4)


def core_kernel(
    cycle, field_ref, left_ref, right_ref, weights_ref, o_ref,
    pieces_ref, first, staged, second, send_sem, recv_sem, enter=True,
):
    g = lax.axis_index("gx")
    a = lax.axis_index("af")
    quarters, planes, slab = pieces_ref.shape[:3]
    blocks = weights_ref.shape[0]
    rank = right_ref.shape[0]
    for p in range(planes):
        left = jnp.dot(
            left_ref[:, rank:], field_ref[p],
            precision=lax.Precision.HIGHEST, preferred_element_type=jnp.float32,
        )
        projected = lax.dot_general(
            left, right_ref[:, rank:], (((1,), (1,)), ((), ())),
            precision=lax.Precision.HIGHEST, preferred_element_type=jnp.float32,
        )
        for q in range(quarters):
            pieces_ref[q, p] = projected[q * slab:(q + 1) * slab, :]
    k = g // cycle
    c = g % cycle
    peers = [(a + d) % quarters for d in range(1, quarters)]
    owners = [(k + d) % blocks for d in range(1, blocks)]

    def peer(j):
        return (g, j)

    def owner(j):
        return (j * cycle + c, a)

    if enter:
        barrier = pltpu.get_barrier_semaphore()
        for device in [peer(j) for j in peers] + [owner(j) for j in owners]:
            pl.semaphore_signal(barrier, inc=1, device_id=device, device_id_type=MESH)
        pl.semaphore_wait(barrier, len(peers) + len(owners))

    def start(n, source, target, device):
        copy = pltpu.make_async_remote_copy(
            src_ref=source,
            dst_ref=target,
            send_sem=send_sem.at[n],
            recv_sem=recv_sem.at[n],
            device_id=device,
            device_id_type=MESH,
        )
        copy.start()
        return copy

    copies = [start(n, pieces_ref.at[j], first.at[n], peer(j)) for n, j in enumerate(peers)]
    for copy in copies:
        copy.wait()
    total = pieces_ref[a]
    for n in range(len(peers)):
        total = total + first[n]
    for j in range(blocks):
        staged[j] = weights_ref[j] * total
    base = len(peers)
    copies = [
        start(base + n, staged.at[j], second.at[n], owner(j)) for n, j in enumerate(owners)
    ]
    for copy in copies:
        copy.wait()
    result = staged[k]
    for n in range(len(owners)):
        result = result + second[n]
    o_ref[...] = result


def core_exchange(field, left, right, weights, cycle, quarters):
    planes, rank = field.shape[0], right.shape[0]
    blocks = weights.shape[0]
    piece = (planes, rank // quarters, rank)
    dtype = field.dtype
    return pl.pallas_call(
        functools.partial(core_kernel, cycle),
        out_shape=jax.ShapeDtypeStruct(piece, dtype),
        in_specs=[pl.BlockSpec(memory_space=pltpu.VMEM)] * 4,
        out_specs=pl.BlockSpec(memory_space=pltpu.VMEM),
        scratch_shapes=[
            pltpu.VMEM((quarters,) + piece, dtype),
            pltpu.VMEM((quarters - 1,) + piece, dtype),
            pltpu.VMEM((blocks,) + piece, dtype),
            pltpu.VMEM((blocks - 1,) + piece, dtype),
            pltpu.SemaphoreType.DMA((quarters + blocks - 2,)),
            pltpu.SemaphoreType.DMA((quarters + blocks - 2,)),
        ],
        compiler_params=pltpu.CompilerParams(collective_id=1, has_side_effects=True),
    )(field, left, right, weights)


def body(
    scalar_field, plane_sketch, second_sketch, third_sketch, mixing, plane_targets, plane_signs
):
    planes, rows, cells = scalar_field.shape
    rank_cols = mixing.shape[2]
    gx_index = lax.axis_index("gx")
    af_index = lax.axis_index("af")
    gx_size = lax.axis_size("gx")
    af_size = lax.axis_size("af")

    along_second = jnp.einsum("pjl,lk->pjk", scalar_field, third_sketch, precision=precise)
    partial_second = jnp.einsum(
        "pjk,pk->jk", along_second, plane_sketch[:, 0, :], precision=precise
    )
    along_third = jnp.einsum("pjl,jk->plk", scalar_field, second_sketch, precision=precise)
    partial_third = jnp.einsum("plk,pk->lk", along_third, plane_sketch[:, 1, :], precision=precise)

    range_second_block = jnp.dot(partial_second, mixing[0], precision=precise)
    range_third = jnp.dot(partial_third, mixing[1], precision=precise)
    full_rows = rows * af_size
    range_second = lax.dynamic_update_slice_in_dim(
        jnp.zeros((full_rows, rank_cols), jnp.float32), range_second_block, af_index * rows, 0
    )
    cycle = BLOCK // planes
    groups = gx_size // cycle
    assert planes * gx_size == BLOCKS * BLOCK and groups == BLOCKS
    own_targets = lax.dynamic_slice_in_dim(plane_targets, gx_index * planes, planes, 0)
    own_signs = lax.dynamic_slice_in_dim(plane_signs, gx_index * planes, planes, 0)
    sign_values = (2 * own_signs - 1).astype(jnp.float32)
    block_ids = jnp.arange(groups, dtype=jnp.int32)
    weights = jnp.sum(
        jnp.where(own_targets[None, :, :] == block_ids[:, None, None], sign_values[None, :, :], 0.0),
        axis=2,
    )
    lane_weights = jnp.broadcast_to(weights[:, :, None, None], (groups, planes, 1, rank_cols))
    panel_third, panel_second, core_sketch = allreduce_all(
        jnp.concatenate([range_second, range_third], axis=0), rows,
        scalar_field, lane_weights, cycle, af_size,
    )
    factor_third_all = panel_third[:, rank_cols:].T
    basis_second = panel_second[:, rank_cols:].T

    out_second = full_rows // (gx_size * af_size)
    assert rows == gx_size * out_second
    factor_second = lax.dynamic_slice_in_dim(basis_second, gx_index * out_second, out_second, 0)
    factor_third = lax.dynamic_slice_in_dim(
        factor_third_all, (gx_index * af_size + af_index) * out_second, out_second, 0
    )
    return (factor_second, factor_third, core_sketch)


def solution(mesh):
    in_specs = (P("gx", "af", None), P("gx", None, None), P("af", None), P(), P(), P(), P())
    out_specs = (P(("af", "gx"), None), P(("gx", "af"), None), P("gx", "af", None))
    return jax.shard_map(body, mesh=mesh, in_specs=in_specs, out_specs=out_specs, check_vma=False)
```
